32 devices in a mesh: groups: 2 (over y), seq: 4 (over z), head: 4 (over x, core).
Axes of the slice: x: 2, y: 2, z: 4, core: 2. Of those that a mesh axis runs over, the one named last changes fastest.
Arguments:
- queries: bfloat16 [4096, 2048], P(('groups', 'seq'), 'head'), parts along dimension 0, may hold values from -8 to 8
- keys: bfloat16 [4096, 2048], P(('groups', 'seq'), 'head'), parts along dimension 0, may hold values from -8 to 8
- values: bfloat16 [4096, 2048], P(('groups', 'seq'), 'head'), parts along dimension 0, may hold values from -12 to 12
- w_out: bfloat16 [2048, 2048], replicated, may hold values from -0.125 to 0.125
Outputs:
- projected: bfloat16 [4096, 2048], P(('groups', 'seq', 'head')), parts along dimension 0
The draws below stay inside these ranges and needn't reach their ends.
There are 2 independent parts, one for each index of `groups`. The reference program is written for one: setup_inputs(seed, part) draws one part's arguments, and reference() takes and returns one part's arrays. A program takes and returns all parts, laid end to end along the dimension named above; an argument that names none is the same for every part. Nothing has to cross between parts.
All inputs are finite; a program needn't handle non-finite values.
Results may differ from the reference program's by a relative error of at most 0.005.
Values may be sent and summed in bfloat16 or wider, within the bound.
A program may use at most 128 MiB of HBM per device.

```python
import math
import jax
import jax.numpy as jnp
from jax import lax

HEADS = 16
HD = 128
D = 2048
WINDOW = 2048
TOKENS = 2048


def draw_queries(key, part):
    width = HEADS * HD
    spread = 1.4
    noise_key = jax.random.fold_in(key, 1)
    scale_key = jax.random.fold_in(key, 2)
    row_scale = jnp.exp(jax.random.uniform(scale_key, (TOKENS, 1), jnp.float32, math.log(0.7), math.log(2.0)))
    noise = jax.random.normal(noise_key, (TOKENS, width), jnp.float32)
    result = jnp.clip(noise * spread * row_scale, -8.0, 8.0)
    return result.astype(jnp.bfloat16)


def draw_keys(key, part):
    width = HEADS * HD
    spread = 1.6
    noise_key = jax.random.fold_in(key, 3)
    noise = jax.random.normal(noise_key, (TOKENS, width), jnp.float32)
    result = jnp.clip(noise * spread, -8.0, 8.0)
    return result.astype(jnp.bfloat16)


def draw_values(key, part):
    width = HEADS * HD
    noise_key = jax.random.fold_in(key, 5)
    column_scale = jnp.exp(jax.random.uniform(jax.random.fold_in(key, 6), (1, width), jnp.float32, math.log(0.3), math.log(3.0)))
    noise = jax.random.normal(noise_key, (TOKENS, width), jnp.float32)
    result = noise * column_scale
    return jnp.clip(result, -12.0, 12.0).astype(jnp.bfloat16)


def gaussian(rng, extent, scale, limit, kind=jnp.bfloat16):
    values = jax.random.normal(rng, extent, jnp.float32) * scale
    return jnp.minimum(jnp.maximum(values, -limit), limit).astype(kind)


def setup_inputs(seed: int = 0, part: int = 0) -> dict:
    arg_keys = jax.random.split(jax.random.key(seed), 5)
    part_splits = jax.random.split(jax.random.fold_in(arg_keys[4], part), 5)
    return {
        "queries": draw_queries(jax.random.fold_in(jax.random.fold_in(arg_keys[4], part), 71), part),
        "keys": draw_keys(jax.random.fold_in(jax.random.fold_in(arg_keys[4], part), 71), part),
        "values": draw_values(jax.random.fold_in(jax.random.fold_in(arg_keys[4], part), 71), part),
        "w_out": gaussian(arg_keys[3], (HEADS * HD, D), (HEADS * HD) ** -0.5, 0.125),
    }


def reference(queries, keys, values, w_out):
    block_rows = min(512, TOKENS)
    block_count = TOKENS // block_rows
    highest = lax.Precision.HIGHEST
    query_full = queries.astype(jnp.float32).reshape(TOKENS, HEADS, HD)
    key_full = keys.astype(jnp.float32).reshape(TOKENS, HEADS, HD)
    value_full = values.astype(jnp.float32).reshape(TOKENS, HEADS, HD)
    causal = jnp.arange(block_rows)[:, None] >= jnp.arange(block_rows)[None, :]

    def linear_step(state, inputs):
        query_part, key_part, value_part = inputs
        local = jnp.einsum('qhd,khd->hqk', query_part, key_part, precision=highest)
        local = jnp.where(causal[None], local, 0.0)
        intra = jnp.einsum('hqk,khe->qhe', local, value_part, precision=highest)
        inter = jnp.einsum('qhd,hde->qhe', query_part, state, precision=highest)
        state = state + jnp.einsum('khd,khe->hde', key_part, value_part, precision=highest)
        return (state, intra + inter)
    final_state, linear = lax.scan(linear_step, jnp.zeros((HEADS, HD, HD), jnp.float32), (query_full.reshape(block_count, block_rows, HEADS, HD), key_full.reshape(block_count, block_rows, HEADS, HD), value_full.reshape(block_count, block_rows, HEADS, HD)))
    linear = linear.reshape(TOKENS, HEADS, HD)
    normed = linear / jnp.sqrt(lax.optimization_barrier(jnp.mean(linear * linear, axis=-1, keepdims=True)) + 1e-06)
    span = WINDOW + block_rows
    wide_keys = jnp.concatenate([jnp.zeros((WINDOW, HEADS, HD), jnp.float32), key_full], 0)
    wide_values = jnp.concatenate([jnp.zeros((WINDOW, HEADS, HD), jnp.float32), value_full], 0)
    query_pos = jnp.arange(block_rows, dtype=jnp.int32)[:, None]
    key_pos = jnp.arange(span, dtype=jnp.int32)[None, :]
    band = (key_pos > query_pos) & (key_pos <= query_pos + WINDOW)
    scale = 1.0 / math.sqrt(HD)

    def window_block(index):
        begin = (index * block_rows).astype(jnp.int32)
        rows_q = lax.dynamic_slice_in_dim(query_full, begin, block_rows, 0)
        span_k = lax.dynamic_slice_in_dim(wide_keys, begin, span, 0)
        span_v = lax.dynamic_slice_in_dim(wide_values, begin, span, 0)
        valid = band & (begin - WINDOW + key_pos >= 0)
        scores = jnp.einsum('qhd,khd->hqk', rows_q, span_k, precision=highest) * scale
        scores = jnp.where(valid[None], scores, -1e+30)
        top = lax.optimization_barrier(jnp.max(scores, axis=-1, keepdims=True))
        expo = jnp.where(valid[None], jnp.exp(scores - top), 0.0)
        total = lax.optimization_barrier(jnp.sum(expo, axis=-1))
        weights = expo.astype(jnp.bfloat16).astype(jnp.float32)
        summed = jnp.einsum('hqk,khe->qhe', weights, span_v, precision=highest)
        return summed / jnp.transpose(total)[:, :, None]
    windowed = lax.map(window_block, jnp.arange(block_count, dtype=jnp.int32))
    windowed = windowed.reshape(TOKENS, HEADS, HD)
    mixed = (normed + windowed).astype(jnp.bfloat16).reshape(TOKENS, HEADS * HD)
    return jnp.dot(mixed, w_out, preferred_element_type=jnp.float32).astype(jnp.bfloat16)
```

```python
import functools
import math

import jax
import jax.numpy as jnp
from jax import lax
from jax.experimental import pallas as pl
from jax.experimental.pallas import tpu as pltpu
from jax.sharding import PartitionSpec as P

HD = 128
WINDOW = 2048
MESH = pl.DeviceIdType.MESH
F32 = jnp.float32
BF16 = jnp.bfloat16
RATE = math.log2(math.e) / math.sqrt(HD)
FLOOR = -1e30


def dot_nt(a, b):
    return lax.dot_general(a, b, (((1,), (1,)), ((), ())), preferred_element_type=F32)


def dot_tn(a, b):
    return lax.dot_general(a, b, (((0,), (0,)), ((), ())), preferred_element_type=F32)


def recip(x):
    return 1.0 / x


def lanes(index, size):
    return pl.ds(pl.multiple_of(index * size, size), size)


def kernel(
    peers, q_hbm, k_hbm, v_hbm, w_hbm, out_ref, q_ref, k_ref, v_ref,
    w_ref, summed, kbuf, vbuf, qbuf, ebuf, pacc, pstat, o_send, o_recv, o_part, l_send, l_recv, l_part,
    s_send, s_recv, acc, lin, stat, mixed, gathered,
    in_sem, w_sem, kv_tx, kv_rx, q_tx, q_rx, o_tx, o_rx, l_tx, l_rx, p_tx, p_rx, s_tx, s_rx, m_tx, m_rx, turn,
):
    seq = lax.axis_index("seq")
    here = lax.axis_index("head")
    length, width = q_ref.shape
    heads = width // HD
    share = length // peers
    chip, core = here // 2, here % 2
    chips = peers // 2
    order = list(range(2, peers)) + [1, 0]

    def peer_of(index, sign=1):
        hop, flip = index // 2, index % 2
        other = lax.rem(chip + sign * hop + chips, chips)
        return other * 2 + (1 - core if flip else core)

    barrier = pltpu.get_barrier_semaphore()

    def greet(device):
        pl.semaphore_signal(barrier, inc=1, device_id=device, device_id_type=MESH)

    for index in range(1, peers):
        greet({"head": peer_of(index)})
    circle = {0: (1,), 1: (0, 2, 3), 2: (1, 3), 3: (1, 2)}
    for place, friends in circle.items():
        @pl.when(seq == place)
        def _():
            for friend in friends:
                greet({"seq": friend})

    loads = [
        pltpu.make_async_copy(source, target, in_sem.at[i])
        for i, (source, target) in enumerate(((q_hbm, q_ref), (k_hbm, k_ref), (v_hbm, v_ref)))
    ]
    for load in loads:
        load.start()

    def load_w(h, peer):
        return pltpu.make_async_copy(
            w_hbm.at[pl.ds(pl.multiple_of(peer * width + h * HD, HD), HD), :],
            w_ref.at[h, pl.ds(peer * HD, HD), :],
            w_sem.at[h, peer],
        )

    def load_head(h):
        for peer in range(peers):
            load_w(h, peer).start()

    for place, friends in circle.items():
        @pl.when(seq == place)
        def _():
            pl.semaphore_wait(barrier, len(friends) + peers - 1)
    for load in loads:
        load.wait()

    def cols(h):
        return lanes(h, HD)

    def remote(source, target, tx, rx, device):
        return pltpu.make_async_remote_copy(
            src_ref=source, dst_ref=target, send_sem=tx, recv_sem=rx,
            device_id=device, device_id_type=MESH,
        )

    def kv_copies(h):
        return [
            remote(
                source.at[:, cols(h)], target.at[:, cols(h)], kv_tx.at[i, h], kv_rx.at[i, h], {"seq": 1}
            )
            for i, (source, target) in enumerate(((k_ref, kbuf), (v_ref, vbuf)))
        ]

    def near_copies():
        return [
            remote(
                source.at[:, cols(0)], target.at[:, cols(1)], kv_tx.at[i, 1], kv_rx.at[i, 1], {"seq": 2}
            )
            for i, (source, target) in enumerate(((k_ref, kbuf), (v_ref, vbuf)))
        ]

    def far_copies():
        return [
            remote(
                buffer.at[:, cols(0)], buffer.at[:, cols(0)], kv_tx.at[i, 0], kv_rx.at[i, 0], {"seq": 2}
            )
            for i, buffer in enumerate((kbuf, vbuf))
        ]

    def query_copy(h, slot, target):
        return remote(
            q_ref.at[:, cols(h)], qbuf.at[slot, :, cols(h)],
            q_tx.at[slot, h], q_rx.at[slot, h], {"seq": target},
        )

    def relay_copy(h):
        return remote(
            qbuf.at[1, :, cols(h)], qbuf.at[1, :, cols(h)], q_tx.at[1, h], q_rx.at[1, h], {"seq": 1}
        )

    def level_copy(h, slot):
        return remote(
            l_send.at[slot, h], l_recv.at[h], l_tx.at[slot, h], l_rx.at[h], {"seq": 2 + slot}
        )

    def chunk_copy(h, slot, index):
        place = lanes(peer_of(index), share)
        return remote(
            o_send.at[slot, h, :, place], o_recv.at[h, :, place],
            o_tx.at[slot, h, index], o_rx.at[h, index], {"seq": 2 + slot},
        )

    def part_copies(h):
        return (
            remote(l_send.at[1, h], l_part.at[h], p_tx.at[0, h], p_rx.at[0, h], {"seq": 3}),
            remote(o_send.at[1, h], o_part.at[h], p_tx.at[1, h], p_rx.at[1, h], {"seq": 3}),
        )

    def state_copy(h, tx_slot, in_slot, target):
        return remote(
            s_send.at[h], s_recv.at[in_slot, h], s_tx.at[tx_slot, h], s_rx.at[in_slot, h],
            {"seq": target},
        )

    def prefix_copy(h):
        return remote(
            s_recv.at[0, h], s_recv.at[0, h], s_tx.at[1, h], s_rx.at[0, h], {"seq": 3}
        )

    def mixed_copy(h, index):
        target = peer_of(index)
        return remote(
            mixed.at[cols(h), lanes(target, share)], gathered.at[h, lanes(here, HD), :],
            m_tx.at[h, index], m_rx.at[h, index], {"head": target},
        )

    def loop(body, first=0):
        lax.fori_loop(first, heads, lambda h, c: (body(h), c)[1], 0)

    causal = lax.broadcasted_iota(jnp.int32, (length, length), 0) <= lax.broadcasted_iota(
        jnp.int32, (length, length), 1
    )

    def level(top, total):
        return top * RATE + jnp.log2(total)

    def own(h):
        query, key, value = q_ref[:, cols(h)], k_ref[:, cols(h)], v_ref[:, cols(h)]
        scores = dot_nt(key, query)
        kept = jnp.where(causal, scores, 0.0)
        coarse = kept.astype(BF16)
        fine = (kept - coarse.astype(F32)).astype(BF16)
        lin[h] = dot_tn(value, coarse) + dot_tn(value, fine)
        scores = jnp.where(causal, scores, FLOOR)
        top = jnp.max(scores, axis=0, keepdims=True)
        expo = jnp.exp2((scores - top) * RATE)
        total = jnp.sum(expo, axis=0, keepdims=True)
        stat[h, 0:1, :] = level(top, total)
        acc[h] = dot_tn(value, expo.astype(BF16)) * recip(total)

    def part(query, pairs):
        scores = [dot_nt(key, query) for key, _ in pairs]
        top = functools.reduce(jnp.maximum, [jnp.max(s, axis=0, keepdims=True) for s in scores])
        expo = [jnp.exp2((s - top) * RATE) for s in scores]
        total = sum(jnp.sum(e, axis=0, keepdims=True) for e in expo)
        output = sum(dot_tn(value, e.astype(BF16)) for e, (_, value) in zip(expo, pairs))
        return level(top, total), output * recip(total)

    def blend(a, b):
        top = jnp.maximum(a[0], b[0])
        left, right = jnp.exp2(a[0] - top), jnp.exp2(b[0] - top)
        total = left + right
        scale = recip(total)
        return top + jnp.log2(total), (left * scale) * a[1] + (right * scale) * b[1]

    def current(h):
        return stat[h, 0:1, :], acc[h]

    def norm(linear):
        square = jnp.mean(linear * linear, axis=0, keepdims=True)
        return linear * recip(jnp.sqrt(square + 1e-06))

    def finish(h, windowed, linear):
        mixed[cols(h), :] = (norm(linear) + windowed).astype(BF16)
        for index in order[:-1]:
            mixed_copy(h, index).start()
        gathered[h, lanes(here, HD), :] = mixed[cols(h), lanes(here, share)]

    def arrive(h):
        level_copy(h, 0).wait_recv()
        for index in order:
            chunk_copy(h, 0, index).wait_recv()
            place = lanes(peer_of(index), share)
            mine = stat[h, 0:1, place], acc[h, :, place]
            theirs = l_recv[h, 0:1, place], o_recv[h, :, place].astype(F32)
            piece = (lin[h, :, place] + blend(mine, theirs)[1]).astype(BF16)
            if index:
                mixed[cols(h), place] = piece
                mixed_copy(h, index).start()
            else:
                gathered[h, lanes(here, HD), :] = piece

    tile = math.gcd(w_ref.shape[2], 512)

    def project(h):
        for peer in range(peers):
            load_w(h, peer).wait()
        for index in range(1, peers):
            mixed_copy(h, index).wait()
        left = gathered[h].T

        @pl.loop(0, w_ref.shape[2] // tile)
        def _(index):
            part_cols = lanes(index, tile)
            summed[:, part_cols] += jnp.dot(
                left, w_ref[h, :, part_cols], preferred_element_type=F32
            )

    def project_before(h):
        @pl.when(h > 0)
        def _():
            project(h - 1)

    def weights():
        lax.fori_loop(0, heads, lambda h, c: (load_head(h), c)[1], 0)
        summed[...] = jnp.zeros_like(summed)

    @pl.when(seq == 0)
    def _():
        def send(h):
            for copy in kv_copies(h):
                copy.start()

        def work(h):
            own(h)
            finish(h, acc[h], lin[h])
            project_before(h)

        def drain(h):
            kv_copies(h)[1].wait_send()

            @pl.when(h > 0)
            def _():
                kv_copies(h)[0].wait_send()

        @pl.when(core == 0)
        def _():
            loop(send)
            kv_copies(0)[0].wait_send()
            pl.semaphore_signal(
                turn, inc=1, device_id={"head": peer_of(1)}, device_id_type=MESH
            )

        weights()

        @pl.when(core == 1)
        def _():
            pl.semaphore_wait(turn, 1)
            loop(send)
            kv_copies(0)[0].wait_send()

        loop(work)
        loop(drain)

    @pl.when(seq == 1)
    def _():
        for copy in near_copies():
            copy.start()
        weights()
        loop(own)

        def pre(h):
            for slot in range(2):
                query_copy(h, slot, 1).wait_recv()
                bottom, output = part(
                    qbuf[slot, :, cols(h)], ((k_ref[:, cols(h)], v_ref[:, cols(h)]),)
                )
                pstat[slot, 0:1, :] = bottom
                pacc[slot] = output

        def rest(h, early):
            query = q_ref[:, cols(h)]
            windowed = blend(current(h), part(query, ((kbuf[:, cols(h)], vbuf[:, cols(h)]),)))[1]
            finish(h, windowed, lin[h] + dot_nt(early, query))

        def early_state(h):
            return dot_tn(vbuf[:, cols(h)], kbuf[:, cols(h)])

        for arrived, onward in zip(kv_copies(0), far_copies()):
            arrived.wait_recv()
            onward.start()
        rest(0, early_state(0).astype(BF16))
        pre(1)

        def work(h):
            arrived = kv_copies(h)
            arrived[0].wait_recv()
            for slot in range(2):
                scores = dot_nt(kbuf[:, cols(h)], qbuf[slot, :, cols(h)])
                top = jnp.max(scores, axis=0, keepdims=True)
                expo = jnp.exp2((scores - top) * RATE)
                total = jnp.sum(expo, axis=0, keepdims=True)
                pstat[slot, 1:2, :] = level(top, total)
                pstat[slot, 2:3, :] = recip(total)
                ebuf[slot] = expo.astype(BF16)
            arrived[1].wait_recv()
            early = early_state(h)
            s_send[h] = (early + dot_tn(v_ref[:, cols(h)], k_ref[:, cols(h)])).astype(BF16)
            state_copy(h, 0, 0, 2).start()
            for slot in (1, 0):
                fresh = dot_tn(vbuf[:, cols(h)], ebuf[slot]) * pstat[slot, 2:3, :]
                bottom, output = blend(
                    (pstat[slot, 0:1, :], pacc[slot]), (pstat[slot, 1:2, :], fresh)
                )
                l_send[slot, h] = bottom
                o_send[slot, h] = output.astype(BF16)
                level_copy(h, slot).start()
                for index in order:
                    chunk_copy(h, slot, index).start()

            @pl.when(h + 1 < heads)
            def _():
                pre(h + 1)

            rest(h, early.astype(BF16))
            project(h - 1)

        def drain(h):
            state_copy(h, 0, 0, 2).wait_send()
            for slot in range(2):
                level_copy(h, slot).wait_send()
                for index in order:
                    chunk_copy(h, slot, index).wait_send()

        loop(work, 1)
        for copy in near_copies() + far_copies():
            copy.wait_send()
        loop(drain, 1)

    @pl.when(seq == 2)
    def _():
        loop(lambda h: query_copy(h, 0, 1).start(), 1)
        weights()

        def first(h):
            own(h)
            s_send[h] = dot_tn(v_ref[:, cols(h)], k_ref[:, cols(h)]).astype(BF16)
            state_copy(h, 0, 1, 3).start()

        def emit(h, pairs):
            bottom, output = part(qbuf[1, :, cols(h)], pairs)
            l_send[1, h] = bottom
            o_send[1, h] = output.astype(BF16)
            for copy in part_copies(h):
                copy.start()

        def middle(h):
            query_copy(h, 1, 2).wait_recv()
            relay_copy(h).start()
            emit(h, ((k_ref[:, cols(h)], v_ref[:, cols(h)]),))

        loop(first)
        loop(middle, 1)
        query_copy(0, 1, 2).wait_recv()
        for copy in near_copies() + far_copies():
            copy.wait_recv()
        pairs = [(kbuf[:, cols(i)], vbuf[:, cols(i)]) for i in range(2)]
        s_recv[0, 0] = sum(dot_tn(value, key) for key, value in pairs).astype(BF16)
        prefix_copy(0).start()
        emit(0, pairs + [(k_ref[:, cols(0)], v_ref[:, cols(0)])])
        query = q_ref[:, cols(0)]
        windowed = blend(current(0), part(query, pairs))[1]
        finish(0, windowed, lin[0] + dot_nt(s_recv[0, 0], query))

        def second(h):
            state_copy(h, 0, 0, 2).wait_recv()
            prefix_copy(h).start()
            lin[h] = norm(lin[h] + dot_nt(s_recv[0, h], q_ref[:, cols(h)]))
            arrive(h)
            project(h - 1)

        def drain(h):
            @pl.when(h > 0)
            def _():
                query_copy(h, 0, 1).wait_send()
                relay_copy(h).wait_send()

            state_copy(h, 0, 1, 3).wait_send()
            prefix_copy(h).wait_send()
            for copy in part_copies(h):
                copy.wait_send()

        loop(second, 1)
        loop(drain)

    @pl.when(seq == 3)
    def _():
        for h in [1, 0] + list(range(2, heads)):
            query_copy(h, 1, 2).start()
        weights()
        loop(own)

        def join(h):
            for copy in part_copies(h):
                copy.wait_recv()
            bottom, output = blend(current(h), (l_part[h], o_part[h].astype(F32)))
            stat[h, 0:1, :] = bottom
            acc[h] = output
            state_copy(h, 0, 1, 3).wait_recv()
            lin[h] += dot_nt(s_recv[1, h], q_ref[:, cols(h)])

        def linear(h):
            prefix_copy(h).wait_recv()
            return lin[h] + dot_nt(s_recv[0, h], q_ref[:, cols(h)])

        loop(join, 1)
        join(0)
        finish(0, acc[0], linear(0))

        def work(h):
            lin[h] = norm(linear(h))
            arrive(h)
            project(h - 1)

        loop(work, 1)
        loop(lambda h: query_copy(h, 1, 2).wait_send())

    project(heads - 1)
    out_ref[...] = summed[...].astype(BF16)


def fused(queries, keys, values, w_out):
    peers = lax.axis_size("head")
    length, width = queries.shape
    heads = width // HD
    share = length // peers
    dma = pltpu.SemaphoreType.DMA
    vmem = pl.BlockSpec(memory_space=pltpu.VMEM)
    return pl.pallas_call(
        functools.partial(kernel, peers),
        out_shape=jax.ShapeDtypeStruct((share, w_out.shape[1]), BF16),
        in_specs=[pl.BlockSpec(memory_space=pltpu.HBM)] * 4,
        out_specs=vmem,
        scratch_shapes=[
            pltpu.VMEM((length, width), BF16),
            pltpu.VMEM((length, width), BF16),
            pltpu.VMEM((length, width), BF16),
            pltpu.VMEM((heads, peers * HD, w_out.shape[1]), BF16),
            pltpu.VMEM((share, w_out.shape[1]), F32),
            pltpu.VMEM((length, width), BF16),
            pltpu.VMEM((length, width), BF16),
            pltpu.VMEM((2, length, width), BF16),
            pltpu.VMEM((2, length, length), BF16),
            pltpu.VMEM((2, HD, length), F32),
            pltpu.VMEM((2, 8, length), F32),
            pltpu.VMEM((2, heads, HD, length), BF16),
            pltpu.VMEM((heads, HD, length), BF16),
            pltpu.VMEM((heads, HD, length), BF16),
            pltpu.VMEM((2, heads, 1, length), F32),
            pltpu.VMEM((heads, 1, length), F32),
            pltpu.VMEM((heads, 1, length), F32),
            pltpu.VMEM((heads, HD, HD), BF16),
            pltpu.VMEM((2, heads, HD, HD), BF16),
            pltpu.VMEM((heads, HD, length), F32),
            pltpu.VMEM((heads, HD, length), F32),
            pltpu.VMEM((heads, 8, length), F32),
            pltpu.VMEM((width, length), BF16),
            pltpu.VMEM((heads, peers * HD, share), BF16),
            dma((3,)), dma((heads, peers)), dma((2, heads)), dma((2, heads)), dma((2, heads)), dma((2, heads)),
            dma((2, heads, peers)), dma((heads, peers)), dma((2, heads)), dma((heads,)), dma((2, heads)), dma((2, heads)),
            dma((2, heads)), dma((2, heads)), dma((heads, peers)), dma((heads, peers)),
            pltpu.SemaphoreType.REGULAR,
        ],
        compiler_params=pltpu.CompilerParams(
            collective_id=0, has_side_effects=True, vmem_limit_bytes=56 * 1024 * 1024
        ),
    )(queries, keys, values, w_out)


def shifted(value, axis, steps):
    count = lax.axis_size(axis)
    first, last = (max(0, -steps), min(count, count - steps))
    return lax.ppermute(value, axis, [(source, source + steps) for source in range(first, last)])


def fits(queries):
    length, width = queries.shape
    blocks = lax.axis_size("seq")
    share = length // lax.axis_size("head")
    whole = share % HD == 0 and width % HD == 0 and width > HD and lax.axis_size("head") % 2 == 0
    return blocks == 4 and blocks * length <= WINDOW and whole


def per_device(queries, keys, values, w_out):
    if fits(queries):
        return fused(queries, keys, values, w_out)
    length_dev, width = queries.shape
    heads_dev = width // HD
    block_rows = min(512, length_dev)
    block_count = length_dev // block_rows
    highest = lax.Precision.HIGHEST
    seq_index = lax.axis_index("seq")
    q_blocks = queries.reshape(block_count, block_rows, heads_dev, HD)
    k_blocks = keys.reshape(block_count, block_rows, heads_dev, HD)
    v_blocks = values.reshape(block_count, block_rows, heads_dev, HD)
    block_states = jnp.einsum(
        "bkhd,bkhe->bhde", k_blocks, v_blocks, preferred_element_type=jnp.float32
    )
    own_state = jnp.sum(block_states, axis=0)
    earlier = jnp.cumsum(block_states, axis=0) - block_states
    piece = lax.all_gather(own_state[None], "seq", axis=0, tiled=True)
    order = jnp.arange(piece.shape[0], dtype=jnp.int32)
    keep = order < seq_index
    prefix = jnp.sum(jnp.where(keep[:, None, None, None], piece, 0.0), axis=0)
    causal = jnp.arange(block_rows)[:, None] >= jnp.arange(block_rows)[None, :]
    local_scores = jnp.einsum(
        "bqhd,bkhd->bhqk", q_blocks, k_blocks, preferred_element_type=jnp.float32
    )
    local_scores = jnp.where(causal, local_scores, 0.0)
    intra = jnp.einsum(
        "bhqk,bkhe->bqhe", local_scores, v_blocks.astype(jnp.float32), precision=highest
    )
    state_before = prefix[None] + earlier
    inter = jnp.einsum(
        "bqhd,bhde->bqhe", q_blocks.astype(jnp.float32), state_before, precision=highest
    )
    linear = (intra + inter).reshape(length_dev, heads_dev, HD)
    normed = linear / jnp.sqrt(jnp.mean(linear * linear, axis=-1, keepdims=True) + 1e-06)
    reach = min(WINDOW // length_dev, lax.axis_size("seq") - 1)
    received = [shifted((keys, values), "seq", distance) for distance in range(1, reach + 1)]
    pad_rows = WINDOW - reach * length_dev
    filler = jnp.zeros((pad_rows, width), keys.dtype)
    wide_keys = jnp.concatenate([filler] + [pair[0] for pair in reversed(received)] + [keys], 0)
    wide_values = jnp.concatenate([filler] + [pair[1] for pair in reversed(received)] + [values], 0)
    wide_keys = wide_keys.reshape(-1, heads_dev, HD)
    wide_values = wide_values.reshape(-1, heads_dev, HD)
    scale = 1.0 / math.sqrt(HD)
    span = WINDOW + block_rows
    query_pos = jnp.arange(block_rows, dtype=jnp.int32)[:, None]
    key_pos = jnp.arange(span, dtype=jnp.int32)[None, :]
    band = (key_pos > query_pos) & (key_pos <= query_pos + WINDOW)
    rows_q = queries.reshape(block_rows, heads_dev, HD)
    anchor = seq_index * length_dev + 0 - WINDOW
    valid = band & (anchor + key_pos >= 0)
    scores = (
        jnp.einsum("qhd,khd->hqk", rows_q, wide_keys, preferred_element_type=jnp.float32) * scale
    )
    scores = jnp.where(valid[None], scores, -1e30)
    top = jnp.max(scores, axis=-1, keepdims=True)
    expo = jnp.where(valid[None], jnp.exp(scores - top), 0.0)
    total = jnp.sum(expo, axis=-1)
    weights = expo.astype(jnp.bfloat16)
    summed = jnp.einsum("hqk,khe->qhe", weights, wide_values, preferred_element_type=jnp.float32)
    pieces = summed / jnp.transpose(total)[:, :, None]
    mixed = (normed + pieces).astype(jnp.bfloat16).reshape(length_dev, width)
    head_count = lax.axis_size("head")
    share = length_dev // head_count
    grouped = mixed.reshape(head_count, share, width)
    return jnp.dot(
        lax.all_to_all(grouped, "head", split_axis=0, concat_axis=2, tiled=True)[0],
        w_out,
        preferred_element_type=jnp.float32,
    ).astype(jnp.bfloat16)


def solution(mesh):
    return jax.shard_map(
        per_device,
        mesh=mesh,
        in_specs=(
            P(("groups", "seq"), "head"),
            P(("groups", "seq"), "head"),
            P(("groups", "seq"), "head"),
            P(),
        ),
        out_specs=P(("groups", "seq", "head"), None),
        check_vma=False,
    )
```

```python
import functools
import math

import jax
import jax.numpy as jnp
from jax import lax
from jax.experimental import pallas as pl
from jax.experimental.pallas import tpu as pltpu
from jax.sharding import PartitionSpec as P

HD = 128
WINDOW = 2048
MESH = pl.DeviceIdType.MESH
F32 = jnp.float32
BF16 = jnp.bfloat16
RATE = math.log2(math.e) / math.sqrt(HD)
FLOOR = -1e30


def dot_nt(a, b):
    return lax.dot_general(a, b, (((1,), (1,)), ((), ())), preferred_element_type=F32)


def dot_tn(a, b):
    return lax.dot_general(a, b, (((0,), (0,)), ((), ())), preferred_element_type=F32)


def recip(x):
    return 1.0 / x


def lanes(index, size):
    return pl.ds(pl.multiple_of(index * size, size), size)


def kernel(
    peers, q_hbm, k_hbm, v_hbm, w_hbm, out_ref, q_ref, k_ref, v_ref,
    w_ref, summed, kbuf, vbuf, qbuf, ebuf, pacc, pstat, o_send, o_recv, o_part, l_send, l_recv, l_part,
    s_send, s_recv, acc, lin, stat, mixed, gathered,
    in_sem, w_sem, tx, kv_rx, q_rx, o_rx, l_rx, s_rx, m_rx,
):
    seq = lax.axis_index("seq")
    here = lax.axis_index("head")
    length, width = q_ref.shape
    heads = width // HD
    share = length // peers
    chip, core = here // 2, here % 2
    chips = peers // 2
    order = list(range(2, peers)) + [1, 0]

    def peer_of(index, sign=1):
        hop, flip = index // 2, index % 2
        other = lax.rem(chip + sign * hop + chips, chips)
        return other * 2 + (1 - core if flip else core)

    barrier = pltpu.get_barrier_semaphore()

    def greet(device):
        pl.semaphore_signal(barrier, inc=1, device_id=device, device_id_type=MESH)

    for index in range(1, peers):
        greet({"head": peer_of(index)})
    circle = {0: (1,), 1: (0, 2, 3), 2: (1, 3), 3: (1, 2)}
    for place, friends in circle.items():
        @pl.when(seq == place)
        def _():
            for friend in friends:
                greet({"seq": friend})

    loads = [
        pltpu.make_async_copy(source, target, in_sem.at[i])
        for i, (source, target) in enumerate(((q_hbm, q_ref), (k_hbm, k_ref), (v_hbm, v_ref)))
    ]
    for load in loads:
        load.start()

    def load_w(h, peer):
        return pltpu.make_async_copy(
            w_hbm.at[pl.ds(pl.multiple_of(peer * width + h * HD, HD), HD), :],
            w_ref.at[h, pl.ds(peer * HD, HD), :],
            w_sem.at[h],
        )

    def load_head(h):
        for peer in range(peers):
            load_w(h, peer).start()

    for place, friends in circle.items():
        @pl.when(seq == place)
        def _():
            pl.semaphore_wait(barrier, len(friends) + peers - 1)
    for load in loads:
        load.wait()

    def cols(h):
        return lanes(h, HD)

    def remote(source, target, sent, landed, device):
        return pltpu.make_async_remote_copy(
            src_ref=source, dst_ref=target, send_sem=tx.at[sent], recv_sem=landed,
            device_id=device, device_id_type=MESH,
        )

    def settle(ref, semaphore):
        pltpu.make_async_copy(ref, ref, semaphore).wait()

    def kv_copies(h, target=1, first=0):
        return [
            remote(
                source.at[:, cols(h)], buffer.at[:, cols(h)], first + i, kv_rx.at[i, h], {"seq": target}
            )
            for i, (source, buffer) in enumerate(((k_ref, kbuf), (v_ref, vbuf)))
        ]

    def near_copies():
        return [
            remote(
                source.at[:, cols(0)], buffer.at[:, cols(1)], i, kv_rx.at[i, 1], {"seq": 2}
            )
            for i, (source, buffer) in enumerate(((k_ref, kbuf), (v_ref, vbuf)))
        ]

    def far_copies():
        return [
            remote(
                buffer.at[:, cols(0)], buffer.at[:, cols(0)], 2 + i, kv_rx.at[i, 0], {"seq": 2}
            )
            for i, buffer in enumerate((kbuf, vbuf))
        ]

    def query_copy(h, slot, target, sent):
        return remote(
            q_ref.at[:, cols(h)], qbuf.at[slot, :, cols(h)], sent, q_rx.at[slot, h], {"seq": target}
        )

    def relay_copy(h):
        return remote(
            qbuf.at[1, :, cols(h)], qbuf.at[1, :, cols(h)], 1, q_rx.at[1, h], {"seq": 1}
        )

    def level_copy(h, slot):
        return remote(l_send.at[slot, h], l_recv.at[h], 5, l_rx.at[h - 1], {"seq": 2 + slot})

    def chunk_copy(h, slot, index):
        place = lanes(peer_of(index), share)
        return remote(
            o_send.at[slot, h, :, place], o_recv.at[h, :, place], 6, o_rx.at[h - 1, index],
            {"seq": 2 + slot},
        )

    def part_copies(h):
        return (
            remote(l_send.at[1, h], l_part.at[h], 5, q_rx.at[0, h], {"seq": 3}),
            remote(o_send.at[1, h], o_part.at[h], 6, q_rx.at[1, h], {"seq": 3}),
        )

    def state_copy(h, slot, target):
        return remote(
            s_send.at[h], s_recv.at[slot, h], 4, s_rx.at[slot, h], {"seq": target}
        )

    def prefix_copy(h):
        return remote(
            s_recv.at[0, h], s_recv.at[0, h], 7, s_rx.at[0, h], {"seq": 3}
        )

    def mixed_copy(h, index):
        target = peer_of(index)
        return remote(
            mixed.at[cols(h), lanes(target, share)], gathered.at[h, lanes(here, HD), :],
            8, m_rx.at[h], {"head": target},
        )

    def loop(body, first=0, last=heads):
        lax.fori_loop(first, last, lambda h, c: (body(h), c)[1], 0)

    causal = lax.broadcasted_iota(jnp.int32, (length, length), 0) <= lax.broadcasted_iota(
        jnp.int32, (length, length), 1
    )

    def level(top, total):
        return top * RATE + jnp.log2(total)

    def own(h):
        query, key, value = q_ref[:, cols(h)], k_ref[:, cols(h)], v_ref[:, cols(h)]
        scores = dot_nt(key, query)
        kept = jnp.where(causal, scores, 0.0)
        coarse = kept.astype(BF16)
        fine = (kept - coarse.astype(F32)).astype(BF16)
        lin[h] = dot_tn(value, coarse) + dot_tn(value, fine)
        scores = jnp.where(causal, scores, FLOOR)
        top = jnp.max(scores, axis=0, keepdims=True)
        expo = jnp.exp2((scores - top) * RATE)
        total = jnp.sum(expo, axis=0, keepdims=True)
        stat[h, 0:1, :] = level(top, total)
        acc[h] = dot_tn(value, expo.astype(BF16)) * recip(total)

    def part(query, pairs):
        scores = [dot_nt(key, query) for key, _ in pairs]
        top = functools.reduce(jnp.maximum, [jnp.max(s, axis=0, keepdims=True) for s in scores])
        expo = [jnp.exp2((s - top) * RATE) for s in scores]
        total = sum(jnp.sum(e, axis=0, keepdims=True) for e in expo)
        output = sum(dot_tn(value, e.astype(BF16)) for e, (_, value) in zip(expo, pairs))
        return level(top, total), output * recip(total)

    def blend(a, b):
        top = jnp.maximum(a[0], b[0])
        left, right = jnp.exp2(a[0] - top), jnp.exp2(b[0] - top)
        total = left + right
        scale = recip(total)
        return top + jnp.log2(total), (left * scale) * a[1] + (right * scale) * b[1]

    def current(h):
        return stat[h, 0:1, :], acc[h]

    def norm(linear):
        square = jnp.mean(linear * linear, axis=0, keepdims=True)
        return linear * recip(jnp.sqrt(square + 1e-06))

    def finish(h, windowed, linear):
        mixed[cols(h), :] = (norm(linear) + windowed).astype(BF16)
        for index in order[:-1]:
            mixed_copy(h, index).start()
        gathered[h, lanes(here, HD), :] = mixed[cols(h), lanes(here, share)]

    def arrive(h):
        level_copy(h, 0).wait_recv()
        for index in order:
            chunk_copy(h, 0, index).wait_recv()
            place = lanes(peer_of(index), share)
            mine = stat[h, 0:1, place], acc[h, :, place]
            theirs = l_recv[h, 0:1, place], o_recv[h, :, place].astype(F32)
            piece = (lin[h, :, place] + blend(mine, theirs)[1]).astype(BF16)
            if index:
                mixed[cols(h), place] = piece
                mixed_copy(h, index).start()
            else:
                gathered[h, lanes(here, HD), :] = piece

    tile = math.gcd(w_ref.shape[2], 512)

    def project(h, target=None):
        settle(w_ref.at[h], w_sem.at[h])
        settle(gathered.at[h, pl.ds(0, (peers - 1) * HD)], m_rx.at[h])
        left = gathered[h].T
        target = summed if target is None else target
        for begin in range(0, w_ref.shape[2], tile):
            piece = slice(begin, begin + tile)
            product = jnp.dot(left, w_ref[h, :, piece], preferred_element_type=F32)
            target[:, piece] = (summed[:, piece] + product).astype(target.dtype)

    def project_before(h):
        @pl.when(h > 0)
        def _():
            project(h - 1)

    def weights():
        lax.fori_loop(0, heads, lambda h, c: (load_head(h), c)[1], 0)
        summed[...] = jnp.zeros_like(summed)

    direct = range(1, heads - 1)
    wide = [0, heads - 1]
    later = pl.ds(1, heads - 1)

    @pl.when(seq == 0)
    def _():
        def send(h):
            for copy in kv_copies(h):
                copy.start()

        def work(h):
            finish(h, acc[h], lin[h])
            project_before(h)

        @pl.when(core == 0)
        def _():
            loop(send)

        loop(own, 0, 2)

        @pl.when(core == 1)
        def _():
            loop(send)

        weights()
        loop(own, 2)
        loop(work)
        settle(k_ref, tx.at[0])
        settle(v_ref, tx.at[1])

    @pl.when(seq == 1)
    def _():
        for copy in near_copies():
            copy.start()
        weights()
        loop(own)

        def pre(h):
            for slot in range(2):
                query_copy(h, slot, 1, 0).wait_recv()
                bottom, output = part(
                    qbuf[slot, :, cols(h)], ((k_ref[:, cols(h)], v_ref[:, cols(h)]),)
                )
                pstat[slot, 0:1, :] = bottom
                pacc[slot] = output

        def rest(h, early):
            query = q_ref[:, cols(h)]
            windowed = blend(current(h), part(query, ((kbuf[:, cols(h)], vbuf[:, cols(h)]),)))[1]
            finish(h, windowed, lin[h] + dot_nt(early, query))

        def early_state(h):
            return dot_tn(vbuf[:, cols(h)], kbuf[:, cols(h)])

        for arrived, onward in zip(kv_copies(0), far_copies()):
            arrived.wait_recv()
            onward.start()
        rest(0, early_state(0).astype(BF16))
        pre(1)

        def work(h):
            arrived = kv_copies(h)
            arrived[0].wait_recv()
            for slot in range(2):
                scores = dot_nt(kbuf[:, cols(h)], qbuf[slot, :, cols(h)])
                top = jnp.max(scores, axis=0, keepdims=True)
                expo = jnp.exp2((scores - top) * RATE)
                total = jnp.sum(expo, axis=0, keepdims=True)
                pstat[slot, 1:2, :] = level(top, total)
                pstat[slot, 2:3, :] = recip(total)
                ebuf[slot] = expo.astype(BF16)
            arrived[1].wait_recv()
            early = early_state(h)
            s_send[h] = (early + dot_tn(v_ref[:, cols(h)], k_ref[:, cols(h)])).astype(BF16)
            state_copy(h, 0, 2).start()
            for slot in (1, 0):
                fresh = dot_tn(vbuf[:, cols(h)], ebuf[slot]) * pstat[slot, 2:3, :]
                bottom, output = blend(
                    (pstat[slot, 0:1, :], pacc[slot]), (pstat[slot, 1:2, :], fresh)
                )
                l_send[slot, h] = bottom
                o_send[slot, h] = output.astype(BF16)
                level_copy(h, slot).start()
                for index in order[:-2]:
                    chunk_copy(h, slot, index).start()
            for slot in (1, 0):
                for index in order[-2:]:
                    chunk_copy(h, slot, index).start()

            @pl.when(h + 1 < heads)
            def _():
                pre(h + 1)

            rest(h, early.astype(BF16))
            project(h - 1)

        loop(work, 1)
        for copy in near_copies() + far_copies():
            copy.wait_send()
        settle(s_send.at[later], tx.at[4])
        settle(l_send.at[:, later], tx.at[5])
        settle(o_send.at[:, later], tx.at[6])

    @pl.when(seq == 2)
    def _():
        for h in range(1, heads):
            query_copy(h, 0, 1, 0).start()
        for h in direct:
            for copy in kv_copies(h, 3, 2):
                copy.start()
        weights()
        loop(own)
        for h in wide:
            s_send[h] = dot_tn(v_ref[:, cols(h)], k_ref[:, cols(h)]).astype(BF16)
            state_copy(h, 1, 3).start()

        def emit(h, pairs):
            bottom, output = part(qbuf[1, :, cols(h)], pairs)
            l_send[1, h] = bottom
            o_send[1, h] = output.astype(BF16)
            for copy in part_copies(h):
                copy.start()

        def pair(h):
            return k_ref[:, cols(h)], v_ref[:, cols(h)]

        query_copy(heads - 1, 1, 2, 0).wait_recv()
        relay_copy(heads - 1).start()
        emit(heads - 1, (pair(heads - 1),))
        query_copy(0, 1, 2, 0).wait_recv()
        for copy in near_copies() + far_copies():
            copy.wait_recv()
        pairs = [(kbuf[:, cols(i)], vbuf[:, cols(i)]) for i in range(2)]
        s_recv[0, 0] = sum(dot_tn(value, key) for key, value in pairs).astype(BF16)
        prefix_copy(0).start()
        emit(0, pairs + [pair(0)])
        query = q_ref[:, cols(0)]
        windowed = blend(current(0), part(query, pairs))[1]
        finish(0, windowed, lin[0] + dot_nt(s_recv[0, 0], query))

        def second(h):
            state_copy(h, 0, 2).wait_recv()
            prefix_copy(h).start()
            lin[h] = norm(lin[h] + dot_nt(s_recv[0, h], q_ref[:, cols(h)]))
            arrive(h)
            project(h - 1)

        loop(second, 1)
        settle(q_ref.at[:, pl.ds(HD, width - HD)], tx.at[0])
        relay_copy(heads - 1).wait_send()
        if len(direct):
            inner = pl.ds(HD, width - 2 * HD)
            settle(k_ref.at[:, inner], tx.at[2])
            settle(v_ref.at[:, inner], tx.at[3])
        settle(s_send.at[pl.ds(0, 2)], tx.at[4])
        settle(l_send.at[1, pl.ds(0, 2)], tx.at[5])
        settle(o_send.at[1, pl.ds(0, 2)], tx.at[6])
        settle(s_recv.at[0], tx.at[7])

    @pl.when(seq == 3)
    def _():
        for h in sorted(range(heads), key=lambda h: h if h else 1.5):
            if h in direct:
                query_copy(h, 1, 1, 0).start()
            else:
                query_copy(h, 1, 2, 1).start()
        weights()
        loop(own)

        def join(h):
            query = q_ref[:, cols(h)]
            if h in direct:
                for copy in kv_copies(h, 3, 2):
                    copy.wait_recv()
                key, value = kbuf[:, cols(h)], vbuf[:, cols(h)]
                extra = part(query, ((key, value),))
                step = dot_tn(value, key).astype(BF16)
            else:
                for copy in part_copies(h):
                    copy.wait_recv()
                state_copy(h, 1, 3).wait_recv()
                extra = l_part[h], o_part[h].astype(F32)
                step = s_recv[1, h]
            bottom, output = blend(current(h), extra)
            stat[h, 0:1, :] = bottom
            acc[h] = output
            lin[h] += dot_nt(step, query)

        def linear(h):
            prefix_copy(h).wait_recv()
            return lin[h] + dot_nt(s_recv[0, h], q_ref[:, cols(h)])

        def work(h):
            lin[h] = norm(linear(h))
            arrive(h)
            project(h - 1)

        for h in direct:
            join(h)
        join(heads - 1)
        join(0)
        finish(0, acc[0], linear(0))
        loop(work, 1)
        if len(direct):
            settle(q_ref.at[:, pl.ds(HD, width - 2 * HD)], tx.at[0])
        settle(q_ref.at[:, pl.ds(0, 2 * HD)], tx.at[1])

    project(heads - 1, out_ref)
    settle(mixed.at[:, pl.ds(0, length - share)], tx.at[8])


def fused(queries, keys, values, w_out):
    peers = lax.axis_size("head")
    length, width = queries.shape
    heads = width // HD
    share = length // peers
    dma = pltpu.SemaphoreType.DMA
    vmem = pl.BlockSpec(memory_space=pltpu.VMEM)
    return pl.pallas_call(
        functools.partial(kernel, peers),
        out_shape=pltpu.VMEM((share, w_out.shape[1]), BF16),
        in_specs=[pl.BlockSpec(memory_space=pltpu.HBM)] * 4,
        out_specs=vmem,
        scratch_shapes=[
            pltpu.VMEM((length, width), BF16),
            pltpu.VMEM((length, width), BF16),
            pltpu.VMEM((length, width), BF16),
            pltpu.VMEM((heads, peers * HD, w_out.shape[1]), BF16),
            pltpu.VMEM((share, w_out.shape[1]), F32),
            pltpu.VMEM((length, width), BF16),
            pltpu.VMEM((length, width), BF16),
            pltpu.VMEM((2, length, width), BF16),
            pltpu.VMEM((2, length, length), BF16),
            pltpu.VMEM((2, HD, length), F32),
            pltpu.VMEM((2, 8, length), F32),
            pltpu.VMEM((2, heads, HD, length), BF16),
            pltpu.VMEM((heads, HD, length), BF16),
            pltpu.VMEM((heads, HD, length), BF16),
            pltpu.VMEM((2, heads, 1, length), F32),
            pltpu.VMEM((heads, 1, length), F32),
            pltpu.VMEM((heads, 1, length), F32),
            pltpu.VMEM((heads, HD, HD), BF16),
            pltpu.VMEM((2, heads, HD, HD), BF16),
            pltpu.VMEM((heads, HD, length), F32),
            pltpu.VMEM((heads, HD, length), F32),
            pltpu.VMEM((heads, 8, length), F32),
            pltpu.VMEM((width, length), BF16),
            pltpu.VMEM((heads, peers * HD, share), BF16),
            dma((3,)), dma((heads,)), dma((9,)), dma((2, heads)), dma((2, heads)), dma((heads - 1, peers)),
            dma((heads - 1,)), dma((2, heads)), dma((heads,)),
        ],
        compiler_params=pltpu.CompilerParams(
            collective_id=0, has_side_effects=True, vmem_limit_bytes=56 * 1024 * 1024
        ),
    )(queries, keys, values, w_out)


def shifted(value, axis, steps):
    count = lax.axis_size(axis)
    first, last = (max(0, -steps), min(count, count - steps))
    return lax.ppermute(value, axis, [(source, source + steps) for source in range(first, last)])


def fits(queries):
    length, width = queries.shape
    blocks = lax.axis_size("seq")
    share = length // lax.axis_size("head")
    whole = share % HD == 0 and width % HD == 0 and width > HD and lax.axis_size("head") % 2 == 0
    return blocks == 4 and blocks * length <= WINDOW and whole


def per_device(queries, keys, values, w_out):
    if fits(queries):
        return fused(queries, keys, values, w_out)
    length_dev, width = queries.shape
    heads_dev = width // HD
    block_rows = min(512, length_dev)
    block_count = length_dev // block_rows
    highest = lax.Precision.HIGHEST
    seq_index = lax.axis_index("seq")
    q_blocks = queries.reshape(block_count, block_rows, heads_dev, HD)
    k_blocks = keys.reshape(block_count, block_rows, heads_dev, HD)
    v_blocks = values.reshape(block_count, block_rows, heads_dev, HD)
    block_states = jnp.einsum(
        "bkhd,bkhe->bhde", k_blocks, v_blocks, preferred_element_type=jnp.float32
    )
    own_state = jnp.sum(block_states, axis=0)
    earlier = jnp.cumsum(block_states, axis=0) - block_states
    piece = lax.all_gather(own_state[None], "seq", axis=0, tiled=True)
    order = jnp.arange(piece.shape[0], dtype=jnp.int32)
    keep = order < seq_index
    prefix = jnp.sum(jnp.where(keep[:, None, None, None], piece, 0.0), axis=0)
    causal = jnp.arange(block_rows)[:, None] >= jnp.arange(block_rows)[None, :]
    local_scores = jnp.einsum(
        "bqhd,bkhd->bhqk", q_blocks, k_blocks, preferred_element_type=jnp.float32
    )
    local_scores = jnp.where(causal, local_scores, 0.0)
    intra = jnp.einsum(
        "bhqk,bkhe->bqhe", local_scores, v_blocks.astype(jnp.float32), precision=highest
    )
    state_before = prefix[None] + earlier
    inter = jnp.einsum(
        "bqhd,bhde->bqhe", q_blocks.astype(jnp.float32), state_before, precision=highest
    )
    linear = (intra + inter).reshape(length_dev, heads_dev, HD)
    normed = linear / jnp.sqrt(jnp.mean(linear * linear, axis=-1, keepdims=True) + 1e-06)
    reach = min(WINDOW // length_dev, lax.axis_size("seq") - 1)
    received = [shifted((keys, values), "seq", distance) for distance in range(1, reach + 1)]
    pad_rows = WINDOW - reach * length_dev
    filler = jnp.zeros((pad_rows, width), keys.dtype)
    wide_keys = jnp.concatenate([filler] + [pair[0] for pair in reversed(received)] + [keys], 0)
    wide_values = jnp.concatenate([filler] + [pair[1] for pair in reversed(received)] + [values], 0)
    wide_keys = wide_keys.reshape(-1, heads_dev, HD)
    wide_values = wide_values.reshape(-1, heads_dev, HD)
    scale = 1.0 / math.sqrt(HD)
    span = WINDOW + block_rows
    query_pos = jnp.arange(block_rows, dtype=jnp.int32)[:, None]
    key_pos = jnp.arange(span, dtype=jnp.int32)[None, :]
    band = (key_pos > query_pos) & (key_pos <= query_pos + WINDOW)
    rows_q = queries.reshape(block_rows, heads_dev, HD)
    anchor = seq_index * length_dev + 0 - WINDOW
    valid = band & (anchor + key_pos >= 0)
    scores = (
        jnp.einsum("qhd,khd->hqk", rows_q, wide_keys, preferred_element_type=jnp.float32) * scale
    )
    scores = jnp.where(valid[None], scores, -1e30)
    top = jnp.max(scores, axis=-1, keepdims=True)
    expo = jnp.where(valid[None], jnp.exp(scores - top), 0.0)
    total = jnp.sum(expo, axis=-1)
    weights = expo.astype(jnp.bfloat16)
    summed = jnp.einsum("hqk,khe->qhe", weights, wide_values, preferred_element_type=jnp.float32)
    pieces = summed / jnp.transpose(total)[:, :, None]
    mixed = (normed + pieces).astype(jnp.bfloat16).reshape(length_dev, width)
    head_count = lax.axis_size("head")
    share = length_dev // head_count
    grouped = mixed.reshape(head_count, share, width)
    return jnp.dot(
        lax.all_to_all(grouped, "head", split_axis=0, concat_axis=2, tiled=True)[0],
        w_out,
        preferred_element_type=jnp.float32,
    ).astype(jnp.bfloat16)


def solution(mesh):
    return jax.shard_map(
        per_device,
        mesh=mesh,
        in_specs=(
            P(("groups", "seq"), "head"),
            P(("groups", "seq"), "head"),
            P(("groups", "seq"), "head"),
            P(),
        ),
        out_specs=P(("groups", "seq", "head"), None),
        check_vma=False,
    )
```

```python
import functools
import math

import jax
import jax.numpy as jnp
from jax import lax
from jax.experimental import pallas as pl
from jax.experimental.pallas import tpu as pltpu
from jax.sharding import PartitionSpec as P

HD = 128
WINDOW = 2048
MESH = pl.DeviceIdType.MESH
F32 = jnp.float32
BF16 = jnp.bfloat16
RATE = math.log2(math.e) / math.sqrt(HD)
FLOOR = -1e30


def dot_nt(a, b):
    return lax.dot_general(a, b, (((1,), (1,)), ((), ())), preferred_element_type=F32)


def dot_tn(a, b):
    return lax.dot_general(a, b, (((0,), (0,)), ((), ())), preferred_element_type=F32)


def recip(x):
    return 1.0 / x


def lanes(index, size):
    return pl.ds(pl.multiple_of(index * size, size), size)


def kernel(
    peers, q_hbm, k_hbm, v_hbm, w_hbm, out_ref, q_ref, k_ref, v_ref,
    w_ref, summed, kbuf, vbuf, qbuf, ebuf, pacc, pstat, o_send, o_recv, l_send, l_recv,
    s_own, s_send, s_recv, acc, lin, stat, mixed, gathered,
    in_sem, w_sem, tx, kv_rx, q_rx, o_rx, l_rx, s_rx, m_rx, gate,
):
    seq = lax.axis_index("seq")
    here = lax.axis_index("head")
    length, width = q_ref.shape
    heads = width // HD
    share = length // peers
    chip, core = here // 2, here % 2
    chips = peers // 2
    order = list(range(2, peers)) + [1, 0]

    def peer_of(index, sign=1):
        hop, flip = index // 2, index % 2
        other = lax.rem(chip + sign * hop + chips, chips)
        return other * 2 + (1 - core if flip else core)

    barrier = pltpu.get_barrier_semaphore()

    def greet(device):
        pl.semaphore_signal(barrier, inc=1, device_id=device, device_id_type=MESH)

    circle = {0: (1,), 1: (0, 2, 3), 2: (1, 3), 3: (2,)}
    near = {0: (1,), 1: (), 2: range(1, peers), 3: range(1, peers)}
    for place, friends in circle.items():
        @pl.when(seq == place)
        def _():
            for friend in friends:
                greet({"seq": friend})

            for index in near[place]:
                greet({"head": peer_of(index)})

    loads = [
        pltpu.make_async_copy(source, target, in_sem.at[i])
        for i, (source, target) in enumerate(((q_hbm, q_ref), (k_hbm, k_ref), (v_hbm, v_ref)))
    ]
    for load in loads:
        load.start()

    def load_w(h, peer):
        return pltpu.make_async_copy(
            w_hbm.at[pl.ds(pl.multiple_of(peer * width + h * HD, HD), HD), :],
            w_ref.at[h, pl.ds(peer * HD, HD), :],
            w_sem.at[h],
        )

    def load_head(h):
        for peer in range(peers):
            load_w(h, peer).start()

    for place in circle:
        @pl.when(seq == place)
        def _():
            count = sum(place in friends for friends in circle.values())
            pl.semaphore_wait(barrier, count + len(near[place]))
    for load in loads:
        load.wait()

    def cols(h):
        return lanes(h, HD)

    def remote(source, target, sent, landed, device):
        return pltpu.make_async_remote_copy(
            src_ref=source, dst_ref=target, send_sem=tx.at[sent], recv_sem=landed,
            device_id=device, device_id_type=MESH,
        )

    def settle(ref, semaphore):
        pltpu.make_async_copy(ref, ref, semaphore).wait()

    def kv_copies(h):
        return [
            remote(
                source.at[:, cols(h)], buffer.at[:, cols(h)], i, kv_rx.at[i, h], {"seq": 1}
            )
            for i, (source, buffer) in enumerate(((k_ref, kbuf), (v_ref, vbuf)))
        ]

    def near_copies():
        return [
            remote(
                source.at[:, cols(0)], buffer.at[:, cols(1)], i, kv_rx.at[i, 1], {"seq": 2}
            )
            for i, (source, buffer) in enumerate(((k_ref, kbuf), (v_ref, vbuf)))
        ]

    def far_copies():
        return [
            remote(
                buffer.at[:, cols(0)], buffer.at[:, cols(0)], 2 + i, kv_rx.at[i, 0], {"seq": 2}
            )
            for i, buffer in enumerate((kbuf, vbuf))
        ]

    def query_copy(h, slot, target, sent):
        return remote(
            q_ref.at[:, cols(h)], qbuf.at[slot, :, cols(h)], sent, q_rx.at[slot, h], {"seq": target}
        )

    def relay_copy(h):
        return remote(
            qbuf.at[1, :, cols(h)], qbuf.at[1, :, cols(h)], 1, q_rx.at[1, h], {"seq": 1}
        )

    def row(h, slot):
        return slot * (heads - 1) + h - 1

    def level_copy(h, slot):
        return remote(
            l_send.at[slot, h], l_recv.at[slot, h], 5, l_rx.at[row(h, slot)], {"seq": 2}
        )

    def chunk_copy(h, slot, index):
        place = lanes(peer_of(index), share)
        return remote(
            o_send.at[slot, h, :, place], o_recv.at[slot, h, :, place], 6,
            o_rx.at[row(h, slot), index], {"seq": 2},
        )

    def level_onward(h):
        return remote(l_send.at[1, h], l_recv.at[1, h], 5, l_rx.at[h], {"seq": 3})

    def chunk_onward(h, index):
        place = lanes(peer_of(index), share)
        return remote(
            o_send.at[1, h, :, place], o_recv.at[1, h, :, place], 6, o_rx.at[h, index], {"seq": 3}
        )

    def part_copies():
        h = heads - 1
        return (
            remote(l_send.at[0, h], l_recv.at[0, h], 2, q_rx.at[0, 0], {"seq": 3}),
            remote(o_send.at[0, h], o_recv.at[0, h], 3, q_rx.at[1, 0], {"seq": 3}),
        )

    def state_copy(h, target):
        return remote(s_send.at[h], s_recv.at[h], 4, s_rx.at[h], {"seq": target})

    def mixed_copy(h, index):
        target = peer_of(index)
        return remote(
            mixed.at[cols(h), lanes(target, share)], gathered.at[h, lanes(here, HD), :],
            8, m_rx.at[h], {"head": target},
        )

    def loop(body, first=0, last=heads):
        lax.fori_loop(first, last, lambda h, c: (body(h), c)[1], 0)

    causal = lax.broadcasted_iota(jnp.int32, (length, length), 0) <= lax.broadcasted_iota(
        jnp.int32, (length, length), 1
    )

    def level(top, total):
        return top * RATE + jnp.log2(total)

    def own(h):
        query, key, value = q_ref[:, cols(h)], k_ref[:, cols(h)], v_ref[:, cols(h)]
        scores = dot_nt(key, query)
        kept = jnp.where(causal, scores, 0.0)
        coarse = kept.astype(BF16)
        fine = (kept - coarse.astype(F32)).astype(BF16)
        lin[h] = dot_tn(value, coarse) + dot_tn(value, fine)
        scores = jnp.where(causal, scores, FLOOR)
        top = jnp.max(scores, axis=0, keepdims=True)
        expo = jnp.exp2((scores - top) * RATE)
        total = jnp.sum(expo, axis=0, keepdims=True)
        stat[h, 0:1, :] = level(top, total)
        acc[h] = dot_tn(value, expo.astype(BF16)) * recip(total)

    def part(query, pairs):
        scores = [dot_nt(key, query) for key, _ in pairs]
        top = functools.reduce(jnp.maximum, [jnp.max(s, axis=0, keepdims=True) for s in scores])
        expo = [jnp.exp2((s - top) * RATE) for s in scores]
        total = sum(jnp.sum(e, axis=0, keepdims=True) for e in expo)
        output = sum(dot_tn(value, e.astype(BF16)) for e, (_, value) in zip(expo, pairs))
        return level(top, total), output * recip(total)

    def blend(a, b):
        top = jnp.maximum(a[0], b[0])
        left, right = jnp.exp2(a[0] - top), jnp.exp2(b[0] - top)
        total = left + right
        scale = recip(total)
        return top + jnp.log2(total), (left * scale) * a[1] + (right * scale) * b[1]

    def current(h):
        return stat[h, 0:1, :], acc[h]

    def norm(linear):
        square = jnp.mean(linear * linear, axis=0, keepdims=True)
        return linear * recip(jnp.sqrt(square + 1e-06))

    def finish(h, windowed, linear):
        mixed[cols(h), :] = (norm(linear) + windowed).astype(BF16)
        for index in order[:-1]:
            mixed_copy(h, index).start()
        gathered[h, lanes(here, HD), :] = mixed[cols(h), lanes(here, share)]

    def arrive(h, slot, level_of, chunk_of, final=False):
        level_of(h).wait_recv()
        for index in order:
            if final and index == order[-2]:
                project_before(h)
            chunk_of(h, index).wait_recv()
            place = lanes(peer_of(index), share)
            mine = stat[h, 0:1, place], acc[h, :, place]
            theirs = l_recv[slot, h, 0:1, place], o_recv[slot, h, :, place].astype(F32)
            piece = (lin[h, :, place] + blend(mine, theirs)[1]).astype(BF16)
            if index:
                mixed[cols(h), place] = piece
                mixed_copy(h, index).start()
            else:
                gathered[h, lanes(here, HD), :] = piece

    tile = math.gcd(w_ref.shape[2], 512)

    def project(h, target=None):
        settle(w_ref.at[h], w_sem.at[h])
        settle(gathered.at[h, pl.ds(0, (peers - 1) * HD)], m_rx.at[h])
        left = gathered[h].T
        target = summed if target is None else target
        for begin in range(0, w_ref.shape[2], tile):
            piece = slice(begin, begin + tile)
            product = jnp.dot(left, w_ref[h, :, piece], preferred_element_type=F32)
            target[:, piece] = (summed[:, piece] + product).astype(target.dtype)

    def project_before(h):
        if isinstance(h, int):
            project(h - 1)
        else:
            pl.when(h > 0)(lambda: project(h - 1))

    def weights():
        lax.fori_loop(0, heads, lambda h, c: (load_head(h), c)[1], 0)
        summed[...] = jnp.zeros_like(summed)

    def tell(slot, device):
        pl.semaphore_signal(gate.at[slot], inc=1, device_id=device, device_id_type=MESH)

    def own_state(h):
        return dot_tn(v_ref[:, cols(h)], k_ref[:, cols(h)])

    later = pl.ds(1, heads - 1)

    @pl.when(seq == 0)
    def _():
        def send(h):
            for copy in kv_copies(h):
                copy.start()

        def work(h):
            finish(h, acc[h], lin[h])
            project_before(h)

        @pl.when(core == 0)
        def _():
            loop(send)
            tell(1, {"head": peer_of(1)})

        weights()

        @pl.when(core == 1)
        def _():
            pl.semaphore_wait(gate.at[1], 1)

        loop(own, 0, 2)

        @pl.when(core == 1)
        def _():
            loop(send)

        loop(own, 2)
        pl.semaphore_wait(gate.at[0], 1)
        loop(work)
        settle(k_ref, tx.at[0])
        settle(v_ref, tx.at[1])

    @pl.when(seq == 1)
    def _():
        for copy in near_copies():
            copy.start()
        tell(0, {"seq": 2})
        weights()

        def first(h):
            own(h)
            s_own[h] = own_state(h)

        loop(first)

        def pre(h):
            for slot in range(2):
                query_copy(h, slot, 1, 0).wait_recv()
                bottom, output = part(
                    qbuf[slot, :, cols(h)], ((k_ref[:, cols(h)], v_ref[:, cols(h)]),)
                )
                pstat[slot, 0:1, :] = bottom
                pacc[slot] = output

        def rest(h, early):
            query = q_ref[:, cols(h)]
            windowed = blend(current(h), part(query, ((kbuf[:, cols(h)], vbuf[:, cols(h)]),)))[1]
            finish(h, windowed, lin[h] + dot_nt(early, query))

        def early_state(h):
            return dot_tn(vbuf[:, cols(h)], kbuf[:, cols(h)])

        for arrived, onward in zip(kv_copies(0), far_copies()):
            arrived.wait_recv()
            onward.start()
        pl.semaphore_wait(gate.at[0], 1)
        tell(0, {"seq": 0})
        rest(0, early_state(0).astype(BF16))
        pre(1)

        def work(h, final=False):
            arrived = kv_copies(h)
            arrived[0].wait_recv()
            for slot in range(2):
                scores = dot_nt(kbuf[:, cols(h)], qbuf[slot, :, cols(h)])
                top = jnp.max(scores, axis=0, keepdims=True)
                expo = jnp.exp2((scores - top) * RATE)
                total = jnp.sum(expo, axis=0, keepdims=True)
                pstat[slot, 1:2, :] = level(top, total)
                pstat[slot, 2:3, :] = recip(total)
                ebuf[slot] = expo.astype(BF16)
            arrived[1].wait_recv()
            early = early_state(h)
            s_send[h] = (early + s_own[h]).astype(BF16)
            state_copy(h, 2).start()
            for slot in (1, 0):
                fresh = dot_tn(vbuf[:, cols(h)], ebuf[slot]) * pstat[slot, 2:3, :]
                bottom, output = blend(
                    (pstat[slot, 0:1, :], pacc[slot]), (pstat[slot, 1:2, :], fresh)
                )
                l_send[slot, h] = bottom
                o_send[slot, h] = output.astype(BF16)
                straight = final and slot
                (level_onward(h) if straight else level_copy(h, slot)).start()
                for index in order[:-2] if final else order:
                    (chunk_onward(h, index) if straight else chunk_copy(h, slot, index)).start()
            if final:
                for index in order[-2:]:
                    chunk_onward(h, index).start()
                    chunk_copy(h, 0, index).start()
            else:
                pre(h + 1)
            rest(h, early.astype(BF16))
            project(h - 1)

        loop(work, 1, heads - 1)
        work(heads - 1, True)
        for copy in near_copies() + far_copies():
            copy.wait_send()
        settle(s_send.at[later], tx.at[4])
        settle(l_send.at[:, later], tx.at[5])
        settle(o_send.at[:, later], tx.at[6])

    @pl.when(seq == 2)
    def _():
        for h in range(1, min(3, heads)):
            query_copy(h, 0, 1, 0).start()
        weights()

        def first(h):
            own(h)
            s_own[h] = own_state(h)

        loop(first, 0, 2)
        pl.semaphore_wait(gate.at[0], 1)
        for index in range(1, peers):
            tell(1, {"head": peer_of(index)})
        loop(first, 2)
        pl.semaphore_wait(gate.at[1], peers - 1)
        tell(0, {"seq": 1})

        def pair(h):
            return k_ref[:, cols(h)], v_ref[:, cols(h)]

        def third(h):
            query_copy(h, 1, 2, 0).wait_recv()
            if h > 1:
                relay_copy(h).start()
                if h + 1 < heads:
                    query_copy(h + 1, 0, 1, 0).start()
            if h:
                bottom, output = part(qbuf[1, :, cols(h)], (pair(h),))
                if h < heads - 1:
                    pstat[h, 0:1, :] = bottom
                    pacc[h] = output
                else:
                    l_send[0, h] = bottom
                    o_send[0, h] = output.astype(BF16)
                    for copy in part_copies():
                        copy.start()

        for h in [*range(2, heads), 0]:
            third(h)
        for copy in near_copies() + far_copies():
            copy.wait_recv()
        pairs = [(kbuf[:, cols(i)], vbuf[:, cols(i)]) for i in range(2)]
        early = sum(dot_tn(value, key) for key, value in pairs)
        s_send[0] = (early + s_own[0]).astype(BF16)
        state_copy(0, 3).start()
        bottom, output = part(qbuf[1, :, cols(0)], pairs + [pair(0)])
        l_send[1, 0] = bottom
        o_send[1, 0] = output.astype(BF16)
        level_onward(0).start()
        for index in order:
            chunk_onward(0, index).start()
        query = q_ref[:, cols(0)]
        windowed = blend(current(0), part(query, pairs))[1]
        finish(0, windowed, lin[0] + dot_nt(early.astype(BF16), query))
        if heads > 2:
            third(1)

        def state(h):
            state_copy(h, 2).wait_recv()
            s_send[h] = (s_recv[h].astype(F32) + s_own[h]).astype(BF16)
            state_copy(h, 3).start()

        def close(h):
            lin[h] = norm(lin[h] + dot_nt(s_recv[h], q_ref[:, cols(h)]))
            final = isinstance(h, int)
            arrive(
                h, 0, lambda h: level_copy(h, 0), lambda h, index: chunk_copy(h, 0, index), final
            )
            if not final:
                project(h - 1)

        def second(h):
            state(h)
            level_copy(h, 1).wait_recv()
            mine, theirs = pstat[h, 0:1, :], l_recv[1, h]
            top = jnp.maximum(mine, theirs)
            left, right = jnp.exp2(mine - top), jnp.exp2(theirs - top)
            total = left + right
            l_send[1, h] = top + jnp.log2(total)
            pstat[h, 1:2, :] = left * recip(total)
            pstat[h, 2:3, :] = right * recip(total)
            level_onward(h).start()
            for index in order:
                chunk_copy(h, 1, index).wait_recv()
                place = lanes(peer_of(index), share)
                output = pstat[h, 1:2, place] * pacc[h, :, place]
                output += pstat[h, 2:3, place] * o_recv[1, h, :, place].astype(F32)
                o_send[1, h, :, place] = output.astype(BF16)
                chunk_onward(h, index).start()
            close(h)

        loop(second, 1, heads - 1)
        state(heads - 1)
        close(heads - 1)
        for copy in part_copies():
            copy.wait_send()
        settle(q_ref.at[:, pl.ds(HD, width - HD)], tx.at[0])
        if heads > 2:
            settle(q_ref.at[:, pl.ds(2 * HD, width - 2 * HD)], tx.at[1])
        settle(s_send, tx.at[4])
        settle(l_send.at[1, pl.ds(0, heads - 1)], tx.at[5])
        settle(o_send.at[1, pl.ds(0, heads - 1)], tx.at[6])

    @pl.when(seq == 3)
    def _():
        query_copy(1, 1, 1, 0).start()
        for h in [*range(2, heads), 0, 1]:
            query_copy(h, 1, 2, 1).start()
        weights()
        loop(own)

        def work(h):
            state_copy(h, 3).wait_recv()
            lin[h] = norm(lin[h] + dot_nt(s_recv[h], q_ref[:, cols(h)]))
            final = isinstance(h, int)
            arrive(h, 1, level_onward, chunk_onward, final)
            if not final:
                project_before(h)

        loop(work, 0, heads - 1)
        for copy in part_copies():
            copy.wait_recv()
        last = heads - 1
        bottom, output = blend(current(last), (l_recv[0, last], o_recv[0, last].astype(F32)))
        stat[last, 0:1, :] = bottom
        acc[last] = output
        work(last)
        query_copy(1, 1, 1, 0).wait_send()
        settle(q_ref, tx.at[1])

    project(heads - 1, out_ref)
    settle(mixed.at[:, pl.ds(0, length - share)], tx.at[8])


def fused(queries, keys, values, w_out):
    peers = lax.axis_size("head")
    length, width = queries.shape
    heads = width // HD
    share = length // peers
    dma = pltpu.SemaphoreType.DMA
    vmem = pl.BlockSpec(memory_space=pltpu.VMEM)
    return pl.pallas_call(
        functools.partial(kernel, peers),
        out_shape=pltpu.VMEM((share, w_out.shape[1]), BF16),
        in_specs=[pl.BlockSpec(memory_space=pltpu.HBM)] * 4,
        out_specs=vmem,
        scratch_shapes=[
            pltpu.VMEM((length, width), BF16),
            pltpu.VMEM((length, width), BF16),
            pltpu.VMEM((length, width), BF16),
            pltpu.VMEM((heads, peers * HD, w_out.shape[1]), BF16),
            pltpu.VMEM((share, w_out.shape[1]), F32),
            pltpu.VMEM((length, width), BF16),
            pltpu.VMEM((length, width), BF16),
            pltpu.VMEM((2, length, width), BF16),
            pltpu.VMEM((2, length, length), BF16),
            pltpu.VMEM((heads, HD, length), F32),
            pltpu.VMEM((heads, 8, length), F32),
            pltpu.VMEM((2, heads, HD, length), BF16),
            pltpu.VMEM((2, heads, HD, length), BF16),
            pltpu.VMEM((2, heads, 1, length), F32),
            pltpu.VMEM((2, heads, 1, length), F32),
            pltpu.VMEM((heads, HD, HD), F32),
            pltpu.VMEM((heads, HD, HD), BF16),
            pltpu.VMEM((heads, HD, HD), BF16),
            pltpu.VMEM((heads, HD, length), F32),
            pltpu.VMEM((heads, HD, length), F32),
            pltpu.VMEM((heads, 8, length), F32),
            pltpu.VMEM((width, length), BF16),
            pltpu.VMEM((heads, peers * HD, share), BF16),
            dma((3,)), dma((heads,)), dma((9,)), dma((2, heads)), dma((2, heads)),
            dma((2 * (heads - 1), peers)), dma((2 * (heads - 1),)), dma((heads,)), dma((heads,)),
            pltpu.SemaphoreType.REGULAR((2,)),
        ],
        compiler_params=pltpu.CompilerParams(
            collective_id=0, has_side_effects=True, vmem_limit_bytes=56 * 1024 * 1024
        ),
    )(queries, keys, values, w_out)


def shifted(value, axis, steps):
    count = lax.axis_size(axis)
    first, last = (max(0, -steps), min(count, count - steps))
    return lax.ppermute(value, axis, [(source, source + steps) for source in range(first, last)])


def fits(queries):
    length, width = queries.shape
    blocks = lax.axis_size("seq")
    share = length // lax.axis_size("head")
    whole = share % HD == 0 and width % HD == 0 and width > HD and lax.axis_size("head") % 2 == 0
    return blocks == 4 and blocks * length <= WINDOW and whole


def per_device(queries, keys, values, w_out):
    if fits(queries):
        return fused(queries, keys, values, w_out)
    length_dev, width = queries.shape
    heads_dev = width // HD
    block_rows = min(512, length_dev)
    block_count = length_dev // block_rows
    highest = lax.Precision.HIGHEST
    seq_index = lax.axis_index("seq")
    q_blocks = queries.reshape(block_count, block_rows, heads_dev, HD)
    k_blocks = keys.reshape(block_count, block_rows, heads_dev, HD)
    v_blocks = values.reshape(block_count, block_rows, heads_dev, HD)
    block_states = jnp.einsum(
        "bkhd,bkhe->bhde", k_blocks, v_blocks, preferred_element_type=jnp.float32
    )
    own_state = jnp.sum(block_states, axis=0)
    earlier = jnp.cumsum(block_states, axis=0) - block_states
    piece = lax.all_gather(own_state[None], "seq", axis=0, tiled=True)
    order = jnp.arange(piece.shape[0], dtype=jnp.int32)
    keep = order < seq_index
    prefix = jnp.sum(jnp.where(keep[:, None, None, None], piece, 0.0), axis=0)
    causal = jnp.arange(block_rows)[:, None] >= jnp.arange(block_rows)[None, :]
    local_scores = jnp.einsum(
        "bqhd,bkhd->bhqk", q_blocks, k_blocks, preferred_element_type=jnp.float32
    )
    local_scores = jnp.where(causal, local_scores, 0.0)
    intra = jnp.einsum(
        "bhqk,bkhe->bqhe", local_scores, v_blocks.astype(jnp.float32), precision=highest
    )
    state_before = prefix[None] + earlier
    inter = jnp.einsum(
        "bqhd,bhde->bqhe", q_blocks.astype(jnp.float32), state_before, precision=highest
    )
    linear = (intra + inter).reshape(length_dev, heads_dev, HD)
    normed = linear / jnp.sqrt(jnp.mean(linear * linear, axis=-1, keepdims=True) + 1e-06)
    reach = min(WINDOW // length_dev, lax.axis_size("seq") - 1)
    received = [shifted((keys, values), "seq", distance) for distance in range(1, reach + 1)]
    pad_rows = WINDOW - reach * length_dev
    filler = jnp.zeros((pad_rows, width), keys.dtype)
    wide_keys = jnp.concatenate([filler] + [pair[0] for pair in reversed(received)] + [keys], 0)
    wide_values = jnp.concatenate([filler] + [pair[1] for pair in reversed(received)] + [values], 0)
    wide_keys = wide_keys.reshape(-1, heads_dev, HD)
    wide_values = wide_values.reshape(-1, heads_dev, HD)
    scale = 1.0 / math.sqrt(HD)
    span = WINDOW + block_rows
    query_pos = jnp.arange(block_rows, dtype=jnp.int32)[:, None]
    key_pos = jnp.arange(span, dtype=jnp.int32)[None, :]
    band = (key_pos > query_pos) & (key_pos <= query_pos + WINDOW)
    rows_q = queries.reshape(block_rows, heads_dev, HD)
    anchor = seq_index * length_dev + 0 - WINDOW
    valid = band & (anchor + key_pos >= 0)
    scores = (
        jnp.einsum("qhd,khd->hqk", rows_q, wide_keys, preferred_element_type=jnp.float32) * scale
    )
    scores = jnp.where(valid[None], scores, -1e30)
    top = jnp.max(scores, axis=-1, keepdims=True)
    expo = jnp.where(valid[None], jnp.exp(scores - top), 0.0)
    total = jnp.sum(expo, axis=-1)
    weights = expo.astype(jnp.bfloat16)
    summed = jnp.einsum("hqk,khe->qhe", weights, wide_values, preferred_element_type=jnp.float32)
    pieces = summed / jnp.transpose(total)[:, :, None]
    mixed = (normed + pieces).astype(jnp.bfloat16).reshape(length_dev, width)
    head_count = lax.axis_size("head")
    share = length_dev // head_count
    grouped = mixed.reshape(head_count, share, width)
    return jnp.dot(
        lax.all_to_all(grouped, "head", split_axis=0, concat_axis=2, tiled=True)[0],
        w_out,
        preferred_element_type=jnp.float32,
    ).astype(jnp.bfloat16)


def solution(mesh):
    return jax.shard_map(
        per_device,
        mesh=mesh,
        in_specs=(
            P(("groups", "seq"), "head"),
            P(("groups", "seq"), "head"),
            P(("groups", "seq"), "head"),
            P(),
        ),
        out_specs=P(("groups", "seq", "head"), None),
        check_vma=False,
    )
```

```python
import functools
import math

import jax
import jax.numpy as jnp
from jax import lax
from jax.experimental import pallas as pl
from jax.experimental.pallas import tpu as pltpu
from jax.sharding import PartitionSpec as P

HD = 128
WINDOW = 2048
MESH = pl.DeviceIdType.MESH
F32 = jnp.float32
BF16 = jnp.bfloat16
RATE = math.log2(math.e) / math.sqrt(HD)
FLOOR = -1e30


def dot_nt(a, b):
    return lax.dot_general(a, b, (((1,), (1,)), ((), ())), preferred_element_type=F32)


def dot_tn(a, b):
    return lax.dot_general(a, b, (((0,), (0,)), ((), ())), preferred_element_type=F32)


def recip(x):
    return 1.0 / x


def lanes(index, size):
    return pl.ds(pl.multiple_of(index * size, size), size)


def kernel(
    peers, q_hbm, k_hbm, v_hbm, w_hbm, out_ref, q_ref, k_ref, v_ref,
    w_ref, summed, kbuf, vbuf, qbuf, ebuf, pacc, pstat, o_send, o_recv, l_send, l_recv,
    s_own, s_send, s_recv, acc, lin, stat, mixed, gathered,
    in_sem, w_sem, tx, kv_rx, q_rx, o_rx, l_rx, s_rx, m_rx, gate,
):
    seq = lax.axis_index("seq")
    here = lax.axis_index("head")
    length, width = q_ref.shape
    heads = width // HD
    share = length // peers
    chip, core = here // 2, here % 2
    chips = peers // 2
    order = list(range(2, peers)) + [1, 0]

    def peer_of(index, sign=1):
        hop, flip = index // 2, index % 2
        other = lax.rem(chip + sign * hop + chips, chips)
        return other * 2 + (1 - core if flip else core)

    barrier = pltpu.get_barrier_semaphore()

    def greet(device):
        pl.semaphore_signal(barrier, inc=1, device_id=device, device_id_type=MESH)

    circle = {0: (1,), 1: (0, 2, 3), 2: (1, 3), 3: (2,)}
    near = {0: (1,), 1: (), 2: range(1, peers), 3: range(1, peers)}
    for place, friends in circle.items():
        @pl.when(seq == place)
        def _():
            for friend in friends:
                greet({"seq": friend})

            for index in near[place]:
                greet({"head": peer_of(index)})

    loads = [
        pltpu.make_async_copy(source, target, in_sem.at[i])
        for i, (source, target) in enumerate(((q_hbm, q_ref), (k_hbm, k_ref), (v_hbm, v_ref)))
    ]
    for load in loads:
        load.start()

    def load_w(h, peer):
        return pltpu.make_async_copy(
            w_hbm.at[pl.ds(pl.multiple_of(peer * width + h * HD, HD), HD), :],
            w_ref.at[h, pl.ds(peer * HD, HD), :],
            w_sem.at[h],
        )

    def load_head(h):
        for peer in range(peers):
            load_w(h, peer).start()

    for place in circle:
        @pl.when(seq == place)
        def _():
            count = sum(place in friends for friends in circle.values())
            pl.semaphore_wait(barrier, count + len(near[place]))
    for load in loads:
        load.wait()

    def cols(h):
        return lanes(h, HD)

    def remote(source, target, sent, landed, device):
        return pltpu.make_async_remote_copy(
            src_ref=source, dst_ref=target, send_sem=tx.at[sent], recv_sem=landed,
            device_id=device, device_id_type=MESH,
        )

    def settle(ref, semaphore):
        pltpu.make_async_copy(ref, ref, semaphore).wait()

    def kv_copies(h):
        return [
            remote(
                source.at[:, cols(h)], buffer.at[:, cols(h)], i, kv_rx.at[i, h], {"seq": 1}
            )
            for i, (source, buffer) in enumerate(((k_ref, kbuf), (v_ref, vbuf)))
        ]

    def near_copies():
        return [
            remote(
                source.at[:, cols(0)], buffer.at[:, cols(1)], i, kv_rx.at[i, 1], {"seq": 2}
            )
            for i, (source, buffer) in enumerate(((k_ref, kbuf), (v_ref, vbuf)))
        ]

    def far_copies():
        return [
            remote(
                buffer.at[:, cols(0)], buffer.at[:, cols(0)], 2 + i, kv_rx.at[i, 0], {"seq": 2}
            )
            for i, buffer in enumerate((kbuf, vbuf))
        ]

    def query_copy(h, slot, target, sent):
        return remote(
            q_ref.at[:, cols(h)], qbuf.at[slot, :, cols(h)], sent, q_rx.at[slot, h], {"seq": target}
        )

    def relay_copy(h):
        return remote(
            qbuf.at[1, :, cols(h)], qbuf.at[1, :, cols(h)], 1, q_rx.at[1, h], {"seq": 1}
        )

    def row(h, slot):
        return slot * (heads - 1) + h - 1

    def level_copy(h, slot):
        return remote(
            l_send.at[slot, h], l_recv.at[slot, h], 5, l_rx.at[row(h, slot)], {"seq": 2}
        )

    def chunk_copy(h, slot, index):
        place = lanes(peer_of(index), share)
        return remote(
            o_send.at[slot, h, :, place], o_recv.at[slot, h, :, place], 6,
            o_rx.at[row(h, slot), index], {"seq": 2},
        )

    def level_onward(h):
        return remote(l_send.at[1, h], l_recv.at[1, h], 5, l_rx.at[h], {"seq": 3})

    def chunk_onward(h, index):
        place = lanes(peer_of(index), share)
        return remote(
            o_send.at[1, h, :, place], o_recv.at[1, h, :, place], 6, o_rx.at[h, index], {"seq": 3}
        )

    def part_copies():
        h = heads - 1
        return (
            remote(l_send.at[0, h], l_recv.at[0, h], 2, q_rx.at[0, 0], {"seq": 3}),
            remote(o_send.at[0, h], o_recv.at[0, h], 3, q_rx.at[1, 0], {"seq": 3}),
        )

    def state_copy(h, target):
        return remote(s_send.at[h], s_recv.at[h], 4, s_rx.at[h], {"seq": target})

    def mixed_copy(h, index):
        target = peer_of(index)
        return remote(
            mixed.at[cols(h), lanes(target, share)], gathered.at[h, lanes(here, HD), :],
            8, m_rx.at[h], {"head": target},
        )

    def loop(body, first=0, last=heads):
        lax.fori_loop(first, last, lambda h, c: (body(h), c)[1], 0)

    causal = lax.broadcasted_iota(jnp.int32, (length, length), 0) <= lax.broadcasted_iota(
        jnp.int32, (length, length), 1
    )

    def level(top, total):
        return top * RATE + jnp.log2(total)

    def own(h):
        query, key, value = q_ref[:, cols(h)], k_ref[:, cols(h)], v_ref[:, cols(h)]
        scores = dot_nt(key, query)
        kept = jnp.where(causal, scores, 0.0)
        coarse = kept.astype(BF16)
        fine = (kept - coarse.astype(F32)).astype(BF16)
        lin[h] = dot_tn(value, coarse) + dot_tn(value, fine)
        scores = jnp.where(causal, scores, FLOOR)
        top = jnp.max(scores, axis=0, keepdims=True)
        expo = jnp.exp2((scores - top) * RATE)
        total = jnp.sum(expo, axis=0, keepdims=True)
        stat[h, 0:1, :] = level(top, total)
        acc[h] = dot_tn(value, expo.astype(BF16)) * recip(total)

    def part(query, pairs):
        scores = [dot_nt(key, query) for key, _ in pairs]
        top = functools.reduce(jnp.maximum, [jnp.max(s, axis=0, keepdims=True) for s in scores])
        expo = [jnp.exp2((s - top) * RATE) for s in scores]
        total = sum(jnp.sum(e, axis=0, keepdims=True) for e in expo)
        output = sum(dot_tn(value, e.astype(BF16)) for e, (_, value) in zip(expo, pairs))
        return level(top, total), output * recip(total)

    def blend(a, b):
        top = jnp.maximum(a[0], b[0])
        left, right = jnp.exp2(a[0] - top), jnp.exp2(b[0] - top)
        total = left + right
        scale = recip(total)
        return top + jnp.log2(total), (left * scale) * a[1] + (right * scale) * b[1]

    def current(h):
        return stat[h, 0:1, :], acc[h]

    def norm(linear):
        square = jnp.mean(linear * linear, axis=0, keepdims=True)
        return linear * recip(jnp.sqrt(square + 1e-06))

    def finish(h, windowed, linear):
        mixed[cols(h), :] = (norm(linear) + windowed).astype(BF16)
        for index in order[:-1]:
            mixed_copy(h, index).start()
        gathered[h, lanes(here, HD), :] = mixed[cols(h), lanes(here, share)]

    def arrive(h, slot, level_of, chunk_of):
        level_of(h).wait_recv()
        for index in order:
            chunk_of(h, index).wait_recv()
            place = lanes(peer_of(index), share)
            mine = stat[h, 0:1, place], acc[h, :, place]
            theirs = l_recv[slot, h, 0:1, place], o_recv[slot, h, :, place].astype(F32)
            piece = (lin[h, :, place] + blend(mine, theirs)[1]).astype(BF16)
            if index:
                mixed[cols(h), place] = piece
                mixed_copy(h, index).start()
            else:
                gathered[h, lanes(here, HD), :] = piece

    tile = math.gcd(w_ref.shape[2], 512)

    def project(h, target=None):
        settle(w_ref.at[h], w_sem.at[h])
        settle(gathered.at[h, pl.ds(0, (peers - 1) * HD)], m_rx.at[h])
        left = gathered[h].T
        target = summed if target is None else target
        for begin in range(0, w_ref.shape[2], tile):
            piece = slice(begin, begin + tile)
            product = jnp.dot(left, w_ref[h, :, piece], preferred_element_type=F32)
            target[:, piece] = (summed[:, piece] + product).astype(target.dtype)

    def project_before(h):
        pl.when(h > 0)(lambda: project(h - 1))

    def weights():
        lax.fori_loop(0, heads, lambda h, c: (load_head(h), c)[1], 0)
        summed[...] = jnp.zeros_like(summed)

    def tell(slot, device):
        pl.semaphore_signal(gate.at[slot], inc=1, device_id=device, device_id_type=MESH)

    def own_state(h):
        return dot_tn(v_ref[:, cols(h)], k_ref[:, cols(h)])

    last = heads - 1
    later = pl.ds(1, last)

    @pl.when(seq == 0)
    def _():
        def send(h):
            for copy in kv_copies(h):
                copy.start()

        def work(h):
            finish(h, acc[h], lin[h])
            project_before(h)

        @pl.when(core == 1)
        def _():
            loop(send, 0, 2)
            tell(1, {"head": peer_of(1)})

        @pl.when(core == 0)
        def _():
            pl.semaphore_wait(gate.at[1], 1)

        own(0)

        @pl.when(core == 0)
        def _():
            loop(send, 0, 2)

        s_send[last] = own_state(last).astype(BF16)
        state_copy(last, 1).start()
        loop(send, 2)
        weights()
        loop(own, 1)
        pl.semaphore_wait(gate.at[0], 1)
        loop(work)
        settle(k_ref, tx.at[0])
        settle(v_ref, tx.at[1])
        state_copy(last, 1).wait_send()

    @pl.when(seq == 1)
    def _():
        for copy in near_copies():
            copy.start()
        tell(0, {"seq": 2})
        weights()

        def first(h):
            own(h)
            s_own[h] = own_state(h)

        loop(first)

        def pre(h):
            for slot in range(2):
                query_copy(h, slot, 1, 0).wait_recv()
                bottom, output = part(
                    qbuf[slot, :, cols(h)], ((k_ref[:, cols(h)], v_ref[:, cols(h)]),)
                )
                pstat[slot, 0:1, :] = bottom
                pacc[slot] = output

        def rest(h, early):
            query = q_ref[:, cols(h)]
            windowed = blend(current(h), part(query, ((kbuf[:, cols(h)], vbuf[:, cols(h)]),)))[1]
            finish(h, windowed, lin[h] + dot_nt(early, query))

        def early_state(h):
            return dot_tn(vbuf[:, cols(h)], kbuf[:, cols(h)])

        for arrived, onward in zip(kv_copies(0), far_copies()):
            arrived.wait_recv()
            onward.start()
        pl.semaphore_wait(gate.at[0], 1)
        tell(0, {"seq": 0})
        rest(0, early_state(0).astype(BF16))
        pre(1)

        def early_last():
            state_copy(last, 1).wait_recv()
            s_send[last] = (s_recv[last].astype(F32) + s_own[last]).astype(BF16)
            state_copy(last, 2).start()

        def work(h, final=False):
            arrived = kv_copies(h)
            arrived[0].wait_recv()
            for slot in range(2):
                scores = dot_nt(kbuf[:, cols(h)], qbuf[slot, :, cols(h)])
                top = jnp.max(scores, axis=0, keepdims=True)
                expo = jnp.exp2((scores - top) * RATE)
                total = jnp.sum(expo, axis=0, keepdims=True)
                pstat[slot, 1:2, :] = level(top, total)
                pstat[slot, 2:3, :] = recip(total)
                ebuf[slot] = expo.astype(BF16)
            arrived[1].wait_recv()
            if final:
                early = s_recv[h]
            else:
                early = early_state(h)
                s_send[h] = (early + s_own[h]).astype(BF16)
                state_copy(h, 2).start()
                early = early.astype(BF16)
            for slot in (1, 0):
                fresh = dot_tn(vbuf[:, cols(h)], ebuf[slot]) * pstat[slot, 2:3, :]
                bottom, output = blend(
                    (pstat[slot, 0:1, :], pacc[slot]), (pstat[slot, 1:2, :], fresh)
                )
                l_send[slot, h] = bottom
                o_send[slot, h] = output.astype(BF16)
                straight = final and slot
                (level_onward(h) if straight else level_copy(h, slot)).start()
                for index in order[:-2] if final else order:
                    (chunk_onward(h, index) if straight else chunk_copy(h, slot, index)).start()
            if final:
                for index in order[-2:]:
                    chunk_onward(h, index).start()
                    chunk_copy(h, 0, index).start()
            else:
                @pl.when(h == 1)
                def _():
                    early_last()

                pre(h + 1)

            rest(h, early)
            project(h - 1)

        if last == 1:
            early_last()
        loop(work, 1, last)
        work(last, True)
        for copy in near_copies() + far_copies():
            copy.wait_send()
        settle(s_send.at[later], tx.at[4])
        settle(l_send.at[:, later], tx.at[5])
        settle(o_send.at[:, later], tx.at[6])

    @pl.when(seq == 2)
    def _():
        for h in range(1, min(3, heads)):
            query_copy(h, 0, 1, 0).start()
        weights()

        def first(h):
            own(h)
            s_own[h] = own_state(h)

        loop(first, 0, 2)
        pl.semaphore_wait(gate.at[0], 1)
        for index in range(1, peers):
            tell(1, {"head": peer_of(index)})
        loop(first, 2)
        pl.semaphore_wait(gate.at[1], peers - 1)
        tell(0, {"seq": 1})

        def pair(h):
            return k_ref[:, cols(h)], v_ref[:, cols(h)]

        def third(h):
            query_copy(h, 1, 2, 0).wait_recv()
            if h > 1:
                relay_copy(h).start()
                if h + 1 < heads:
                    query_copy(h + 1, 0, 1, 0).start()
            if h:
                bottom, output = part(qbuf[1, :, cols(h)], (pair(h),))
                if h < heads - 1:
                    pstat[h, 0:1, :] = bottom
                    pacc[h] = output
                else:
                    l_send[0, h] = bottom
                    o_send[0, h] = output.astype(BF16)
                    for copy in part_copies():
                        copy.start()

        for h in [*range(2, heads), 0]:
            third(h)
        for copy in near_copies() + far_copies():
            copy.wait_recv()
        pairs = [(kbuf[:, cols(i)], vbuf[:, cols(i)]) for i in range(2)]
        early = sum(dot_tn(value, key) for key, value in pairs)
        s_send[0] = (early + s_own[0]).astype(BF16)
        state_copy(0, 3).start()
        bottom, output = part(qbuf[1, :, cols(0)], pairs + [pair(0)])
        l_send[1, 0] = bottom
        o_send[1, 0] = output.astype(BF16)
        level_onward(0).start()
        for index in order:
            chunk_onward(0, index).start()
        query = q_ref[:, cols(0)]
        windowed = blend(current(0), part(query, pairs))[1]
        finish(0, windowed, lin[0] + dot_nt(early.astype(BF16), query))
        if heads > 2:
            third(1)

        def state(h):
            state_copy(h, 2).wait_recv()
            s_send[h] = (s_recv[h].astype(F32) + s_own[h]).astype(BF16)
            state_copy(h, 3).start()

            lin[h] = norm(lin[h] + dot_nt(s_recv[h], q_ref[:, cols(h)]))

        def close(h):
            arrive(h, 0, lambda h: level_copy(h, 0), lambda h, index: chunk_copy(h, 0, index))
            project(h - 1)

        def second(h):
            state(h)
            level_copy(h, 1).wait_recv()
            mine, theirs = pstat[h, 0:1, :], l_recv[1, h]
            top = jnp.maximum(mine, theirs)
            left, right = jnp.exp2(mine - top), jnp.exp2(theirs - top)
            total = left + right
            l_send[1, h] = top + jnp.log2(total)
            pstat[h, 1:2, :] = left * recip(total)
            pstat[h, 2:3, :] = right * recip(total)
            level_onward(h).start()
            for index in order:
                chunk_copy(h, 1, index).wait_recv()
                place = lanes(peer_of(index), share)
                output = pstat[h, 1:2, place] * pacc[h, :, place]
                output += pstat[h, 2:3, place] * o_recv[1, h, :, place].astype(F32)
                o_send[1, h, :, place] = output.astype(BF16)
                chunk_onward(h, index).start()

            @pl.when(h == 1)
            def _():
                state(last)

            close(h)

        loop(second, 1, last)
        close(last)
        for copy in part_copies():
            copy.wait_send()
        settle(q_ref.at[:, pl.ds(HD, width - HD)], tx.at[0])
        if heads > 2:
            settle(q_ref.at[:, pl.ds(2 * HD, width - 2 * HD)], tx.at[1])
        settle(s_send, tx.at[4])
        settle(l_send.at[1, pl.ds(0, heads - 1)], tx.at[5])
        settle(o_send.at[1, pl.ds(0, heads - 1)], tx.at[6])

    @pl.when(seq == 3)
    def _():
        query_copy(1, 1, 1, 0).start()
        for h in [*range(2, heads), 0, 1]:
            query_copy(h, 1, 2, 1).start()
        weights()
        loop(own)

        def state(h):
            state_copy(h, 3).wait_recv()
            lin[h] = norm(lin[h] + dot_nt(s_recv[h], q_ref[:, cols(h)]))

        def work(h):
            state(h)
            arrive(h, 1, level_onward, chunk_onward)
            project_before(h)

        loop(work, 0, last)
        state(last)
        for copy in part_copies():
            copy.wait_recv()
        bottom, output = blend(current(last), (l_recv[0, last], o_recv[0, last].astype(F32)))
        stat[last, 0:1, :] = bottom
        acc[last] = output
        arrive(last, 1, level_onward, chunk_onward)
        project(last - 1)
        query_copy(1, 1, 1, 0).wait_send()
        settle(q_ref, tx.at[1])

    project(heads - 1, out_ref)
    settle(mixed.at[:, pl.ds(0, length - share)], tx.at[8])


def fused(queries, keys, values, w_out):
    peers = lax.axis_size("head")
    length, width = queries.shape
    heads = width // HD
    share = length // peers
    dma = pltpu.SemaphoreType.DMA
    vmem = pl.BlockSpec(memory_space=pltpu.VMEM)
    return pl.pallas_call(
        functools.partial(kernel, peers),
        out_shape=pltpu.VMEM((share, w_out.shape[1]), BF16),
        in_specs=[pl.BlockSpec(memory_space=pltpu.HBM)] * 4,
        out_specs=vmem,
        scratch_shapes=[
            pltpu.VMEM((length, width), BF16),
            pltpu.VMEM((length, width), BF16),
            pltpu.VMEM((length, width), BF16),
            pltpu.VMEM((heads, peers * HD, w_out.shape[1]), BF16),
            pltpu.VMEM((share, w_out.shape[1]), F32),
            pltpu.VMEM((length, width), BF16),
            pltpu.VMEM((length, width), BF16),
            pltpu.VMEM((2, length, width), BF16),
            pltpu.VMEM((2, length, length), BF16),
            pltpu.VMEM((heads, HD, length), F32),
            pltpu.VMEM((heads, 8, length), F32),
            pltpu.VMEM((2, heads, HD, length), BF16),
            pltpu.VMEM((2, heads, HD, length), BF16),
            pltpu.VMEM((2, heads, 1, length), F32),
            pltpu.VMEM((2, heads, 1, length), F32),
            pltpu.VMEM((heads, HD, HD), F32),
            pltpu.VMEM((heads, HD, HD), BF16),
            pltpu.VMEM((heads, HD, HD), BF16),
            pltpu.VMEM((heads, HD, length), F32),
            pltpu.VMEM((heads, HD, length), F32),
            pltpu.VMEM((heads, 8, length), F32),
            pltpu.VMEM((width, length), BF16),
            pltpu.VMEM((heads, peers * HD, share), BF16),
            dma((3,)), dma((heads,)), dma((9,)), dma((2, heads)), dma((2, heads)),
            dma((2 * (heads - 1), peers)), dma((2 * (heads - 1),)), dma((heads,)), dma((heads,)),
            pltpu.SemaphoreType.REGULAR((2,)),
        ],
        compiler_params=pltpu.CompilerParams(
            collective_id=0, has_side_effects=True, vmem_limit_bytes=56 * 1024 * 1024
        ),
    )(queries, keys, values, w_out)


def shifted(value, axis, steps):
    count = lax.axis_size(axis)
    first, last = (max(0, -steps), min(count, count - steps))
    return lax.ppermute(value, axis, [(source, source + steps) for source in range(first, last)])


def fits(queries):
    length, width = queries.shape
    blocks = lax.axis_size("seq")
    share = length // lax.axis_size("head")
    whole = share % HD == 0 and width % HD == 0 and width > HD and lax.axis_size("head") % 2 == 0
    return blocks == 4 and blocks * length <= WINDOW and whole


def per_device(queries, keys, values, w_out):
    if fits(queries):
        return fused(queries, keys, values, w_out)
    length_dev, width = queries.shape
    heads_dev = width // HD
    block_rows = min(512, length_dev)
    block_count = length_dev // block_rows
    highest = lax.Precision.HIGHEST
    seq_index = lax.axis_index("seq")
    q_blocks = queries.reshape(block_count, block_rows, heads_dev, HD)
    k_blocks = keys.reshape(block_count, block_rows, heads_dev, HD)
    v_blocks = values.reshape(block_count, block_rows, heads_dev, HD)
    block_states = jnp.einsum(
        "bkhd,bkhe->bhde", k_blocks, v_blocks, preferred_element_type=jnp.float32
    )
    own_state = jnp.sum(block_states, axis=0)
    earlier = jnp.cumsum(block_states, axis=0) - block_states
    piece = lax.all_gather(own_state[None], "seq", axis=0, tiled=True)
    order = jnp.arange(piece.shape[0], dtype=jnp.int32)
    keep = order < seq_index
    prefix = jnp.sum(jnp.where(keep[:, None, None, None], piece, 0.0), axis=0)
    causal = jnp.arange(block_rows)[:, None] >= jnp.arange(block_rows)[None, :]
    local_scores = jnp.einsum(
        "bqhd,bkhd->bhqk", q_blocks, k_blocks, preferred_element_type=jnp.float32
    )
    local_scores = jnp.where(causal, local_scores, 0.0)
    intra = jnp.einsum(
        "bhqk,bkhe->bqhe", local_scores, v_blocks.astype(jnp.float32), precision=highest
    )
    state_before = prefix[None] + earlier
    inter = jnp.einsum(
        "bqhd,bhde->bqhe", q_blocks.astype(jnp.float32), state_before, precision=highest
    )
    linear = (intra + inter).reshape(length_dev, heads_dev, HD)
    normed = linear / jnp.sqrt(jnp.mean(linear * linear, axis=-1, keepdims=True) + 1e-06)
    reach = min(WINDOW // length_dev, lax.axis_size("seq") - 1)
    received = [shifted((keys, values), "seq", distance) for distance in range(1, reach + 1)]
    pad_rows = WINDOW - reach * length_dev
    filler = jnp.zeros((pad_rows, width), keys.dtype)
    wide_keys = jnp.concatenate([filler] + [pair[0] for pair in reversed(received)] + [keys], 0)
    wide_values = jnp.concatenate([filler] + [pair[1] for pair in reversed(received)] + [values], 0)
    wide_keys = wide_keys.reshape(-1, heads_dev, HD)
    wide_values = wide_values.reshape(-1, heads_dev, HD)
    scale = 1.0 / math.sqrt(HD)
    span = WINDOW + block_rows
    query_pos = jnp.arange(block_rows, dtype=jnp.int32)[:, None]
    key_pos = jnp.arange(span, dtype=jnp.int32)[None, :]
    band = (key_pos > query_pos) & (key_pos <= query_pos + WINDOW)
    rows_q = queries.reshape(block_rows, heads_dev, HD)
    anchor = seq_index * length_dev + 0 - WINDOW
    valid = band & (anchor + key_pos >= 0)
    scores = (
        jnp.einsum("qhd,khd->hqk", rows_q, wide_keys, preferred_element_type=jnp.float32) * scale
    )
    scores = jnp.where(valid[None], scores, -1e30)
    top = jnp.max(scores, axis=-1, keepdims=True)
    expo = jnp.where(valid[None], jnp.exp(scores - top), 0.0)
    total = jnp.sum(expo, axis=-1)
    weights = expo.astype(jnp.bfloat16)
    summed = jnp.einsum("hqk,khe->qhe", weights, wide_values, preferred_element_type=jnp.float32)
    pieces = summed / jnp.transpose(total)[:, :, None]
    mixed = (normed + pieces).astype(jnp.bfloat16).reshape(length_dev, width)
    head_count = lax.axis_size("head")
    share = length_dev // head_count
    grouped = mixed.reshape(head_count, share, width)
    return jnp.dot(
        lax.all_to_all(grouped, "head", split_axis=0, concat_axis=2, tiled=True)[0],
        w_out,
        preferred_element_type=jnp.float32,
    ).astype(jnp.bfloat16)


def solution(mesh):
    return jax.shard_map(
        per_device,
        mesh=mesh,
        in_specs=(
            P(("groups", "seq"), "head"),
            P(("groups", "seq"), "head"),
            P(("groups", "seq"), "head"),
            P(),
        ),
        out_specs=P(("groups", "seq", "head"), None),
        check_vma=False,
    )
```

```python
import functools
import math

import jax
import jax.numpy as jnp
from jax import lax
from jax.experimental import pallas as pl
from jax.experimental.pallas import tpu as pltpu
from jax.sharding import PartitionSpec as P

HD = 128
WINDOW = 2048
MESH = pl.DeviceIdType.MESH
F32 = jnp.float32
BF16 = jnp.bfloat16
RATE = math.log2(math.e) / math.sqrt(HD)
FLOOR = -1e30


def dot_nt(a, b):
    return lax.dot_general(a, b, (((1,), (1,)), ((), ())), preferred_element_type=F32)


def dot_tn(a, b):
    return lax.dot_general(a, b, (((0,), (0,)), ((), ())), preferred_element_type=F32)


def recip(x):
    return 1.0 / x


def lanes(index, size):
    return pl.ds(pl.multiple_of(index * size, size), size)


def kernel(
    peers, q_hbm, k_hbm, v_hbm, w_hbm, out_ref, q_ref, k_ref, v_ref,
    w_ref, summed, kbuf, vbuf, qbuf, ebuf, pacc, pstat, o_send, o_recv, l_send, l_recv,
    s_own, s_send, s_recv, acc, lin, stat, mixed, gathered,
    in_sem, w_sem, tx, kv_rx, q_rx, o_rx, l_rx, s_rx, m_rx, gate,
):
    seq = lax.axis_index("seq")
    here = lax.axis_index("head")
    length, width = q_ref.shape
    heads = width // HD
    share = length // peers
    chip, core = here // 2, here % 2
    chips = peers // 2
    order = list(range(2, peers)) + [1, 0]
    last = heads - 1
    inner = last - 1

    def peer_of(index, sign=1):
        hop, flip = index // 2, index % 2
        other = lax.rem(chip + sign * hop + chips, chips)
        return other * 2 + (1 - core if flip else core)

    barrier = pltpu.get_barrier_semaphore()

    def greet(device):
        pl.semaphore_signal(barrier, inc=1, device_id=device, device_id_type=MESH)

    circle = {0: (1,), 1: (0, 2, 3), 2: (1, 3), 3: (2,)}
    near = {0: (1,), 1: (), 2: range(1, peers), 3: range(1, peers)}
    for place, friends in circle.items():
        @pl.when(seq == place)
        def _():
            for friend in friends:
                greet({"seq": friend})

            for index in near[place]:
                greet({"head": peer_of(index)})

    loads = [
        pltpu.make_async_copy(source, target, in_sem.at[i])
        for i, (source, target) in enumerate(((q_hbm, q_ref), (k_hbm, k_ref), (v_hbm, v_ref)))
    ]
    for load in loads:
        load.start()

    def load_w(h, peer):
        return pltpu.make_async_copy(
            w_hbm.at[pl.ds(pl.multiple_of(peer * width + h * HD, HD), HD), :],
            w_ref.at[h, pl.ds(peer * HD, HD), :],
            w_sem.at[h],
        )

    def load_head(h):
        for peer in range(peers):
            load_w(h, peer).start()

    for place in circle:
        @pl.when(seq == place)
        def _():
            count = sum(place in friends for friends in circle.values())
            pl.semaphore_wait(barrier, count + len(near[place]))
    for load in loads:
        load.wait()

    def cols(h):
        return lanes(h, HD)

    def remote(source, target, sent, landed, device):
        return pltpu.make_async_remote_copy(
            src_ref=source, dst_ref=target, send_sem=tx.at[sent], recv_sem=landed,
            device_id=device, device_id_type=MESH,
        )

    def settle(ref, semaphore):
        pltpu.make_async_copy(ref, ref, semaphore).wait()

    def kv_copies(h, first=0, target=1):
        return [
            remote(
                source.at[:, cols(h)], buffer.at[:, cols(h)], first + i, kv_rx.at[i, h],
                {"seq": target},
            )
            for i, (source, buffer) in enumerate(((k_ref, kbuf), (v_ref, vbuf)))
        ]

    def near_copies():
        return [
            remote(
                source.at[:, cols(0)], buffer.at[:, cols(1)], i, kv_rx.at[i, 1], {"seq": 2}
            )
            for i, (source, buffer) in enumerate(((k_ref, kbuf), (v_ref, vbuf)))
        ]

    def far_copies():
        return [
            remote(
                buffer.at[:, cols(0)], buffer.at[:, cols(0)], 2 + i, kv_rx.at[i, 0], {"seq": 2}
            )
            for i, buffer in enumerate((kbuf, vbuf))
        ]

    def query_copy(h, slot, target, sent):
        return remote(
            q_ref.at[:, cols(h)], qbuf.at[slot, :, cols(h)], sent, q_rx.at[slot, h], {"seq": target}
        )

    def row(h, slot):
        return slot * (heads - 1) + h - 1

    def level_copy(h, slot):
        return remote(
            l_send.at[slot, h], l_recv.at[slot, h], 5, l_rx.at[row(h, slot)], {"seq": 2}
        )

    def chunk_copy(h, slot, index):
        place = lanes(peer_of(index), share)
        return remote(
            o_send.at[slot, h, :, place], o_recv.at[slot, h, :, place], 6,
            o_rx.at[row(h, slot), index], {"seq": 2},
        )

    def level_onward(h):
        return remote(l_send.at[1, h], l_recv.at[1, h], 5, l_rx.at[h], {"seq": 3})

    def chunk_onward(h, index):
        place = lanes(peer_of(index), share)
        return remote(
            o_send.at[1, h, :, place], o_recv.at[1, h, :, place], 6, o_rx.at[h, index], {"seq": 3}
        )

    def state_copy(h, target):
        return remote(s_send.at[h], s_recv.at[h], 4, s_rx.at[h], {"seq": target})

    def mixed_copy(h, index):
        target = peer_of(index)
        return remote(
            mixed.at[cols(h), lanes(target, share)], gathered.at[h, lanes(here, HD), :],
            8, m_rx.at[h + h // last if index == 1 else h], {"head": target},
        )

    def loop(body, first=0, last=heads):
        lax.fori_loop(first, last, lambda h, c: (body(h), c)[1], 0)

    causal = lax.broadcasted_iota(jnp.int32, (length, length), 0) <= lax.broadcasted_iota(
        jnp.int32, (length, length), 1
    )

    def level(top, total):
        return top * RATE + jnp.log2(total)

    def own(h):
        query, key, value = q_ref[:, cols(h)], k_ref[:, cols(h)], v_ref[:, cols(h)]
        scores = dot_nt(key, query)
        kept = jnp.where(causal, scores, 0.0)
        coarse = kept.astype(BF16)
        fine = (kept - coarse.astype(F32)).astype(BF16)
        lin[h] = dot_tn(value, coarse) + dot_tn(value, fine)
        scores = jnp.where(causal, scores, FLOOR)
        top = jnp.max(scores, axis=0, keepdims=True)
        expo = jnp.exp2((scores - top) * RATE)
        total = jnp.sum(expo, axis=0, keepdims=True)
        stat[h, 0:1, :] = level(top, total)
        acc[h] = dot_tn(value, expo.astype(BF16)) * recip(total)

    def part(query, pairs):
        scores = [dot_nt(key, query) for key, _ in pairs]
        top = functools.reduce(jnp.maximum, [jnp.max(s, axis=0, keepdims=True) for s in scores])
        expo = [jnp.exp2((s - top) * RATE) for s in scores]
        total = sum(jnp.sum(e, axis=0, keepdims=True) for e in expo)
        output = sum(dot_tn(value, e.astype(BF16)) for e, (_, value) in zip(expo, pairs))
        return level(top, total), output * recip(total)

    def blend(a, b):
        top = jnp.maximum(a[0], b[0])
        left, right = jnp.exp2(a[0] - top), jnp.exp2(b[0] - top)
        total = left + right
        scale = recip(total)
        return top + jnp.log2(total), (left * scale) * a[1] + (right * scale) * b[1]

    def current(h):
        return stat[h, 0:1, :], acc[h]

    def norm(linear):
        square = jnp.mean(linear * linear, axis=0, keepdims=True)
        return linear * recip(jnp.sqrt(square + 1e-06))

    def finish(h, windowed, linear):
        mixed[cols(h), :] = (norm(linear) + windowed).astype(BF16)
        for index in order[:-1]:
            mixed_copy(h, index).start()
        gathered[h, lanes(here, HD), :] = mixed[cols(h), lanes(here, share)]

    def take(h, slot, indices, chunk_of):
        for index in indices:
            chunk_of(h, index).wait_recv()
            place = lanes(peer_of(index), share)
            mine = stat[h, 0:1, place], acc[h, :, place]
            theirs = l_recv[slot, h, 0:1, place], o_recv[slot, h, :, place].astype(F32)
            piece = (lin[h, :, place] + blend(mine, theirs)[1]).astype(BF16)
            if index:
                mixed[cols(h), place] = piece
                mixed_copy(h, index).start()
            else:
                gathered[h, lanes(here, HD), :] = piece

    tile = math.gcd(w_ref.shape[2], 512)

    def multiply(h, rows, target):
        left = gathered[h, rows, :].T
        for begin in range(0, w_ref.shape[2], tile):
            piece = slice(begin, begin + tile)
            product = jnp.dot(left, w_ref[h, rows, piece], preferred_element_type=F32)
            target[:, piece] = (summed[:, piece] + product).astype(target.dtype)

    def project(h):
        settle(w_ref.at[h], w_sem.at[h])
        settle(gathered.at[h, pl.ds(0, (peers - 1) * HD)], m_rx.at[h])
        multiply(h, pl.ds(0, peers * HD), summed)

    def project_far():
        settle(w_ref.at[last], w_sem.at[last])
        if chips > 1:
            settle(gathered.at[last, pl.ds(0, (peers - 2) * HD)], m_rx.at[last])
        for hop in range(1, chips):
            multiply(last, lanes(lax.rem(chip + hop, chips), 2 * HD), summed)

    def project_near():
        settle(gathered.at[last, pl.ds(0, HD)], m_rx.at[heads])
        multiply(last, lanes(chip, 2 * HD), out_ref)

    def wind_up(slot, level_of, chunk_of):
        level_of(inner).wait_recv()
        take(inner, slot, order[:-2], chunk_of)
        project(inner - 1)
        level_of(last).wait_recv()
        take(last, slot, order[:-1], chunk_of)
        take(inner, slot, order[-2:], chunk_of)
        project(inner)
        project_far()
        take(last, slot, order[-1:], chunk_of)

    def project_before(h):
        pl.when(h > 0)(lambda: project(h - 1))

    def weights():
        lax.fori_loop(0, heads, lambda h, c: (load_head(h), c)[1], 0)
        summed[...] = jnp.zeros_like(summed)

    def tell(slot, device):
        pl.semaphore_signal(gate.at[slot], inc=1, device_id=device, device_id_type=MESH)

    def own_state(h):
        return dot_tn(v_ref[:, cols(h)], k_ref[:, cols(h)])

    later = pl.ds(1, last)

    @pl.when(seq == 0)
    def _():
        def send(h):
            for copy in kv_copies(h):
                copy.start()

        def work(h):
            finish(h, acc[h], lin[h])
            project_before(h)

        @pl.when(core == 1)
        def _():
            loop(send, 0, 2)
            tell(1, {"head": peer_of(1)})

        @pl.when(core == 0)
        def _():
            pl.semaphore_wait(gate.at[1], 1)

        own(0)

        @pl.when(core == 0)
        def _():
            loop(send, 0, 2)

        s_send[last] = own_state(last).astype(BF16)
        state_copy(last, 1).start()
        loop(send, 2)
        weights()
        loop(own, 1)
        pl.semaphore_wait(gate.at[0], 1)
        loop(work)
        project_far()
        settle(k_ref, tx.at[0])
        settle(v_ref, tx.at[1])
        state_copy(last, 1).wait_send()

    @pl.when(seq == 1)
    def _():
        for copy in near_copies():
            copy.start()
        tell(0, {"seq": 2})
        weights()

        def first(h):
            own(h)
            s_own[h] = own_state(h)

        loop(first)

        def pre(h):
            for slot in range(2):
                query_copy(h, slot, 1, 0).wait_recv()
                bottom, output = part(
                    qbuf[slot, :, cols(h)], ((k_ref[:, cols(h)], v_ref[:, cols(h)]),)
                )
                pstat[slot, 0:1, :] = bottom
                pacc[slot] = output

        def rest(h, early):
            query = q_ref[:, cols(h)]
            windowed = blend(current(h), part(query, ((kbuf[:, cols(h)], vbuf[:, cols(h)]),)))[1]
            finish(h, windowed, lin[h] + dot_nt(early, query))

        def early_state(h):
            return dot_tn(vbuf[:, cols(h)], kbuf[:, cols(h)])

        for arrived, onward in zip(kv_copies(0), far_copies()):
            arrived.wait_recv()
            onward.start()
        pl.semaphore_wait(gate.at[0], 1)
        tell(0, {"seq": 0})
        rest(0, early_state(0).astype(BF16))
        pre(1)

        def early_last():
            state_copy(last, 1).wait_recv()
            s_send[last] = (s_recv[last].astype(F32) + s_own[last]).astype(BF16)
            state_copy(last, 2).start()

        def work(h, stage=0):
            arrived = kv_copies(h)
            arrived[0].wait_recv()
            for slot in range(2):
                scores = dot_nt(kbuf[:, cols(h)], qbuf[slot, :, cols(h)])
                top = jnp.max(scores, axis=0, keepdims=True)
                expo = jnp.exp2((scores - top) * RATE)
                total = jnp.sum(expo, axis=0, keepdims=True)
                pstat[slot, 1:2, :] = level(top, total)
                pstat[slot, 2:3, :] = recip(total)
                ebuf[slot] = expo.astype(BF16)
            arrived[1].wait_recv()
            if stage == 2:
                early = s_recv[h]
            else:
                early = early_state(h)
                s_send[h] = (early + s_own[h]).astype(BF16)
                state_copy(h, 2).start()
                early = early.astype(BF16)
            for slot in (1, 0):
                fresh = dot_tn(vbuf[:, cols(h)], ebuf[slot]) * pstat[slot, 2:3, :]
                bottom, output = blend(
                    (pstat[slot, 0:1, :], pacc[slot]), (pstat[slot, 1:2, :], fresh)
                )
                l_send[slot, h] = bottom
                o_send[slot, h] = output.astype(BF16)
                straight = stage and slot
                (level_onward(h) if straight else level_copy(h, slot)).start()
                for index in order[:-2] if stage else order:
                    (chunk_onward(h, index) if straight else chunk_copy(h, slot, index)).start()
            if stage == 1:
                @pl.when(core == 1)
                def _():
                    both(h, order[-2:])
            if stage == 2:
                both(h, order[-2:-1])

                @pl.when(core == 0)
                def _():
                    both(inner, order[-2:])

                both(h, order[-1:])
            else:
                if not stage:
                    pl.when(h == 1)(early_last)
                pre(h + 1)

            rest(h, early)
            project(h - 1)

        def both(h, indices):
            for index in indices:
                chunk_onward(h, index).start()
                chunk_copy(h, 0, index).start()

        loop(work, 1, inner)
        work(inner, 1)
        work(last, 2)
        project_far()
        for copy in near_copies() + far_copies():
            copy.wait_send()
        settle(s_send.at[later], tx.at[4])
        settle(l_send.at[:, later], tx.at[5])
        settle(o_send.at[:, later], tx.at[6])

    @pl.when(seq == 2)
    def _():
        for h in range(1, heads):
            query_copy(h, 0, 1, 0).start()
        for h in (inner, last):
            for copy in kv_copies(h, 2, 3):
                copy.start()
        weights()

        def first(h):
            own(h)
            s_own[h] = own_state(h)

        loop(first, 0, 2)
        pl.semaphore_wait(gate.at[0], 1)
        for index in range(1, peers):
            tell(1, {"head": peer_of(index)})
        loop(first, 2)
        pl.semaphore_wait(gate.at[1], peers - 1)
        tell(0, {"seq": 1})

        def pair(h):
            return k_ref[:, cols(h)], v_ref[:, cols(h)]

        def third(h):
            query_copy(h, 1, 2, 0).wait_recv()
            bottom, output = part(qbuf[1, :, cols(h)], (pair(h),))
            pstat[h, 0:1, :] = bottom
            pacc[h] = output

        query_copy(0, 1, 2, 0).wait_recv()
        for copy in near_copies() + far_copies():
            copy.wait_recv()
        pairs = [(kbuf[:, cols(i)], vbuf[:, cols(i)]) for i in range(2)]
        early = sum(dot_tn(value, key) for key, value in pairs)
        s_send[0] = (early + s_own[0]).astype(BF16)
        state_copy(0, 3).start()
        bottom, output = part(qbuf[1, :, cols(0)], pairs + [pair(0)])
        l_send[1, 0] = bottom
        o_send[1, 0] = output.astype(BF16)
        level_onward(0).start()
        for index in order:
            chunk_onward(0, index).start()
        query = q_ref[:, cols(0)]
        windowed = blend(current(0), part(query, pairs))[1]
        finish(0, windowed, lin[0] + dot_nt(early.astype(BF16), query))
        loop(third, 1, inner)

        def state(h):
            state_copy(h, 2).wait_recv()
            s_send[h] = (s_recv[h].astype(F32) + s_own[h]).astype(BF16)
            state_copy(h, 3).start()
            lin[h] = norm(lin[h] + dot_nt(s_recv[h], q_ref[:, cols(h)]))

        def level_here(h):
            return level_copy(h, 0)

        def chunk_here(h, index):
            return chunk_copy(h, 0, index)

        def second(h):
            state(h)
            level_copy(h, 1).wait_recv()
            mine, theirs = pstat[h, 0:1, :], l_recv[1, h]
            top = jnp.maximum(mine, theirs)
            left, right = jnp.exp2(mine - top), jnp.exp2(theirs - top)
            total = left + right
            l_send[1, h] = top + jnp.log2(total)
            pstat[h, 1:2, :] = left * recip(total)
            pstat[h, 2:3, :] = right * recip(total)
            level_onward(h).start()
            for index in order:
                chunk_copy(h, 1, index).wait_recv()
                place = lanes(peer_of(index), share)
                output = pstat[h, 1:2, place] * pacc[h, :, place]
                output += pstat[h, 2:3, place] * o_recv[1, h, :, place].astype(F32)
                o_send[1, h, :, place] = output.astype(BF16)
                chunk_onward(h, index).start()

            pl.when(h == 1)(lambda: state(last))
            level_here(h).wait_recv()
            take(h, 0, order, chunk_here)
            project(h - 1)

        loop(second, 1, inner)
        state(inner)
        wind_up(0, level_here, chunk_here)
        settle(q_ref.at[:, pl.ds(HD, width - HD)], tx.at[0])
        settle(k_ref.at[:, pl.ds(inner * HD, 2 * HD)], tx.at[2])
        settle(v_ref.at[:, pl.ds(inner * HD, 2 * HD)], tx.at[3])
        settle(s_send, tx.at[4])
        settle(l_send.at[1, pl.ds(0, inner)], tx.at[5])
        settle(o_send.at[1, pl.ds(0, inner)], tx.at[6])

    @pl.when(seq == 3)
    def _():
        for h in range(1, heads):
            query_copy(h, 1, 1, 0).start()
            if 1 < h <= inner + 1:
                query_copy(h - 2, 1, 2, 1).start()
        weights()
        loop(own)
        for h in (inner, last):
            for copy in kv_copies(h, 2, 3):
                copy.wait_recv()
            bottom, output = blend(
                current(h), part(q_ref[:, cols(h)], ((kbuf[:, cols(h)], vbuf[:, cols(h)]),))
            )
            stat[h, 0:1, :] = bottom
            acc[h] = output

        def state(h):
            state_copy(h, 3).wait_recv()
            lin[h] = norm(lin[h] + dot_nt(s_recv[h], q_ref[:, cols(h)]))

        def work(h):
            state(h)
            level_onward(h).wait_recv()
            take(h, 1, order, chunk_onward)
            project_before(h)

        loop(work, 0, inner)
        state(last)
        state(inner)
        wind_up(1, level_onward, chunk_onward)
        settle(q_ref.at[:, pl.ds(HD, width - HD)], tx.at[0])
        settle(q_ref.at[:, pl.ds(0, inner * HD)], tx.at[1])

    project_near()
    settle(mixed.at[:, pl.ds(0, length - share)], tx.at[8])


def fused(queries, keys, values, w_out):
    peers = lax.axis_size("head")
    length, width = queries.shape
    heads = width // HD
    share = length // peers
    dma = pltpu.SemaphoreType.DMA
    vmem = pl.BlockSpec(memory_space=pltpu.VMEM)
    return pl.pallas_call(
        functools.partial(kernel, peers),
        out_shape=pltpu.VMEM((share, w_out.shape[1]), BF16),
        in_specs=[pl.BlockSpec(memory_space=pltpu.HBM)] * 4,
        out_specs=vmem,
        scratch_shapes=[
            pltpu.VMEM((length, width), BF16),
            pltpu.VMEM((length, width), BF16),
            pltpu.VMEM((length, width), BF16),
            pltpu.VMEM((heads, peers * HD, w_out.shape[1]), BF16),
            pltpu.VMEM((share, w_out.shape[1]), F32),
            pltpu.VMEM((length, width), BF16),
            pltpu.VMEM((length, width), BF16),
            pltpu.VMEM((2, length, width), BF16),
            pltpu.VMEM((2, length, length), BF16),
            pltpu.VMEM((heads, HD, length), F32),
            pltpu.VMEM((heads, 8, length), F32),
            pltpu.VMEM((2, heads, HD, length), BF16),
            pltpu.VMEM((2, heads, HD, length), BF16),
            pltpu.VMEM((2, heads, 1, length), F32),
            pltpu.VMEM((2, heads, 1, length), F32),
            pltpu.VMEM((heads, HD, HD), F32),
            pltpu.VMEM((heads, HD, HD), BF16),
            pltpu.VMEM((heads, HD, HD), BF16),
            pltpu.VMEM((heads, HD, length), F32),
            pltpu.VMEM((heads, HD, length), F32),
            pltpu.VMEM((heads, 8, length), F32),
            pltpu.VMEM((width, length), BF16),
            pltpu.VMEM((heads, peers * HD, share), BF16),
            dma((3,)), dma((heads,)), dma((9,)), dma((2, heads)), dma((2, heads)),
            dma((2 * (heads - 1), peers)), dma((2 * (heads - 1),)), dma((heads,)), dma((heads + 1,)),
            pltpu.SemaphoreType.REGULAR((2,)),
        ],
        compiler_params=pltpu.CompilerParams(
            collective_id=0, has_side_effects=True, vmem_limit_bytes=56 * 1024 * 1024
        ),
    )(queries, keys, values, w_out)


def shifted(value, axis, steps):
    count = lax.axis_size(axis)
    first, last = (max(0, -steps), min(count, count - steps))
    return lax.ppermute(value, axis, [(source, source + steps) for source in range(first, last)])


def fits(queries):
    length, width = queries.shape
    blocks = lax.axis_size("seq")
    share = length // lax.axis_size("head")
    whole = share % HD == 0 and width % HD == 0 and width >= 4 * HD and lax.axis_size("head") % 2 == 0
    return blocks == 4 and blocks * length <= WINDOW and whole


def per_device(queries, keys, values, w_out):
    if fits(queries):
        return fused(queries, keys, values, w_out)
    length_dev, width = queries.shape
    heads_dev = width // HD
    block_rows = min(512, length_dev)
    block_count = length_dev // block_rows
    highest = lax.Precision.HIGHEST
    seq_index = lax.axis_index("seq")
    q_blocks = queries.reshape(block_count, block_rows, heads_dev, HD)
    k_blocks = keys.reshape(block_count, block_rows, heads_dev, HD)
    v_blocks = values.reshape(block_count, block_rows, heads_dev, HD)
    block_states = jnp.einsum(
        "bkhd,bkhe->bhde", k_blocks, v_blocks, preferred_element_type=jnp.float32
    )
    own_state = jnp.sum(block_states, axis=0)
    earlier = jnp.cumsum(block_states, axis=0) - block_states
    piece = lax.all_gather(own_state[None], "seq", axis=0, tiled=True)
    order = jnp.arange(piece.shape[0], dtype=jnp.int32)
    keep = order < seq_index
    prefix = jnp.sum(jnp.where(keep[:, None, None, None], piece, 0.0), axis=0)
    causal = jnp.arange(block_rows)[:, None] >= jnp.arange(block_rows)[None, :]
    local_scores = jnp.einsum(
        "bqhd,bkhd->bhqk", q_blocks, k_blocks, preferred_element_type=jnp.float32
    )
    local_scores = jnp.where(causal, local_scores, 0.0)
    intra = jnp.einsum(
        "bhqk,bkhe->bqhe", local_scores, v_blocks.astype(jnp.float32), precision=highest
    )
    state_before = prefix[None] + earlier
    inter = jnp.einsum(
        "bqhd,bhde->bqhe", q_blocks.astype(jnp.float32), state_before, precision=highest
    )
    linear = (intra + inter).reshape(length_dev, heads_dev, HD)
    normed = linear / jnp.sqrt(jnp.mean(linear * linear, axis=-1, keepdims=True) + 1e-06)
    reach = min(WINDOW // length_dev, lax.axis_size("seq") - 1)
    received = [shifted((keys, values), "seq", distance) for distance in range(1, reach + 1)]
    pad_rows = WINDOW - reach * length_dev
    filler = jnp.zeros((pad_rows, width), keys.dtype)
    wide_keys = jnp.concatenate([filler] + [pair[0] for pair in reversed(received)] + [keys], 0)
    wide_values = jnp.concatenate([filler] + [pair[1] for pair in reversed(received)] + [values], 0)
    wide_keys = wide_keys.reshape(-1, heads_dev, HD)
    wide_values = wide_values.reshape(-1, heads_dev, HD)
    scale = 1.0 / math.sqrt(HD)
    span = WINDOW + block_rows
    query_pos = jnp.arange(block_rows, dtype=jnp.int32)[:, None]
    key_pos = jnp.arange(span, dtype=jnp.int32)[None, :]
    band = (key_pos > query_pos) & (key_pos <= query_pos + WINDOW)
    rows_q = queries.reshape(block_rows, heads_dev, HD)
    anchor = seq_index * length_dev + 0 - WINDOW
    valid = band & (anchor + key_pos >= 0)
    scores = (
        jnp.einsum("qhd,khd->hqk", rows_q, wide_keys, preferred_element_type=jnp.float32) * scale
    )
    scores = jnp.where(valid[None], scores, -1e30)
    top = jnp.max(scores, axis=-1, keepdims=True)
    expo = jnp.where(valid[None], jnp.exp(scores - top), 0.0)
    total = jnp.sum(expo, axis=-1)
    weights = expo.astype(jnp.bfloat16)
    summed = jnp.einsum("hqk,khe->qhe", weights, wide_values, preferred_element_type=jnp.float32)
    pieces = summed / jnp.transpose(total)[:, :, None]
    mixed = (normed + pieces).astype(jnp.bfloat16).reshape(length_dev, width)
    head_count = lax.axis_size("head")
    share = length_dev // head_count
    grouped = mixed.reshape(head_count, share, width)
    return jnp.dot(
        lax.all_to_all(grouped, "head", split_axis=0, concat_axis=2, tiled=True)[0],
        w_out,
        preferred_element_type=jnp.float32,
    ).astype(jnp.bfloat16)


def solution(mesh):
    return jax.shard_map(
        per_device,
        mesh=mesh,
        in_specs=(
            P(("groups", "seq"), "head"),
            P(("groups", "seq"), "head"),
            P(("groups", "seq"), "head"),
            P(),
        ),
        out_specs=P(("groups", "seq", "head"), None),
        check_vma=False,
    )
```

```python
import functools
import math

import jax
import jax.numpy as jnp
from jax import lax
from jax.experimental import pallas as pl
from jax.experimental.pallas import tpu as pltpu
from jax.sharding import PartitionSpec as P

HD = 128
WINDOW = 2048
MESH = pl.DeviceIdType.MESH
F32 = jnp.float32
BF16 = jnp.bfloat16
RATE = math.log2(math.e) / math.sqrt(HD)
FLOOR = -1e30


def dot_nt(a, b):
    return lax.dot_general(a, b, (((1,), (1,)), ((), ())), preferred_element_type=F32)


def dot_tn(a, b):
    return lax.dot_general(a, b, (((0,), (0,)), ((), ())), preferred_element_type=F32)


def recip(x):
    return 1.0 / x


def lanes(index, size):
    return pl.ds(pl.multiple_of(index * size, size), size)


def kernel(
    peers, q_hbm, k_hbm, v_hbm, w_hbm, out_ref, q_ref, k_ref, v_ref,
    w_ref, summed, kbuf, vbuf, qbuf, ebuf, pacc, pstat, o_send, o_recv, l_send, l_recv,
    s_own, s_send, s_recv, acc, lin, stat, mixed, gathered,
    in_sem, w_sem, tx, kv_rx, q_rx, o_rx, l_rx, s_rx, m_rx, gate,
):
    seq = lax.axis_index("seq")
    here = lax.axis_index("head")
    length, width = q_ref.shape
    heads = width // HD
    share = length // peers
    chip, core = here // 2, here % 2
    chips = peers // 2
    order = list(range(2, peers)) + [1, 0]
    last = heads - 1
    inner = last - 1

    def peer_of(index, sign=1):
        hop, flip = index // 2, index % 2
        other = lax.rem(chip + sign * hop + chips, chips)
        return other * 2 + (1 - core if flip else core)

    barrier = pltpu.get_barrier_semaphore()

    def greet(device):
        pl.semaphore_signal(barrier, inc=1, device_id=device, device_id_type=MESH)

    circle = {0: (1,), 1: (0, 2, 3), 2: (1, 3), 3: (2,)}
    near = {0: (1,), 1: (), 2: range(1, peers), 3: range(1, peers)}
    for place, friends in circle.items():
        @pl.when(seq == place)
        def _():
            for friend in friends:
                greet({"seq": friend})

            for index in near[place]:
                greet({"head": peer_of(index)})

    loads = [
        pltpu.make_async_copy(source, target, in_sem.at[i])
        for i, (source, target) in enumerate(((q_hbm, q_ref), (k_hbm, k_ref), (v_hbm, v_ref)))
    ]
    for load in loads:
        load.start()

    def load_w(h, peer):
        return pltpu.make_async_copy(
            w_hbm.at[pl.ds(pl.multiple_of(peer * width + h * HD, HD), HD), :],
            w_ref.at[h, pl.ds(peer * HD, HD), :],
            w_sem.at[h],
        )

    def load_head(h):
        for peer in range(peers):
            load_w(h, peer).start()

    for place in circle:
        @pl.when(seq == place)
        def _():
            count = sum(place in friends for friends in circle.values())
            pl.semaphore_wait(barrier, count + len(near[place]))
    for load in loads:
        load.wait()

    def cols(h):
        return lanes(h, HD)

    def remote(source, target, sent, landed, device):
        return pltpu.make_async_remote_copy(
            src_ref=source, dst_ref=target, send_sem=tx.at[sent], recv_sem=landed,
            device_id=device, device_id_type=MESH,
        )

    def settle(ref, semaphore):
        pltpu.make_async_copy(ref, ref, semaphore).wait()

    def kv_copies(h, first=0, target=1):
        return [
            remote(
                source.at[:, cols(h)], buffer.at[:, cols(h)], first + i, kv_rx.at[i, h],
                {"seq": target},
            )
            for i, (source, buffer) in enumerate(((k_ref, kbuf), (v_ref, vbuf)))
        ]

    def near_copies():
        return [
            remote(
                source.at[:, cols(0)], buffer.at[:, cols(1)], i, kv_rx.at[i, 1], {"seq": 2}
            )
            for i, (source, buffer) in enumerate(((k_ref, kbuf), (v_ref, vbuf)))
        ]

    def far_copies():
        return [
            remote(
                buffer.at[:, cols(0)], buffer.at[:, cols(0)], 2 + i, kv_rx.at[i, 0], {"seq": 2}
            )
            for i, buffer in enumerate((kbuf, vbuf))
        ]

    def query_copy(h, slot, target, sent):
        return remote(
            q_ref.at[:, cols(h)], qbuf.at[slot, :, cols(h)], sent, q_rx.at[slot, h], {"seq": target}
        )

    def row(h, slot):
        return slot * (heads - 1) + h - 1

    def level_copy(h, slot):
        return remote(
            l_send.at[slot, h], l_recv.at[slot, h], 5, l_rx.at[row(h, slot)], {"seq": 2}
        )

    def chunk_copy(h, slot, index):
        place = lanes(peer_of(index), share)
        return remote(
            o_send.at[slot, h, :, place], o_recv.at[slot, h, :, place], 6,
            o_rx.at[row(h, slot), index], {"seq": 2},
        )

    def level_onward(h):
        return remote(l_send.at[1, h], l_recv.at[1, h], 5, l_rx.at[h], {"seq": 3})

    def chunk_onward(h, index):
        place = lanes(peer_of(index), share)
        return remote(
            o_send.at[1, h, :, place], o_recv.at[1, h, :, place], 6, o_rx.at[h, index], {"seq": 3}
        )

    def state_copy(h, target):
        return remote(s_send.at[h], s_recv.at[h], 4, s_rx.at[h], {"seq": target})

    def mixed_copy(h, index):
        target = peer_of(index)
        return remote(
            mixed.at[cols(h), lanes(target, share)], gathered.at[h, lanes(here, HD), :],
            8, m_rx.at[h + h // last if index == 1 else h], {"head": target},
        )

    def loop(body, first=0, last=heads):
        lax.fori_loop(first, last, lambda h, c: (body(h), c)[1], 0)

    causal = lax.broadcasted_iota(jnp.int32, (length, length), 0) <= lax.broadcasted_iota(
        jnp.int32, (length, length), 1
    )

    def level(top, total):
        return top * RATE + jnp.log2(total)

    def own(h):
        query, key, value = q_ref[:, cols(h)], k_ref[:, cols(h)], v_ref[:, cols(h)]
        scores = dot_nt(key, query)
        kept = jnp.where(causal, scores, 0.0)
        coarse = kept.astype(BF16)
        fine = (kept - coarse.astype(F32)).astype(BF16)
        lin[h] = dot_tn(value, coarse) + dot_tn(value, fine)
        scores = jnp.where(causal, scores, FLOOR)
        top = jnp.max(scores, axis=0, keepdims=True)
        expo = jnp.exp2((scores - top) * RATE)
        total = jnp.sum(expo, axis=0, keepdims=True)
        stat[h, 0:1, :] = level(top, total)
        acc[h] = dot_tn(value, expo.astype(BF16)) * recip(total)

    def part(query, pairs):
        scores = [dot_nt(key, query) for key, _ in pairs]
        top = functools.reduce(jnp.maximum, [jnp.max(s, axis=0, keepdims=True) for s in scores])
        expo = [jnp.exp2((s - top) * RATE) for s in scores]
        total = sum(jnp.sum(e, axis=0, keepdims=True) for e in expo)
        output = sum(dot_tn(value, e.astype(BF16)) for e, (_, value) in zip(expo, pairs))
        return level(top, total), output * recip(total)

    def blend(a, b):
        top = jnp.maximum(a[0], b[0])
        left, right = jnp.exp2(a[0] - top), jnp.exp2(b[0] - top)
        total = left + right
        scale = recip(total)
        return top + jnp.log2(total), (left * scale) * a[1] + (right * scale) * b[1]

    def current(h):
        return stat[h, 0:1, :], acc[h]

    def norm(linear):
        square = jnp.mean(linear * linear, axis=0, keepdims=True)
        return linear * recip(jnp.sqrt(square + 1e-06))

    def finish(h, windowed, linear):
        mixed[cols(h), :] = (norm(linear) + windowed).astype(BF16)
        for index in order[:-1]:
            mixed_copy(h, index).start()
        gathered[h, lanes(here, HD), :] = mixed[cols(h), lanes(here, share)]

    def take(h, slot, indices, chunk_of):
        for index in indices:
            chunk_of(h, index).wait_recv()
            place = lanes(peer_of(index), share)
            mine = stat[h, 0:1, place], acc[h, :, place]
            theirs = l_recv[slot, h, 0:1, place], o_recv[slot, h, :, place].astype(F32)
            piece = (lin[h, :, place] + blend(mine, theirs)[1]).astype(BF16)
            if index:
                mixed[cols(h), place] = piece
                mixed_copy(h, index).start()
            else:
                gathered[h, lanes(here, HD), :] = piece

    tile = math.gcd(w_ref.shape[2], 512)

    def multiply(h, rows, target):
        left = gathered[h, rows, :].T
        for begin in range(0, w_ref.shape[2], tile):
            piece = slice(begin, begin + tile)
            product = jnp.dot(left, w_ref[h, rows, piece], preferred_element_type=F32)
            target[:, piece] = (summed[:, piece] + product).astype(target.dtype)

    def project(h):
        settle(w_ref.at[h], w_sem.at[h])
        settle(gathered.at[h, pl.ds(0, (peers - 1) * HD)], m_rx.at[h])
        multiply(h, pl.ds(0, peers * HD), summed)

    def project_far():
        settle(w_ref.at[last], w_sem.at[last])
        if chips > 1:
            settle(gathered.at[last, pl.ds(0, (peers - 2) * HD)], m_rx.at[last])
        for hop in range(1, chips):
            multiply(last, lanes(lax.rem(chip + hop, chips), 2 * HD), summed)

    def project_near():
        settle(gathered.at[last, pl.ds(0, HD)], m_rx.at[heads])
        multiply(last, lanes(chip, 2 * HD), out_ref)

    def wind_up(slot, level_of, chunk_of):
        level_of(inner).wait_recv()
        take(inner, slot, order[:-2], chunk_of)
        project(inner - 1)
        level_of(last).wait_recv()
        take(last, slot, order[:-1], chunk_of)
        take(inner, slot, order[-2:], chunk_of)
        project(inner)
        project_far()
        take(last, slot, order[-1:], chunk_of)

    def project_before(h):
        pl.when(h > 0)(lambda: project(h - 1))

    def weights():
        lax.fori_loop(0, heads, lambda h, c: (load_head(h), c)[1], 0)
        summed[...] = jnp.zeros_like(summed)

    def tell(slot, device):
        pl.semaphore_signal(gate.at[slot], inc=1, device_id=device, device_id_type=MESH)

    def own_state(h):
        return dot_tn(v_ref[:, cols(h)], k_ref[:, cols(h)])

    later = pl.ds(1, last)

    @pl.when(seq == 0)
    def _():
        def send(h):
            for copy in kv_copies(h):
                copy.start()

        def work(h):
            finish(h, acc[h], lin[h])
            project_before(h)

        @pl.when(core == 1)
        def _():
            loop(send, 0, 2)
            tell(1, {"head": peer_of(1)})

        @pl.when(core == 0)
        def _():
            pl.semaphore_wait(gate.at[1], 1)

        own(0)

        @pl.when(core == 0)
        def _():
            loop(send, 0, 2)

        s_send[last] = own_state(last).astype(BF16)
        state_copy(last, 1).start()
        loop(send, 2)
        weights()
        loop(own, 1)
        pl.semaphore_wait(gate.at[0], 1)
        loop(work)
        project_far()
        settle(k_ref, tx.at[0])
        settle(v_ref, tx.at[1])
        state_copy(last, 1).wait_send()

    @pl.when(seq == 1)
    def _():
        for copy in near_copies():
            copy.start()
        tell(0, {"seq": 2})
        weights()

        def first(h):
            own(h)
            s_own[h] = own_state(h)

        loop(first)

        def pre(h):
            for slot in range(2):
                query_copy(h, slot, 1, 0).wait_recv()
                bottom, output = part(
                    qbuf[slot, :, cols(h)], ((k_ref[:, cols(h)], v_ref[:, cols(h)]),)
                )
                pstat[slot, 0:1, :] = bottom
                pacc[slot] = output

        def rest(h, early):
            query = q_ref[:, cols(h)]
            windowed = blend(current(h), part(query, ((kbuf[:, cols(h)], vbuf[:, cols(h)]),)))[1]
            finish(h, windowed, lin[h] + dot_nt(early, query))

        def early_state(h):
            return dot_tn(vbuf[:, cols(h)], kbuf[:, cols(h)])

        for arrived, onward in zip(kv_copies(0), far_copies()):
            arrived.wait_recv()
            onward.start()
        pl.semaphore_wait(gate.at[0], 1)
        tell(0, {"seq": 0})
        rest(0, early_state(0).astype(BF16))
        pre(1)

        def early_last():
            state_copy(last, 1).wait_recv()
            s_send[last] = (s_recv[last].astype(F32) + s_own[last]).astype(BF16)
            state_copy(last, 2).start()

        def work(h, stage=0):
            arrived = kv_copies(h)
            arrived[0].wait_recv()
            for slot in range(2):
                scores = dot_nt(kbuf[:, cols(h)], qbuf[slot, :, cols(h)])
                top = jnp.max(scores, axis=0, keepdims=True)
                expo = jnp.exp2((scores - top) * RATE)
                total = jnp.sum(expo, axis=0, keepdims=True)
                pstat[slot, 1:2, :] = level(top, total)
                pstat[slot, 2:3, :] = recip(total)
                ebuf[slot] = expo.astype(BF16)
            arrived[1].wait_recv()
            if stage == 2:
                early = s_recv[h]
            else:
                early = early_state(h)
                s_send[h] = (early + s_own[h]).astype(BF16)
                state_copy(h, 2).start()
                early = early.astype(BF16)
            for slot in (1, 0):
                fresh = dot_tn(vbuf[:, cols(h)], ebuf[slot]) * pstat[slot, 2:3, :]
                bottom, output = blend(
                    (pstat[slot, 0:1, :], pacc[slot]), (pstat[slot, 1:2, :], fresh)
                )
                l_send[slot, h] = bottom
                o_send[slot, h] = output.astype(BF16)
                straight = stage and slot
                (level_onward(h) if straight else level_copy(h, slot)).start()
                for index in order[:-2] if stage else order:
                    (chunk_onward(h, index) if straight else chunk_copy(h, slot, index)).start()
            if stage == 1:
                @pl.when(core == 1)
                def _():
                    both(h, order[-2:])
            if stage == 2:
                both(h, order[-2:-1])

                @pl.when(core == 0)
                def _():
                    both(inner, order[-2:])

                both(h, order[-1:])
            else:
                if not stage:
                    pl.when(h == 1)(early_last)
                pre(h + 1)

            rest(h, early)
            project(h - 1)

        def both(h, indices):
            for index in indices:
                chunk_onward(h, index).start()
                chunk_copy(h, 0, index).start()

        loop(work, 1, inner)
        work(inner, 1)
        work(last, 2)
        project_far()
        for copy in near_copies() + far_copies():
            copy.wait_send()
        settle(s_send.at[later], tx.at[4])
        settle(l_send.at[:, later], tx.at[5])
        settle(o_send.at[:, later], tx.at[6])

    @pl.when(seq == 2)
    def _():
        for h in range(1, heads):
            query_copy(h, 0, 1, 0).start()
        for h in (inner, last):
            for copy in kv_copies(h, 2, 3):
                copy.start()
        weights()

        def first(h):
            own(h)
            s_own[h] = own_state(h)

        loop(first, 0, 2)
        pl.semaphore_wait(gate.at[0], 1)
        for index in range(1, peers):
            tell(1, {"head": peer_of(index)})
        loop(first, 2)
        pl.semaphore_wait(gate.at[1], peers - 1)
        tell(0, {"seq": 1})

        def pair(h):
            return k_ref[:, cols(h)], v_ref[:, cols(h)]

        def third(h):
            query_copy(h, 1, 2, 0).wait_recv()
            bottom, output = part(qbuf[1, :, cols(h)], (pair(h),))
            pstat[h, 0:1, :] = bottom
            pacc[h] = output

        query_copy(0, 1, 2, 0).wait_recv()
        for copy in near_copies() + far_copies():
            copy.wait_recv()
        pairs = [(kbuf[:, cols(i)], vbuf[:, cols(i)]) for i in range(2)]
        early = sum(dot_tn(value, key) for key, value in pairs)
        s_send[0] = (early + s_own[0]).astype(BF16)
        state_copy(0, 3).start()
        bottom, output = part(qbuf[1, :, cols(0)], pairs + [pair(0)])
        l_send[1, 0] = bottom
        o_send[1, 0] = output.astype(BF16)
        level_onward(0).start()
        for index in order:
            chunk_onward(0, index).start()
        query = q_ref[:, cols(0)]
        windowed = blend(current(0), part(query, pairs))[1]
        finish(0, windowed, lin[0] + dot_nt(early.astype(BF16), query))
        loop(third, 1, inner)

        def state(h):
            state_copy(h, 2).wait_recv()
            s_send[h] = (s_recv[h].astype(F32) + s_own[h]).astype(BF16)
            state_copy(h, 3).start()
            lin[h] = norm(lin[h] + dot_nt(s_recv[h], q_ref[:, cols(h)]))

        def level_here(h):
            return level_copy(h, 0)

        def chunk_here(h, index):
            return chunk_copy(h, 0, index)

        def second(h):
            state(h)
            level_copy(h, 1).wait_recv()
            mine, theirs = pstat[h, 0:1, :], l_recv[1, h]
            top = jnp.maximum(mine, theirs)
            left, right = jnp.exp2(mine - top), jnp.exp2(theirs - top)
            total = left + right
            l_send[1, h] = top + jnp.log2(total)
            pstat[h, 1:2, :] = left * recip(total)
            pstat[h, 2:3, :] = right * recip(total)
            level_onward(h).start()
            for index in order:
                chunk_copy(h, 1, index).wait_recv()
                place = lanes(peer_of(index), share)
                output = pstat[h, 1:2, place] * pacc[h, :, place]
                output += pstat[h, 2:3, place] * o_recv[1, h, :, place].astype(F32)
                o_send[1, h, :, place] = output.astype(BF16)
                chunk_onward(h, index).start()

            pl.when(h == 1)(lambda: state(last))
            level_here(h).wait_recv()
            take(h, 0, order, chunk_here)
            project(h - 1)

        loop(second, 1, inner)
        state(inner)
        wind_up(0, level_here, chunk_here)
        settle(q_ref.at[:, pl.ds(HD, width - HD)], tx.at[0])
        settle(k_ref.at[:, pl.ds(inner * HD, 2 * HD)], tx.at[2])
        settle(v_ref.at[:, pl.ds(inner * HD, 2 * HD)], tx.at[3])
        settle(s_send, tx.at[4])
        settle(l_send.at[1, pl.ds(0, inner)], tx.at[5])
        settle(o_send.at[1, pl.ds(0, inner)], tx.at[6])

    @pl.when(seq == 3)
    def _():
        query_copy(1, 1, 1, 0).start()
        query_copy(0, 1, 2, 1).start()
        for h in range(2, heads):
            query_copy(h, 1, 1, 0).start()
            if h <= inner:
                query_copy(h - 1, 1, 2, 1).start()
        weights()
        loop(own)
        for h in (inner, last):
            for copy in kv_copies(h, 2, 3):
                copy.wait_recv()
            bottom, output = blend(
                current(h), part(q_ref[:, cols(h)], ((kbuf[:, cols(h)], vbuf[:, cols(h)]),))
            )
            stat[h, 0:1, :] = bottom
            acc[h] = output

        def state(h):
            state_copy(h, 3).wait_recv()
            lin[h] = norm(lin[h] + dot_nt(s_recv[h], q_ref[:, cols(h)]))

        def work(h):
            state(h)
            level_onward(h).wait_recv()
            take(h, 1, order, chunk_onward)
            project_before(h)

        loop(work, 0, inner)
        state(last)
        state(inner)
        wind_up(1, level_onward, chunk_onward)
        settle(q_ref.at[:, pl.ds(HD, width - HD)], tx.at[0])
        settle(q_ref.at[:, pl.ds(0, inner * HD)], tx.at[1])

    project_near()
    settle(mixed.at[:, pl.ds(0, length - share)], tx.at[8])


def fused(queries, keys, values, w_out):
    peers = lax.axis_size("head")
    length, width = queries.shape
    heads = width // HD
    share = length // peers
    dma = pltpu.SemaphoreType.DMA
    vmem = pl.BlockSpec(memory_space=pltpu.VMEM)
    return pl.pallas_call(
        functools.partial(kernel, peers),
        out_shape=pltpu.VMEM((share, w_out.shape[1]), BF16),
        in_specs=[pl.BlockSpec(memory_space=pltpu.HBM)] * 4,
        out_specs=vmem,
        scratch_shapes=[
            pltpu.VMEM((length, width), BF16),
            pltpu.VMEM((length, width), BF16),
            pltpu.VMEM((length, width), BF16),
            pltpu.VMEM((heads, peers * HD, w_out.shape[1]), BF16),
            pltpu.VMEM((share, w_out.shape[1]), F32),
            pltpu.VMEM((length, width), BF16),
            pltpu.VMEM((length, width), BF16),
            pltpu.VMEM((2, length, width), BF16),
            pltpu.VMEM((2, length, length), BF16),
            pltpu.VMEM((heads, HD, length), F32),
            pltpu.VMEM((heads, 8, length), F32),
            pltpu.VMEM((2, heads, HD, length), BF16),
            pltpu.VMEM((2, heads, HD, length), BF16),
            pltpu.VMEM((2, heads, 1, length), F32),
            pltpu.VMEM((2, heads, 1, length), F32),
            pltpu.VMEM((heads, HD, HD), F32),
            pltpu.VMEM((heads, HD, HD), BF16),
            pltpu.VMEM((heads, HD, HD), BF16),
            pltpu.VMEM((heads, HD, length), F32),
            pltpu.VMEM((heads, HD, length), F32),
            pltpu.VMEM((heads, 8, length), F32),
            pltpu.VMEM((width, length), BF16),
            pltpu.VMEM((heads, peers * HD, share), BF16),
            dma((3,)), dma((heads,)), dma((9,)), dma((2, heads)), dma((2, heads)),
            dma((2 * (heads - 1), peers)), dma((2 * (heads - 1),)), dma((heads,)), dma((heads + 1,)),
            pltpu.SemaphoreType.REGULAR((2,)),
        ],
        compiler_params=pltpu.CompilerParams(
            collective_id=0, has_side_effects=True, vmem_limit_bytes=56 * 1024 * 1024
        ),
    )(queries, keys, values, w_out)


def shifted(value, axis, steps):
    count = lax.axis_size(axis)
    first, last = (max(0, -steps), min(count, count - steps))
    return lax.ppermute(value, axis, [(source, source + steps) for source in range(first, last)])


def fits(queries):
    length, width = queries.shape
    blocks = lax.axis_size("seq")
    share = length // lax.axis_size("head")
    whole = share % HD == 0 and width % HD == 0 and width >= 4 * HD and lax.axis_size("head") % 2 == 0
    return blocks == 4 and blocks * length <= WINDOW and whole


def per_device(queries, keys, values, w_out):
    if fits(queries):
        return fused(queries, keys, values, w_out)
    length_dev, width = queries.shape
    heads_dev = width // HD
    block_rows = min(512, length_dev)
    block_count = length_dev // block_rows
    highest = lax.Precision.HIGHEST
    seq_index = lax.axis_index("seq")
    q_blocks = queries.reshape(block_count, block_rows, heads_dev, HD)
    k_blocks = keys.reshape(block_count, block_rows, heads_dev, HD)
    v_blocks = values.reshape(block_count, block_rows, heads_dev, HD)
    block_states = jnp.einsum(
        "bkhd,bkhe->bhde", k_blocks, v_blocks, preferred_element_type=jnp.float32
    )
    own_state = jnp.sum(block_states, axis=0)
    earlier = jnp.cumsum(block_states, axis=0) - block_states
    piece = lax.all_gather(own_state[None], "seq", axis=0, tiled=True)
    order = jnp.arange(piece.shape[0], dtype=jnp.int32)
    keep = order < seq_index
    prefix = jnp.sum(jnp.where(keep[:, None, None, None], piece, 0.0), axis=0)
    causal = jnp.arange(block_rows)[:, None] >= jnp.arange(block_rows)[None, :]
    local_scores = jnp.einsum(
        "bqhd,bkhd->bhqk", q_blocks, k_blocks, preferred_element_type=jnp.float32
    )
    local_scores = jnp.where(causal, local_scores, 0.0)
    intra = jnp.einsum(
        "bhqk,bkhe->bqhe", local_scores, v_blocks.astype(jnp.float32), precision=highest
    )
    state_before = prefix[None] + earlier
    inter = jnp.einsum(
        "bqhd,bhde->bqhe", q_blocks.astype(jnp.float32), state_before, precision=highest
    )
    linear = (intra + inter).reshape(length_dev, heads_dev, HD)
    normed = linear / jnp.sqrt(jnp.mean(linear * linear, axis=-1, keepdims=True) + 1e-06)
    reach = min(WINDOW // length_dev, lax.axis_size("seq") - 1)
    received = [shifted((keys, values), "seq", distance) for distance in range(1, reach + 1)]
    pad_rows = WINDOW - reach * length_dev
    filler = jnp.zeros((pad_rows, width), keys.dtype)
    wide_keys = jnp.concatenate([filler] + [pair[0] for pair in reversed(received)] + [keys], 0)
    wide_values = jnp.concatenate([filler] + [pair[1] for pair in reversed(received)] + [values], 0)
    wide_keys = wide_keys.reshape(-1, heads_dev, HD)
    wide_values = wide_values.reshape(-1, heads_dev, HD)
    scale = 1.0 / math.sqrt(HD)
    span = WINDOW + block_rows
    query_pos = jnp.arange(block_rows, dtype=jnp.int32)[:, None]
    key_pos = jnp.arange(span, dtype=jnp.int32)[None, :]
    band = (key_pos > query_pos) & (key_pos <= query_pos + WINDOW)
    rows_q = queries.reshape(block_rows, heads_dev, HD)
    anchor = seq_index * length_dev + 0 - WINDOW
    valid = band & (anchor + key_pos >= 0)
    scores = (
        jnp.einsum("qhd,khd->hqk", rows_q, wide_keys, preferred_element_type=jnp.float32) * scale
    )
    scores = jnp.where(valid[None], scores, -1e30)
    top = jnp.max(scores, axis=-1, keepdims=True)
    expo = jnp.where(valid[None], jnp.exp(scores - top), 0.0)
    total = jnp.sum(expo, axis=-1)
    weights = expo.astype(jnp.bfloat16)
    summed = jnp.einsum("hqk,khe->qhe", weights, wide_values, preferred_element_type=jnp.float32)
    pieces = summed / jnp.transpose(total)[:, :, None]
    mixed = (normed + pieces).astype(jnp.bfloat16).reshape(length_dev, width)
    head_count = lax.axis_size("head")
    share = length_dev // head_count
    grouped = mixed.reshape(head_count, share, width)
    return jnp.dot(
        lax.all_to_all(grouped, "head", split_axis=0, concat_axis=2, tiled=True)[0],
        w_out,
        preferred_element_type=jnp.float32,
    ).astype(jnp.bfloat16)


def solution(mesh):
    return jax.shard_map(
        per_device,
        mesh=mesh,
        in_specs=(
            P(("groups", "seq"), "head"),
            P(("groups", "seq"), "head"),
            P(("groups", "seq"), "head"),
            P(),
        ),
        out_specs=P(("groups", "seq", "head"), None),
        check_vma=False,
    )
```

```python
import functools
import math

import jax
import jax.numpy as jnp
from jax import lax
from jax.experimental import pallas as pl
from jax.experimental.pallas import tpu as pltpu
from jax.sharding import PartitionSpec as P

HD = 128
WINDOW = 2048
MESH = pl.DeviceIdType.MESH
F32 = jnp.float32
BF16 = jnp.bfloat16
RATE = math.log2(math.e) / math.sqrt(HD)
FLOOR = -1e30


def dot_nt(a, b):
    return lax.dot_general(a, b, (((1,), (1,)), ((), ())), preferred_element_type=F32)


def dot_tn(a, b):
    return lax.dot_general(a, b, (((0,), (0,)), ((), ())), preferred_element_type=F32)


def recip(x):
    return 1.0 / x


def lanes(index, size):
    return pl.ds(pl.multiple_of(index * size, size), size)


def kernel(
    peers, q_hbm, k_hbm, v_hbm, w_hbm, out_ref, q_ref, k_ref, v_ref,
    w_ref, summed, kbuf, vbuf, qbuf, ebuf, pacc, pstat, o_send, o_recv, l_send, l_recv,
    s_own, s_send, s_recv, acc, lin, stat, mixed, gathered,
    in_sem, w_sem, tx, kv_rx, q_rx, o_rx, l_rx, s_rx, m_rx, gate,
):
    seq = lax.axis_index("seq")
    here = lax.axis_index("head")
    length, width = q_ref.shape
    heads = width // HD
    share = length // peers
    chip, core = here // 2, here % 2
    chips = peers // 2
    order = list(range(2, peers)) + [1, 0]
    last = heads - 1
    inner = last - 1

    def peer_of(index, sign=1):
        hop, flip = index // 2, index % 2
        other = lax.rem(chip + sign * hop + chips, chips)
        return other * 2 + (1 - core if flip else core)

    barrier = pltpu.get_barrier_semaphore()

    def greet(device):
        pl.semaphore_signal(barrier, inc=1, device_id=device, device_id_type=MESH)

    circle = {0: (1,), 1: (0, 2, 3), 2: (1, 3), 3: (2,)}
    near = {0: (1,), 1: (), 2: range(1, peers), 3: range(1, peers)}
    for place, friends in circle.items():
        @pl.when(seq == place)
        def _():
            for friend in friends:
                greet({"seq": friend})

            for index in near[place]:
                greet({"head": peer_of(index)})

    loads = [
        pltpu.make_async_copy(source, target, in_sem.at[i])
        for i, (source, target) in enumerate(((q_hbm, q_ref), (k_hbm, k_ref), (v_hbm, v_ref)))
    ]
    for load in loads:
        load.start()

    def load_w(h, peer):
        return pltpu.make_async_copy(
            w_hbm.at[pl.ds(pl.multiple_of(peer * width + h * HD, HD), HD), :],
            w_ref.at[h, pl.ds(peer * HD, HD), :],
            w_sem.at[0],
        )

    def load_head(h):
        for peer in range(peers):
            load_w(h, peer).start()

    for place in circle:
        @pl.when(seq == place)
        def _():
            count = sum(place in friends for friends in circle.values())
            pl.semaphore_wait(barrier, count + len(near[place]))
    for load in loads:
        load.wait()

    def cols(h):
        return lanes(h, HD)

    def remote(source, target, sent, landed, device):
        return pltpu.make_async_remote_copy(
            src_ref=source, dst_ref=target, send_sem=tx.at[sent], recv_sem=landed,
            device_id=device, device_id_type=MESH,
        )

    def settle(ref, semaphore):
        pltpu.make_async_copy(ref, ref, semaphore).wait()

    def kv_copies(h, first=0, target=1):
        return [
            remote(
                source.at[:, cols(h)], buffer.at[:, cols(h)], first + i, kv_rx.at[i, h],
                {"seq": target},
            )
            for i, (source, buffer) in enumerate(((k_ref, kbuf), (v_ref, vbuf)))
        ]

    def near_copies():
        return [
            remote(
                source.at[:, cols(0)], buffer.at[:, cols(1)], i, kv_rx.at[i, 1], {"seq": 2}
            )
            for i, (source, buffer) in enumerate(((k_ref, kbuf), (v_ref, vbuf)))
        ]

    def far_copies():
        return [
            remote(
                buffer.at[:, cols(0)], buffer.at[:, cols(0)], 2 + i, kv_rx.at[i, 0], {"seq": 2}
            )
            for i, buffer in enumerate((kbuf, vbuf))
        ]

    def query_copy(h, slot, target, sent):
        return remote(
            q_ref.at[:, cols(h)], qbuf.at[slot, :, cols(h)], sent, q_rx.at[slot, h], {"seq": target}
        )

    def row(h, slot):
        return slot * (heads - 1) + h - 1

    def level_copy(h, slot):
        return remote(
            l_send.at[slot, h], l_recv.at[slot, h], 5, l_rx.at[row(h, slot)], {"seq": 2}
        )

    def chunk_copy(h, slot, index):
        place = lanes(peer_of(index), share)
        return remote(
            o_send.at[slot, h, :, place], o_recv.at[slot, h, :, place], 6,
            o_rx.at[row(h, slot), index], {"seq": 2},
        )

    def level_onward(h):
        return remote(l_send.at[1, h], l_recv.at[1, h], 5, l_rx.at[h], {"seq": 3})

    def chunk_onward(h, index):
        place = lanes(peer_of(index), share)
        return remote(
            o_send.at[1, h, :, place], o_recv.at[1, h, :, place], 6, o_rx.at[h, index], {"seq": 3}
        )

    def state_copy(h, target):
        return remote(s_send.at[h], s_recv.at[h], 4, s_rx.at[h], {"seq": target})

    def mixed_copy(h, index):
        target = peer_of(index)
        return remote(
            mixed.at[cols(h), lanes(target, share)], gathered.at[h, lanes(here, HD), :],
            8, m_rx.at[h], {"head": target},
        )

    def loop(body, first=0, last=heads):
        lax.fori_loop(first, last, lambda h, c: (body(h), c)[1], 0)

    causal = lax.broadcasted_iota(jnp.int32, (length, length), 0) <= lax.broadcasted_iota(
        jnp.int32, (length, length), 1
    )

    def level(top, total):
        return top * RATE + jnp.log2(total)

    def own(h):
        query, key, value = q_ref[:, cols(h)], k_ref[:, cols(h)], v_ref[:, cols(h)]
        scores = dot_nt(key, query)
        kept = jnp.where(causal, scores, 0.0)
        coarse = kept.astype(BF16)
        fine = (kept - coarse.astype(F32)).astype(BF16)
        lin[h] = dot_tn(value, coarse) + dot_tn(value, fine)
        scores = jnp.where(causal, scores, FLOOR)
        top = jnp.max(scores, axis=0, keepdims=True)
        expo = jnp.exp2((scores - top) * RATE)
        total = jnp.sum(expo, axis=0, keepdims=True)
        stat[h, 0:1, :] = level(top, total)
        acc[h] = dot_tn(value, expo.astype(BF16)) * recip(total)

    def part(query, pairs):
        scores = [dot_nt(key, query) for key, _ in pairs]
        top = functools.reduce(jnp.maximum, [jnp.max(s, axis=0, keepdims=True) for s in scores])
        expo = [jnp.exp2((s - top) * RATE) for s in scores]
        total = sum(jnp.sum(e, axis=0, keepdims=True) for e in expo)
        output = sum(dot_tn(value, e.astype(BF16)) for e, (_, value) in zip(expo, pairs))
        return level(top, total), output * recip(total)

    def blend(a, b):
        top = jnp.maximum(a[0], b[0])
        left, right = jnp.exp2(a[0] - top), jnp.exp2(b[0] - top)
        total = left + right
        scale = recip(total)
        return top + jnp.log2(total), (left * scale) * a[1] + (right * scale) * b[1]

    def current(h):
        return stat[h, 0:1, :], acc[h]

    def norm(linear):
        square = jnp.mean(linear * linear, axis=0, keepdims=True)
        return linear * recip(jnp.sqrt(square + 1e-06))

    def finish(h, windowed, linear):
        mixed[cols(h), :] = (norm(linear) + windowed).astype(BF16)
        for index in order[:-1]:
            mixed_copy(h, index).start()
        gathered[h, lanes(here, HD), :] = mixed[cols(h), lanes(here, share)]

    def take(h, slot, indices, chunk_of):
        for index in indices:
            chunk_of(h, index).wait_recv()
            place = lanes(peer_of(index), share)
            mine = stat[h, 0:1, place], acc[h, :, place]
            theirs = l_recv[slot, h, 0:1, place], o_recv[slot, h, :, place].astype(F32)
            piece = (lin[h, :, place] + blend(mine, theirs)[1]).astype(BF16)
            if index:
                mixed[cols(h), place] = piece
                mixed_copy(h, index).start()
            else:
                gathered[h, lanes(here, HD), :] = piece

    tile = math.gcd(w_ref.shape[2], 512)

    def project(h, target=None):
        settle(gathered.at[h, pl.ds(0, (peers - 1) * HD)], m_rx.at[h])
        rows = pl.ds(0, peers * HD)
        left = gathered[h, rows, :].T
        target = summed if target is None else target
        for begin in range(0, w_ref.shape[2], tile):
            piece = slice(begin, begin + tile)
            product = jnp.dot(left, w_ref[h, rows, piece], preferred_element_type=F32)
            target[:, piece] = (summed[:, piece] + product).astype(target.dtype)

    def wind_up(slot, level_of, chunk_of):
        level_of(inner).wait_recv()
        take(inner, slot, order[:-2], chunk_of)
        project(inner - 1)
        level_of(last).wait_recv()
        take(last, slot, order[:-1], chunk_of)
        take(inner, slot, order[-2:], chunk_of)
        project(inner)
        take(last, slot, order[-1:], chunk_of)

    def project_before(h):
        pl.when(h > 0)(lambda: project(h - 1))

    def weights():
        lax.fori_loop(0, heads, lambda h, c: (load_head(h), c)[1], 0)
        summed[...] = jnp.zeros_like(summed)

    def tell(slot, device):
        pl.semaphore_signal(gate.at[slot], inc=1, device_id=device, device_id_type=MESH)

    def own_state(h):
        return dot_tn(v_ref[:, cols(h)], k_ref[:, cols(h)])

    later = pl.ds(1, last)

    @pl.when(seq == 0)
    def _():
        def send(h):
            for copy in kv_copies(h):
                copy.start()

        def work(h):
            finish(h, acc[h], lin[h])
            project_before(h)

        @pl.when(core == 1)
        def _():
            loop(send, 0, 2)
            tell(1, {"head": peer_of(1)})

        @pl.when(core == 0)
        def _():
            pl.semaphore_wait(gate.at[1], 1)

        own(0)

        @pl.when(core == 0)
        def _():
            loop(send, 0, 2)

        s_send[last] = own_state(last).astype(BF16)
        state_copy(last, 1).start()
        loop(send, 2)
        weights()
        loop(own, 1)
        pl.semaphore_wait(gate.at[0], 1)
        settle(w_ref, w_sem.at[0])
        loop(work)
        settle(k_ref, tx.at[0])
        settle(v_ref, tx.at[1])
        state_copy(last, 1).wait_send()

    @pl.when(seq == 1)
    def _():
        for copy in near_copies():
            copy.start()
        tell(0, {"seq": 2})
        weights()

        def first(h):
            own(h)
            s_own[h] = own_state(h)

        loop(first)

        def pre(h):
            for slot in range(2):
                query_copy(h, slot, 1, 0).wait_recv()
                bottom, output = part(
                    qbuf[slot, :, cols(h)], ((k_ref[:, cols(h)], v_ref[:, cols(h)]),)
                )
                pstat[slot, 0:1, :] = bottom
                pacc[slot] = output

        def rest(h, early):
            query = q_ref[:, cols(h)]
            windowed = blend(current(h), part(query, ((kbuf[:, cols(h)], vbuf[:, cols(h)]),)))[1]
            finish(h, windowed, lin[h] + dot_nt(early, query))

        def early_state(h):
            return dot_tn(vbuf[:, cols(h)], kbuf[:, cols(h)])

        for arrived, onward in zip(kv_copies(0), far_copies()):
            arrived.wait_recv()
            onward.start()
        pl.semaphore_wait(gate.at[0], 1)
        tell(0, {"seq": 0})
        settle(w_ref, w_sem.at[0])
        rest(0, early_state(0).astype(BF16))
        pre(1)

        def early_last():
            state_copy(last, 1).wait_recv()
            s_send[last] = (s_recv[last].astype(F32) + s_own[last]).astype(BF16)
            state_copy(last, 2).start()

        def work(h, stage=0):
            arrived = kv_copies(h)
            arrived[0].wait_recv()
            for slot in range(2):
                scores = dot_nt(kbuf[:, cols(h)], qbuf[slot, :, cols(h)])
                top = jnp.max(scores, axis=0, keepdims=True)
                expo = jnp.exp2((scores - top) * RATE)
                total = jnp.sum(expo, axis=0, keepdims=True)
                pstat[slot, 1:2, :] = level(top, total)
                pstat[slot, 2:3, :] = recip(total)
                ebuf[slot] = expo.astype(BF16)
            arrived[1].wait_recv()
            if stage == 2:
                early = s_recv[h]
            else:
                early = early_state(h)
                s_send[h] = (early + s_own[h]).astype(BF16)
                state_copy(h, 2).start()
                early = early.astype(BF16)
            for slot in (1, 0):
                fresh = dot_tn(vbuf[:, cols(h)], ebuf[slot]) * pstat[slot, 2:3, :]
                bottom, output = blend(
                    (pstat[slot, 0:1, :], pacc[slot]), (pstat[slot, 1:2, :], fresh)
                )
                l_send[slot, h] = bottom
                o_send[slot, h] = output.astype(BF16)
                straight = stage and slot
                (level_onward(h) if straight else level_copy(h, slot)).start()
                if stage < 2:
                    for index in order[:-2] if stage else order:
                        (chunk_onward(h, index) if straight else chunk_copy(h, slot, index)).start()
            if stage == 1:
                @pl.when(core == 1)
                def _():
                    both(h, order[-2:])
            if stage == 2:
                both(h, order[:-1])

                @pl.when(core == 0)
                def _():
                    both(inner, order[-2:])

                both(h, order[-1:])
            else:
                if not stage:
                    pl.when(h == 1)(early_last)
                pre(h + 1)

            rest(h, early)
            project(h - 1)

        def both(h, indices):
            for index in indices:
                chunk_copy(h, 0, index).start()
                chunk_onward(h, index).start()

        loop(work, 1, inner)
        work(inner, 1)
        work(last, 2)
        for copy in near_copies() + far_copies():
            copy.wait_send()
        settle(s_send.at[later], tx.at[4])
        settle(l_send.at[:, later], tx.at[5])
        settle(o_send.at[:, later], tx.at[6])

    @pl.when(seq == 2)
    def _():
        for h in range(1, heads):
            query_copy(h, 0, 1, 0).start()
        for h in (inner, last):
            for copy in kv_copies(h, 2, 3):
                copy.start()
        weights()

        def first(h):
            own(h)
            s_own[h] = own_state(h)

        loop(first, 0, 2)
        pl.semaphore_wait(gate.at[0], 1)
        for index in range(1, peers):
            tell(1, {"head": peer_of(index)})
        loop(first, 2)
        pl.semaphore_wait(gate.at[1], peers - 1)
        tell(0, {"seq": 1})

        def pair(h):
            return k_ref[:, cols(h)], v_ref[:, cols(h)]

        def third(h):
            query_copy(h, 1, 2, 0).wait_recv()
            bottom, output = part(qbuf[1, :, cols(h)], (pair(h),))
            pstat[h, 0:1, :] = bottom
            pacc[h] = output

        query_copy(0, 1, 2, 0).wait_recv()
        settle(w_ref, w_sem.at[0])
        for copy in near_copies() + far_copies():
            copy.wait_recv()
        pairs = [(kbuf[:, cols(i)], vbuf[:, cols(i)]) for i in range(2)]
        early = sum(dot_tn(value, key) for key, value in pairs)
        s_send[0] = (early + s_own[0]).astype(BF16)
        state_copy(0, 3).start()
        bottom, output = part(qbuf[1, :, cols(0)], pairs + [pair(0)])
        l_send[1, 0] = bottom
        o_send[1, 0] = output.astype(BF16)
        level_onward(0).start()
        for index in order:
            chunk_onward(0, index).start()
        query = q_ref[:, cols(0)]
        windowed = blend(current(0), part(query, pairs))[1]
        finish(0, windowed, lin[0] + dot_nt(early.astype(BF16), query))
        loop(third, 1, inner)

        def state(h):
            state_copy(h, 2).wait_recv()
            s_send[h] = (s_recv[h].astype(F32) + s_own[h]).astype(BF16)
            state_copy(h, 3).start()
            lin[h] = norm(lin[h] + dot_nt(s_recv[h], q_ref[:, cols(h)]))

        def level_here(h):
            return level_copy(h, 0)

        def chunk_here(h, index):
            return chunk_copy(h, 0, index)

        def second(h):
            state(h)
            level_copy(h, 1).wait_recv()
            mine, theirs = pstat[h, 0:1, :], l_recv[1, h]
            top = jnp.maximum(mine, theirs)
            left, right = jnp.exp2(mine - top), jnp.exp2(theirs - top)
            total = left + right
            l_send[1, h] = top + jnp.log2(total)
            pstat[h, 1:2, :] = left * recip(total)
            pstat[h, 2:3, :] = right * recip(total)
            level_onward(h).start()
            for index in order:
                chunk_copy(h, 1, index).wait_recv()
                place = lanes(peer_of(index), share)
                output = pstat[h, 1:2, place] * pacc[h, :, place]
                output += pstat[h, 2:3, place] * o_recv[1, h, :, place].astype(F32)
                o_send[1, h, :, place] = output.astype(BF16)
                chunk_onward(h, index).start()

            pl.when(h == 1)(lambda: state(last))
            level_here(h).wait_recv()
            take(h, 0, order, chunk_here)
            project(h - 1)

        loop(second, 1, inner)
        state(inner)
        wind_up(0, level_here, chunk_here)
        settle(q_ref.at[:, pl.ds(HD, width - HD)], tx.at[0])
        settle(k_ref.at[:, pl.ds(inner * HD, 2 * HD)], tx.at[2])
        settle(v_ref.at[:, pl.ds(inner * HD, 2 * HD)], tx.at[3])
        settle(s_send, tx.at[4])
        settle(l_send.at[1, pl.ds(0, inner)], tx.at[5])
        settle(o_send.at[1, pl.ds(0, inner)], tx.at[6])

    @pl.when(seq == 3)
    def _():
        query_copy(1, 1, 1, 0).start()
        query_copy(0, 1, 2, 1).start()
        for h in range(2, heads):
            query_copy(h, 1, 1, 0).start()
            if h <= inner:
                query_copy(h - 1, 1, 2, 1).start()
        weights()
        loop(own)
        for h in (inner, last):
            for copy in kv_copies(h, 2, 3):
                copy.wait_recv()
            bottom, output = blend(
                current(h), part(q_ref[:, cols(h)], ((kbuf[:, cols(h)], vbuf[:, cols(h)]),))
            )
            stat[h, 0:1, :] = bottom
            acc[h] = output

        def state(h):
            state_copy(h, 3).wait_recv()
            lin[h] = norm(lin[h] + dot_nt(s_recv[h], q_ref[:, cols(h)]))

        def work(h):
            state(h)
            level_onward(h).wait_recv()
            take(h, 1, order, chunk_onward)
            project_before(h)

        settle(w_ref, w_sem.at[0])
        loop(work, 0, inner)
        state(last)
        state(inner)
        wind_up(1, level_onward, chunk_onward)
        settle(q_ref.at[:, pl.ds(HD, width - HD)], tx.at[0])
        settle(q_ref.at[:, pl.ds(0, inner * HD)], tx.at[1])

    project(last, out_ref)
    settle(mixed.at[:, pl.ds(0, length - share)], tx.at[8])


def fused(queries, keys, values, w_out):
    peers = lax.axis_size("head")
    length, width = queries.shape
    heads = width // HD
    share = length // peers
    dma = pltpu.SemaphoreType.DMA
    vmem = pl.BlockSpec(memory_space=pltpu.VMEM)
    return pl.pallas_call(
        functools.partial(kernel, peers),
        out_shape=pltpu.VMEM((share, w_out.shape[1]), BF16),
        in_specs=[pl.BlockSpec(memory_space=pltpu.HBM)] * 4,
        out_specs=vmem,
        scratch_shapes=[
            pltpu.VMEM((length, width), BF16),
            pltpu.VMEM((length, width), BF16),
            pltpu.VMEM((length, width), BF16),
            pltpu.VMEM((heads, peers * HD, w_out.shape[1]), BF16),
            pltpu.VMEM((share, w_out.shape[1]), F32),
            pltpu.VMEM((length, width), BF16),
            pltpu.VMEM((length, width), BF16),
            pltpu.VMEM((2, length, width), BF16),
            pltpu.VMEM((2, length, length), BF16),
            pltpu.VMEM((heads, HD, length), F32),
            pltpu.VMEM((heads, 8, length), F32),
            pltpu.VMEM((2, heads, HD, length), BF16),
            pltpu.VMEM((2, heads, HD, length), BF16),
            pltpu.VMEM((2, heads, 1, length), F32),
            pltpu.VMEM((2, heads, 1, length), F32),
            pltpu.VMEM((heads, HD, HD), F32),
            pltpu.VMEM((heads, HD, HD), BF16),
            pltpu.VMEM((heads, HD, HD), BF16),
            pltpu.VMEM((heads, HD, length), F32),
            pltpu.VMEM((heads, HD, length), F32),
            pltpu.VMEM((heads, 8, length), F32),
            pltpu.VMEM((width, length), BF16),
            pltpu.VMEM((heads, peers * HD, share), BF16),
            dma((3,)), dma((1,)), dma((9,)), dma((2, heads)), dma((2, heads)),
            dma((2 * (heads - 1), peers)), dma((2 * (heads - 1),)), dma((heads,)), dma((heads,)),
            pltpu.SemaphoreType.REGULAR((2,)),
        ],
        compiler_params=pltpu.CompilerParams(
            collective_id=0, has_side_effects=True, vmem_limit_bytes=56 * 1024 * 1024
        ),
    )(queries, keys, values, w_out)


def shifted(value, axis, steps):
    count = lax.axis_size(axis)
    first, last = (max(0, -steps), min(count, count - steps))
    return lax.ppermute(value, axis, [(source, source + steps) for source in range(first, last)])


def fits(queries):
    length, width = queries.shape
    blocks = lax.axis_size("seq")
    share = length // lax.axis_size("head")
    whole = share % HD == 0 and width % HD == 0 and width >= 4 * HD and lax.axis_size("head") % 2 == 0
    return blocks == 4 and blocks * length <= WINDOW and whole


def per_device(queries, keys, values, w_out):
    if fits(queries):
        return fused(queries, keys, values, w_out)
    length_dev, width = queries.shape
    heads_dev = width // HD
    block_rows = min(512, length_dev)
    block_count = length_dev // block_rows
    highest = lax.Precision.HIGHEST
    seq_index = lax.axis_index("seq")
    q_blocks = queries.reshape(block_count, block_rows, heads_dev, HD)
    k_blocks = keys.reshape(block_count, block_rows, heads_dev, HD)
    v_blocks = values.reshape(block_count, block_rows, heads_dev, HD)
    block_states = jnp.einsum(
        "bkhd,bkhe->bhde", k_blocks, v_blocks, preferred_element_type=jnp.float32
    )
    own_state = jnp.sum(block_states, axis=0)
    earlier = jnp.cumsum(block_states, axis=0) - block_states
    piece = lax.all_gather(own_state[None], "seq", axis=0, tiled=True)
    order = jnp.arange(piece.shape[0], dtype=jnp.int32)
    keep = order < seq_index
    prefix = jnp.sum(jnp.where(keep[:, None, None, None], piece, 0.0), axis=0)
    causal = jnp.arange(block_rows)[:, None] >= jnp.arange(block_rows)[None, :]
    local_scores = jnp.einsum(
        "bqhd,bkhd->bhqk", q_blocks, k_blocks, preferred_element_type=jnp.float32
    )
    local_scores = jnp.where(causal, local_scores, 0.0)
    intra = jnp.einsum(
        "bhqk,bkhe->bqhe", local_scores, v_blocks.astype(jnp.float32), precision=highest
    )
    state_before = prefix[None] + earlier
    inter = jnp.einsum(
        "bqhd,bhde->bqhe", q_blocks.astype(jnp.float32), state_before, precision=highest
    )
    linear = (intra + inter).reshape(length_dev, heads_dev, HD)
    normed = linear / jnp.sqrt(jnp.mean(linear * linear, axis=-1, keepdims=True) + 1e-06)
    reach = min(WINDOW // length_dev, lax.axis_size("seq") - 1)
    received = [shifted((keys, values), "seq", distance) for distance in range(1, reach + 1)]
    pad_rows = WINDOW - reach * length_dev
    filler = jnp.zeros((pad_rows, width), keys.dtype)
    wide_keys = jnp.concatenate([filler] + [pair[0] for pair in reversed(received)] + [keys], 0)
    wide_values = jnp.concatenate([filler] + [pair[1] for pair in reversed(received)] + [values], 0)
    wide_keys = wide_keys.reshape(-1, heads_dev, HD)
    wide_values = wide_values.reshape(-1, heads_dev, HD)
    scale = 1.0 / math.sqrt(HD)
    span = WINDOW + block_rows
    query_pos = jnp.arange(block_rows, dtype=jnp.int32)[:, None]
    key_pos = jnp.arange(span, dtype=jnp.int32)[None, :]
    band = (key_pos > query_pos) & (key_pos <= query_pos + WINDOW)
    rows_q = queries.reshape(block_rows, heads_dev, HD)
    anchor = seq_index * length_dev + 0 - WINDOW
    valid = band & (anchor + key_pos >= 0)
    scores = (
        jnp.einsum("qhd,khd->hqk", rows_q, wide_keys, preferred_element_type=jnp.float32) * scale
    )
    scores = jnp.where(valid[None], scores, -1e30)
    top = jnp.max(scores, axis=-1, keepdims=True)
    expo = jnp.where(valid[None], jnp.exp(scores - top), 0.0)
    total = jnp.sum(expo, axis=-1)
    weights = expo.astype(jnp.bfloat16)
    summed = jnp.einsum("hqk,khe->qhe", weights, wide_values, preferred_element_type=jnp.float32)
    pieces = summed / jnp.transpose(total)[:, :, None]
    mixed = (normed + pieces).astype(jnp.bfloat16).reshape(length_dev, width)
    head_count = lax.axis_size("head")
    share = length_dev // head_count
    grouped = mixed.reshape(head_count, share, width)
    return jnp.dot(
        lax.all_to_all(grouped, "head", split_axis=0, concat_axis=2, tiled=True)[0],
        w_out,
        preferred_element_type=jnp.float32,
    ).astype(jnp.bfloat16)


def solution(mesh):
    return jax.shard_map(
        per_device,
        mesh=mesh,
        in_specs=(
            P(("groups", "seq"), "head"),
            P(("groups", "seq"), "head"),
            P(("groups", "seq"), "head"),
            P(),
        ),
        out_specs=P(("groups", "seq", "head"), None),
        check_vma=False,
    )
```

```python
import functools
import math

import jax
import jax.numpy as jnp
from jax import lax
from jax.experimental import pallas as pl
from jax.experimental.pallas import tpu as pltpu
from jax.sharding import PartitionSpec as P

HD = 128
WINDOW = 2048
MESH = pl.DeviceIdType.MESH
F32 = jnp.float32
BF16 = jnp.bfloat16
RATE = math.log2(math.e) / math.sqrt(HD)
FLOOR = -1e30


def dot_nt(a, b):
    return lax.dot_general(a, b, (((1,), (1,)), ((), ())), preferred_element_type=F32)


def dot_tn(a, b):
    return lax.dot_general(a, b, (((0,), (0,)), ((), ())), preferred_element_type=F32)


def recip(x):
    return 1.0 / x


def lanes(index, size):
    return pl.ds(pl.multiple_of(index * size, size), size)


def kernel(
    peers, q_hbm, k_hbm, v_hbm, w_hbm, out_ref, q_ref, k_ref, v_ref,
    w_ref, summed, kbuf, vbuf, qbuf, ebuf, pacc, pstat, o_send, o_recv, l_send, l_recv,
    s_own, s_send, s_recv, acc, lin, stat, mixed, gathered,
    in_sem, w_sem, tx, kv_rx, q_rx, o_rx, l_rx, s_rx, m_rx, gate,
):
    seq = lax.axis_index("seq")
    here = lax.axis_index("head")
    length, width = q_ref.shape
    heads = width // HD
    share = length // peers
    chip, core = here // 2, here % 2
    chips = peers // 2
    order = list(range(2, peers)) + [1, 0]
    last = heads - 1
    inner = last - 1

    def peer_of(index, sign=1):
        hop, flip = index // 2, index % 2
        other = lax.rem(chip + sign * hop + chips, chips)
        return other * 2 + (1 - core if flip else core)

    barrier = pltpu.get_barrier_semaphore()

    def greet(device):
        pl.semaphore_signal(barrier, inc=1, device_id=device, device_id_type=MESH)

    circle = {0: (1,), 1: (0, 2, 3), 2: (1, 3), 3: (2,)}
    near = {0: (1,), 1: (), 2: range(1, peers), 3: range(1, peers)}
    for place, friends in circle.items():
        @pl.when(seq == place)
        def _():
            for friend in friends:
                greet({"seq": friend})

            for index in near[place]:
                greet({"head": peer_of(index)})

    loads = [
        pltpu.make_async_copy(source, target, in_sem.at[i])
        for i, (source, target) in enumerate(((q_hbm, q_ref), (k_hbm, k_ref), (v_hbm, v_ref)))
    ]
    for load in loads:
        load.start()

    def load_w(h, peer):
        return pltpu.make_async_copy(
            w_hbm.at[pl.ds(pl.multiple_of(peer * width + h * HD, HD), HD), :],
            w_ref.at[h, pl.ds(peer * HD, HD), :],
            w_sem.at[0],
        )

    def load_head(h):
        for peer in range(peers):
            load_w(h, peer).start()

    for place in circle:
        @pl.when(seq == place)
        def _():
            count = sum(place in friends for friends in circle.values())
            pl.semaphore_wait(barrier, count + len(near[place]))
    for load in loads:
        load.wait()

    def cols(h):
        return lanes(h, HD)

    def remote(source, target, sent, landed, device):
        return pltpu.make_async_remote_copy(
            src_ref=source, dst_ref=target, send_sem=tx.at[sent], recv_sem=landed,
            device_id=device, device_id_type=MESH,
        )

    def settle(ref, semaphore):
        pltpu.make_async_copy(ref, ref, semaphore).wait()

    def kv_copies(h, first=0, target=1):
        return [
            remote(
                source.at[:, cols(h)], buffer.at[:, cols(h)], first + i, kv_rx.at[i, h],
                {"seq": target},
            )
            for i, (source, buffer) in enumerate(((k_ref, kbuf), (v_ref, vbuf)))
        ]

    def near_copies():
        return [
            remote(
                source.at[:, cols(0)], buffer.at[:, cols(1)], i, kv_rx.at[i, 1], {"seq": 2}
            )
            for i, (source, buffer) in enumerate(((k_ref, kbuf), (v_ref, vbuf)))
        ]

    def far_copies():
        return [
            remote(
                buffer.at[:, cols(0)], buffer.at[:, cols(0)], 2 + i, kv_rx.at[i, 0], {"seq": 2}
            )
            for i, buffer in enumerate((kbuf, vbuf))
        ]

    def query_copy(h, slot, target, sent):
        return remote(
            q_ref.at[:, cols(h)], qbuf.at[slot, :, cols(h)], sent, q_rx.at[slot, h], {"seq": target}
        )

    def row(h, slot):
        return slot * (heads - 1) + h - 1

    def level_copy(h, slot):
        return remote(
            l_send.at[slot, h], l_recv.at[slot, h], 5, l_rx.at[row(h, slot)], {"seq": 2}
        )

    def chunk_copy(h, slot, index):
        place = lanes(peer_of(index), share)
        return remote(
            o_send.at[slot, h, :, place], o_recv.at[slot, h, :, place], 6,
            o_rx.at[row(h, slot), index], {"seq": 2},
        )

    def level_onward(h):
        return remote(l_send.at[1, h], l_recv.at[1, h], 5, l_rx.at[h], {"seq": 3})

    def chunk_onward(h, index):
        place = lanes(peer_of(index), share)
        return remote(
            o_send.at[1, h, :, place], o_recv.at[1, h, :, place], 6, o_rx.at[h, index], {"seq": 3}
        )

    def state_copy(h, target):
        return remote(s_send.at[h], s_recv.at[h], 4, s_rx.at[h], {"seq": target})

    def mixed_copy(h, index):
        target = peer_of(index)
        return remote(
            mixed.at[cols(h), lanes(target, share)], gathered.at[h, lanes(here, HD), :],
            8, m_rx.at[h], {"head": target},
        )

    def loop(body, first=0, last=heads):
        lax.fori_loop(first, last, lambda h, c: (body(h), c)[1], 0)

    causal = lax.broadcasted_iota(jnp.int32, (length, length), 0) <= lax.broadcasted_iota(
        jnp.int32, (length, length), 1
    )

    def level(top, total):
        return top * RATE + jnp.log2(total)

    def own(h):
        query, key, value = q_ref[:, cols(h)], k_ref[:, cols(h)], v_ref[:, cols(h)]
        scores = dot_nt(key, query)
        kept = jnp.where(causal, scores, 0.0)
        coarse = kept.astype(BF16)
        fine = (kept - coarse.astype(F32)).astype(BF16)
        lin[h] = dot_tn(value, coarse) + dot_tn(value, fine)
        scores = jnp.where(causal, scores, FLOOR)
        top = jnp.max(scores, axis=0, keepdims=True)
        expo = jnp.exp2((scores - top) * RATE)
        total = jnp.sum(expo, axis=0, keepdims=True)
        stat[h, 0:1, :] = level(top, total)
        acc[h] = dot_tn(value, expo.astype(BF16)) * recip(total)

    def part(query, pairs):
        scores = [dot_nt(key, query) for key, _ in pairs]
        top = functools.reduce(jnp.maximum, [jnp.max(s, axis=0, keepdims=True) for s in scores])
        expo = [jnp.exp2((s - top) * RATE) for s in scores]
        total = sum(jnp.sum(e, axis=0, keepdims=True) for e in expo)
        output = sum(dot_tn(value, e.astype(BF16)) for e, (_, value) in zip(expo, pairs))
        return level(top, total), output * recip(total)

    def blend(a, b):
        top = jnp.maximum(a[0], b[0])
        left, right = jnp.exp2(a[0] - top), jnp.exp2(b[0] - top)
        total = left + right
        scale = recip(total)
        return top + jnp.log2(total), (left * scale) * a[1] + (right * scale) * b[1]

    def current(h):
        return stat[h, 0:1, :], acc[h]

    def norm(linear):
        square = jnp.mean(linear * linear, axis=0, keepdims=True)
        return linear * recip(jnp.sqrt(square + 1e-06))

    def finish(h, windowed, linear):
        mixed[cols(h), :] = (norm(linear) + windowed).astype(BF16)
        for index in order[:-1]:
            mixed_copy(h, index).start()
        gathered[h, lanes(here, HD), :] = mixed[cols(h), lanes(here, share)]

    def take(h, slot, indices, chunk_of):
        for index in indices:
            chunk_of(h, index).wait_recv()
            place = lanes(peer_of(index), share)
            mine = stat[h, 0:1, place], acc[h, :, place]
            theirs = l_recv[slot, h, 0:1, place], o_recv[slot, h, :, place].astype(F32)
            piece = (lin[h, :, place] + blend(mine, theirs)[1]).astype(BF16)
            if index:
                mixed[cols(h), place] = piece
                mixed_copy(h, index).start()
            else:
                gathered[h, lanes(here, HD), :] = piece

    tile = math.gcd(w_ref.shape[2], 512)

    def project(h, target=None):
        settle(gathered.at[h, pl.ds(0, (peers - 1) * HD)], m_rx.at[h])
        rows = pl.ds(0, peers * HD)
        left = gathered[h, rows, :].T
        target = summed if target is None else target
        for begin in range(0, w_ref.shape[2], tile):
            piece = slice(begin, begin + tile)
            product = jnp.dot(left, w_ref[h, rows, piece], preferred_element_type=F32)
            target[:, piece] = (summed[:, piece] + product).astype(target.dtype)

    def wind_up(slot, level_of, chunk_of):
        level_of(inner).wait_recv()
        take(inner, slot, order[:-2], chunk_of)
        project(inner - 1)
        level_of(last).wait_recv()
        take(last, slot, order[:-1], chunk_of)
        take(inner, slot, order[-2:], chunk_of)
        project(inner)
        take(last, slot, order[-1:], chunk_of)

    def project_before(h):
        pl.when(h > 0)(lambda: project(h - 1))

    def weights():
        lax.fori_loop(0, heads, lambda h, c: (load_head(h), c)[1], 0)
        summed[...] = jnp.zeros_like(summed)

    def tell(slot, device):
        pl.semaphore_signal(gate.at[slot], inc=1, device_id=device, device_id_type=MESH)

    def own_state(h):
        return dot_tn(v_ref[:, cols(h)], k_ref[:, cols(h)])

    later = pl.ds(1, last)

    @pl.when(seq == 0)
    def _():
        def send(h):
            for copy in kv_copies(h):
                copy.start()

        def work(h):
            finish(h, acc[h], lin[h])
            project_before(h)

        @pl.when(core == 1)
        def _():
            loop(send, 0, 2)
            tell(1, {"head": peer_of(1)})

        @pl.when(core == 0)
        def _():
            pl.semaphore_wait(gate.at[1], 1)

        own(0)

        @pl.when(core == 0)
        def _():
            loop(send, 0, 2)

        s_send[last] = own_state(last).astype(BF16)
        state_copy(last, 1).start()
        loop(send, 2)
        weights()
        loop(own, 1)
        pl.semaphore_wait(gate.at[0], 1)
        settle(w_ref, w_sem.at[0])
        loop(work)
        settle(k_ref, tx.at[0])
        settle(v_ref, tx.at[1])
        state_copy(last, 1).wait_send()

    @pl.when(seq == 1)
    def _():
        for copy in near_copies():
            copy.start()
        tell(0, {"seq": 2})
        weights()

        def first(h):
            own(h)
            s_own[h] = own_state(h)

        loop(first)

        def pre(h):
            for slot in range(2):
                query_copy(h, slot, 1, 0).wait_recv()
                bottom, output = part(
                    qbuf[slot, :, cols(h)], ((k_ref[:, cols(h)], v_ref[:, cols(h)]),)
                )
                pstat[slot, 0:1, :] = bottom
                pacc[slot] = output

        def rest(h, early):
            query = q_ref[:, cols(h)]
            windowed = blend(current(h), part(query, ((kbuf[:, cols(h)], vbuf[:, cols(h)]),)))[1]
            finish(h, windowed, lin[h] + dot_nt(early, query))

        def early_state(h):
            return dot_tn(vbuf[:, cols(h)], kbuf[:, cols(h)])

        for arrived, onward in zip(kv_copies(0), far_copies()):
            arrived.wait_recv()
            onward.start()
        pl.semaphore_wait(gate.at[0], 1)
        tell(0, {"seq": 0})
        settle(w_ref, w_sem.at[0])
        rest(0, early_state(0).astype(BF16))
        pre(1)

        def early_last():
            state_copy(last, 1).wait_recv()
            s_send[last] = (s_recv[last].astype(F32) + s_own[last]).astype(BF16)
            state_copy(last, 2).start()

        def work(h, stage=0):
            arrived = kv_copies(h)
            arrived[0].wait_recv()
            for slot in range(2):
                scores = dot_nt(kbuf[:, cols(h)], qbuf[slot, :, cols(h)])
                top = jnp.max(scores, axis=0, keepdims=True)
                expo = jnp.exp2((scores - top) * RATE)
                total = jnp.sum(expo, axis=0, keepdims=True)
                pstat[slot, 1:2, :] = level(top, total)
                pstat[slot, 2:3, :] = recip(total)
                ebuf[slot] = expo.astype(BF16)
            arrived[1].wait_recv()
            if stage == 2:
                early = s_recv[h]
            else:
                early = early_state(h)
                s_send[h] = (early + s_own[h]).astype(BF16)
                state_copy(h, 2).start()
                early = early.astype(BF16)
            for slot in (1, 0):
                fresh = dot_tn(vbuf[:, cols(h)], ebuf[slot]) * pstat[slot, 2:3, :]
                bottom, output = blend(
                    (pstat[slot, 0:1, :], pacc[slot]), (pstat[slot, 1:2, :], fresh)
                )
                l_send[slot, h] = bottom
                o_send[slot, h] = output.astype(BF16)
                straight = stage and slot
                (level_onward(h) if straight else level_copy(h, slot)).start()
                if stage < 2:
                    for index in order[:-2] if stage else order:
                        (chunk_onward(h, index) if straight else chunk_copy(h, slot, index)).start()
            if stage == 1:
                @pl.when(core == 1)
                def _():
                    both(h, order[-2:])
            if stage == 2:
                both(h, order[:-1])

                @pl.when(core == 0)
                def _():
                    both(inner, order[-2:])

                both(h, order[-1:])
            elif not stage:
                pl.when(h == 1)(early_last)
            rest(h, early)
            project(h - 1)
            if stage < 2:
                pre(h + 1)

        def both(h, indices):
            for index in indices:
                chunk_copy(h, 0, index).start()
                chunk_onward(h, index).start()

        loop(work, 1, inner)
        work(inner, 1)
        work(last, 2)
        for copy in near_copies() + far_copies():
            copy.wait_send()
        settle(s_send.at[later], tx.at[4])
        settle(l_send.at[:, later], tx.at[5])
        settle(o_send.at[:, later], tx.at[6])

    @pl.when(seq == 2)
    def _():
        for h in range(1, heads):
            query_copy(h, 0, 1, 0).start()
        for h in (inner, last):
            for copy in kv_copies(h, 2, 3):
                copy.start()
        weights()

        def first(h):
            own(h)
            s_own[h] = own_state(h)

        loop(first, 0, 2)
        pl.semaphore_wait(gate.at[0], 1)
        for index in range(1, peers):
            tell(1, {"head": peer_of(index)})
        loop(first, 2)
        pl.semaphore_wait(gate.at[1], peers - 1)
        tell(0, {"seq": 1})

        def pair(h):
            return k_ref[:, cols(h)], v_ref[:, cols(h)]

        def third(h):
            query_copy(h, 1, 2, 0).wait_recv()
            bottom, output = part(qbuf[1, :, cols(h)], (pair(h),))
            pstat[h, 0:1, :] = bottom
            pacc[h] = output

        query_copy(0, 1, 2, 0).wait_recv()
        settle(w_ref, w_sem.at[0])
        for copy in near_copies() + far_copies():
            copy.wait_recv()
        pairs = [(kbuf[:, cols(i)], vbuf[:, cols(i)]) for i in range(2)]
        early = sum(dot_tn(value, key) for key, value in pairs)
        s_send[0] = (early + s_own[0]).astype(BF16)
        state_copy(0, 3).start()
        bottom, output = part(qbuf[1, :, cols(0)], pairs + [pair(0)])
        l_send[1, 0] = bottom
        o_send[1, 0] = output.astype(BF16)
        level_onward(0).start()
        for index in order:
            chunk_onward(0, index).start()
        query = q_ref[:, cols(0)]
        windowed = blend(current(0), part(query, pairs))[1]
        finish(0, windowed, lin[0] + dot_nt(early.astype(BF16), query))
        loop(third, 1, inner)

        def state(h):
            state_copy(h, 2).wait_recv()
            s_send[h] = (s_recv[h].astype(F32) + s_own[h]).astype(BF16)
            state_copy(h, 3).start()
            lin[h] = norm(lin[h] + dot_nt(s_recv[h], q_ref[:, cols(h)]))

        def level_here(h):
            return level_copy(h, 0)

        def chunk_here(h, index):
            return chunk_copy(h, 0, index)

        def second(h):
            state(h)
            level_copy(h, 1).wait_recv()
            mine, theirs = pstat[h, 0:1, :], l_recv[1, h]
            top = jnp.maximum(mine, theirs)
            left, right = jnp.exp2(mine - top), jnp.exp2(theirs - top)
            total = left + right
            l_send[1, h] = top + jnp.log2(total)
            pstat[h, 1:2, :] = left * recip(total)
            pstat[h, 2:3, :] = right * recip(total)
            level_onward(h).start()
            for index in order:
                chunk_copy(h, 1, index).wait_recv()
                place = lanes(peer_of(index), share)
                output = pstat[h, 1:2, place] * pacc[h, :, place]
                output += pstat[h, 2:3, place] * o_recv[1, h, :, place].astype(F32)
                o_send[1, h, :, place] = output.astype(BF16)
                chunk_onward(h, index).start()

            pl.when(h == 1)(lambda: state(last))
            level_here(h).wait_recv()
            take(h, 0, order, chunk_here)
            project(h - 1)

        loop(second, 1, inner)
        state(inner)
        wind_up(0, level_here, chunk_here)
        settle(q_ref.at[:, pl.ds(HD, width - HD)], tx.at[0])
        settle(k_ref.at[:, pl.ds(inner * HD, 2 * HD)], tx.at[2])
        settle(v_ref.at[:, pl.ds(inner * HD, 2 * HD)], tx.at[3])
        settle(s_send, tx.at[4])
        settle(l_send.at[1, pl.ds(0, inner)], tx.at[5])
        settle(o_send.at[1, pl.ds(0, inner)], tx.at[6])

    @pl.when(seq == 3)
    def _():
        query_copy(1, 1, 1, 0).start()
        query_copy(0, 1, 2, 1).start()
        for h in range(2, heads):
            query_copy(h, 1, 1, 0).start()
            if h <= inner:
                query_copy(h - 1, 1, 2, 1).start()
        weights()
        loop(own)
        for h in (inner, last):
            for copy in kv_copies(h, 2, 3):
                copy.wait_recv()
            bottom, output = blend(
                current(h), part(q_ref[:, cols(h)], ((kbuf[:, cols(h)], vbuf[:, cols(h)]),))
            )
            stat[h, 0:1, :] = bottom
            acc[h] = output

        def state(h):
            state_copy(h, 3).wait_recv()
            lin[h] = norm(lin[h] + dot_nt(s_recv[h], q_ref[:, cols(h)]))

        def work(h):
            state(h)
            level_onward(h).wait_recv()
            take(h, 1, order, chunk_onward)
            project_before(h)

        settle(w_ref, w_sem.at[0])
        loop(work, 0, inner)
        state(last)
        state(inner)
        wind_up(1, level_onward, chunk_onward)
        settle(q_ref.at[:, pl.ds(HD, width - HD)], tx.at[0])
        settle(q_ref.at[:, pl.ds(0, inner * HD)], tx.at[1])

    project(last, out_ref)
    settle(mixed.at[:, pl.ds(0, length - share)], tx.at[8])


def fused(queries, keys, values, w_out):
    peers = lax.axis_size("head")
    length, width = queries.shape
    heads = width // HD
    share = length // peers
    dma = pltpu.SemaphoreType.DMA
    vmem = pl.BlockSpec(memory_space=pltpu.VMEM)
    return pl.pallas_call(
        functools.partial(kernel, peers),
        out_shape=pltpu.VMEM((share, w_out.shape[1]), BF16),
        in_specs=[pl.BlockSpec(memory_space=pltpu.HBM)] * 4,
        out_specs=vmem,
        scratch_shapes=[
            pltpu.VMEM((length, width), BF16),
            pltpu.VMEM((length, width), BF16),
            pltpu.VMEM((length, width), BF16),
            pltpu.VMEM((heads, peers * HD, w_out.shape[1]), BF16),
            pltpu.VMEM((share, w_out.shape[1]), F32),
            pltpu.VMEM((length, width), BF16),
            pltpu.VMEM((length, width), BF16),
            pltpu.VMEM((2, length, width), BF16),
            pltpu.VMEM((2, length, length), BF16),
            pltpu.VMEM((heads, HD, length), F32),
            pltpu.VMEM((heads, 8, length), F32),
            pltpu.VMEM((2, heads, HD, length), BF16),
            pltpu.VMEM((2, heads, HD, length), BF16),
            pltpu.VMEM((2, heads, 1, length), F32),
            pltpu.VMEM((2, heads, 1, length), F32),
            pltpu.VMEM((heads, HD, HD), F32),
            pltpu.VMEM((heads, HD, HD), BF16),
            pltpu.VMEM((heads, HD, HD), BF16),
            pltpu.VMEM((heads, HD, length), F32),
            pltpu.VMEM((heads, HD, length), F32),
            pltpu.VMEM((heads, 8, length), F32),
            pltpu.VMEM((width, length), BF16),
            pltpu.VMEM((heads, peers * HD, share), BF16),
            dma((3,)), dma((1,)), dma((9,)), dma((2, heads)), dma((2, heads)),
            dma((2 * (heads - 1), peers)), dma((2 * (heads - 1),)), dma((heads,)), dma((heads,)),
            pltpu.SemaphoreType.REGULAR((2,)),
        ],
        compiler_params=pltpu.CompilerParams(
            collective_id=0, has_side_effects=True, vmem_limit_bytes=56 * 1024 * 1024
        ),
    )(queries, keys, values, w_out)


def shifted(value, axis, steps):
    count = lax.axis_size(axis)
    first, last = (max(0, -steps), min(count, count - steps))
    return lax.ppermute(value, axis, [(source, source + steps) for source in range(first, last)])


def fits(queries):
    length, width = queries.shape
    blocks = lax.axis_size("seq")
    share = length // lax.axis_size("head")
    whole = share % HD == 0 and width % HD == 0 and width >= 4 * HD and lax.axis_size("head") % 2 == 0
    return blocks == 4 and blocks * length <= WINDOW and whole


def per_device(queries, keys, values, w_out):
    if fits(queries):
        return fused(queries, keys, values, w_out)
    length_dev, width = queries.shape
    heads_dev = width // HD
    block_rows = min(512, length_dev)
    block_count = length_dev // block_rows
    highest = lax.Precision.HIGHEST
    seq_index = lax.axis_index("seq")
    q_blocks = queries.reshape(block_count, block_rows, heads_dev, HD)
    k_blocks = keys.reshape(block_count, block_rows, heads_dev, HD)
    v_blocks = values.reshape(block_count, block_rows, heads_dev, HD)
    block_states = jnp.einsum(
        "bkhd,bkhe->bhde", k_blocks, v_blocks, preferred_element_type=jnp.float32
    )
    own_state = jnp.sum(block_states, axis=0)
    earlier = jnp.cumsum(block_states, axis=0) - block_states
    piece = lax.all_gather(own_state[None], "seq", axis=0, tiled=True)
    order = jnp.arange(piece.shape[0], dtype=jnp.int32)
    keep = order < seq_index
    prefix = jnp.sum(jnp.where(keep[:, None, None, None], piece, 0.0), axis=0)
    causal = jnp.arange(block_rows)[:, None] >= jnp.arange(block_rows)[None, :]
    local_scores = jnp.einsum(
        "bqhd,bkhd->bhqk", q_blocks, k_blocks, preferred_element_type=jnp.float32
    )
    local_scores = jnp.where(causal, local_scores, 0.0)
    intra = jnp.einsum(
        "bhqk,bkhe->bqhe", local_scores, v_blocks.astype(jnp.float32), precision=highest
    )
    state_before = prefix[None] + earlier
    inter = jnp.einsum(
        "bqhd,bhde->bqhe", q_blocks.astype(jnp.float32), state_before, precision=highest
    )
    linear = (intra + inter).reshape(length_dev, heads_dev, HD)
    normed = linear / jnp.sqrt(jnp.mean(linear * linear, axis=-1, keepdims=True) + 1e-06)
    reach = min(WINDOW // length_dev, lax.axis_size("seq") - 1)
    received = [shifted((keys, values), "seq", distance) for distance in range(1, reach + 1)]
    pad_rows = WINDOW - reach * length_dev
    filler = jnp.zeros((pad_rows, width), keys.dtype)
    wide_keys = jnp.concatenate([filler] + [pair[0] for pair in reversed(received)] + [keys], 0)
    wide_values = jnp.concatenate([filler] + [pair[1] for pair in reversed(received)] + [values], 0)
    wide_keys = wide_keys.reshape(-1, heads_dev, HD)
    wide_values = wide_values.reshape(-1, heads_dev, HD)
    scale = 1.0 / math.sqrt(HD)
    span = WINDOW + block_rows
    query_pos = jnp.arange(block_rows, dtype=jnp.int32)[:, None]
    key_pos = jnp.arange(span, dtype=jnp.int32)[None, :]
    band = (key_pos > query_pos) & (key_pos <= query_pos + WINDOW)
    rows_q = queries.reshape(block_rows, heads_dev, HD)
    anchor = seq_index * length_dev + 0 - WINDOW
    valid = band & (anchor + key_pos >= 0)
    scores = (
        jnp.einsum("qhd,khd->hqk", rows_q, wide_keys, preferred_element_type=jnp.float32) * scale
    )
    scores = jnp.where(valid[None], scores, -1e30)
    top = jnp.max(scores, axis=-1, keepdims=True)
    expo = jnp.where(valid[None], jnp.exp(scores - top), 0.0)
    total = jnp.sum(expo, axis=-1)
    weights = expo.astype(jnp.bfloat16)
    summed = jnp.einsum("hqk,khe->qhe", weights, wide_values, preferred_element_type=jnp.float32)
    pieces = summed / jnp.transpose(total)[:, :, None]
    mixed = (normed + pieces).astype(jnp.bfloat16).reshape(length_dev, width)
    head_count = lax.axis_size("head")
    share = length_dev // head_count
    grouped = mixed.reshape(head_count, share, width)
    return jnp.dot(
        lax.all_to_all(grouped, "head", split_axis=0, concat_axis=2, tiled=True)[0],
        w_out,
        preferred_element_type=jnp.float32,
    ).astype(jnp.bfloat16)


def solution(mesh):
    return jax.shard_map(
        per_device,
        mesh=mesh,
        in_specs=(
            P(("groups", "seq"), "head"),
            P(("groups", "seq"), "head"),
            P(("groups", "seq"), "head"),
            P(),
        ),
        out_specs=P(("groups", "seq", "head"), None),
        check_vma=False,
    )
```

```python
import functools
import math

import jax
import jax.numpy as jnp
from jax import lax
from jax.experimental import pallas as pl
from jax.experimental.pallas import tpu as pltpu
from jax.sharding import PartitionSpec as P

HD = 128
WINDOW = 2048
MESH = pl.DeviceIdType.MESH
F32 = jnp.float32
BF16 = jnp.bfloat16
RATE = math.log2(math.e) / math.sqrt(HD)
FLOOR = -1e30


def dot_nt(a, b):
    return lax.dot_general(a, b, (((1,), (1,)), ((), ())), preferred_element_type=F32)


def dot_tn(a, b):
    return lax.dot_general(a, b, (((0,), (0,)), ((), ())), preferred_element_type=F32)


def recip(x):
    return 1.0 / x


def lanes(index, size):
    return pl.ds(pl.multiple_of(index * size, size), size)


def kernel(
    peers, q_hbm, k_hbm, v_hbm, w_hbm, out_ref, q_ref, k_ref, v_ref,
    w_ref, summed, kbuf, vbuf, qbuf, ebuf, pacc, pstat, o_send, o_recv, l_send, l_recv,
    s_own, s_send, s_recv, acc, lin, stat, mixed, gathered,
    tx, kv_rx, q_rx, o_rx, l_rx, s_rx, m_rx, gate,
):
    seq = lax.axis_index("seq")
    here = lax.axis_index("head")
    length, width = q_ref.shape
    heads = width // HD
    share = length // peers
    chip, core = here // 2, here % 2
    chips = peers // 2
    order = list(range(2, peers)) + [1, 0]
    last = heads - 1
    inner = last - 1

    def peer_of(index, sign=1):
        hop, flip = index // 2, index % 2
        other = lax.rem(chip + sign * hop + chips, chips)
        return other * 2 + (1 - core if flip else core)

    barrier = pltpu.get_barrier_semaphore()

    def greet(device):
        pl.semaphore_signal(barrier, inc=1, device_id=device, device_id_type=MESH)

    circle = {0: (1,), 1: (0, 2, 3), 2: (1, 3), 3: (2,)}
    near = {0: (1,), 1: (), 2: range(1, peers), 3: range(1, peers)}
    for place, friends in circle.items():
        @pl.when(seq == place)
        def _():
            for friend in friends:
                greet({"seq": friend})

            for index in near[place]:
                greet({"head": peer_of(index)})

    loads = [
        pltpu.make_async_copy(source, target, tx.at[i])
        for i, (source, target) in enumerate(((q_hbm, q_ref), (k_hbm, k_ref), (v_hbm, v_ref)))
    ]
    for load in loads:
        load.start()

    def load_w(h, peer):
        return pltpu.make_async_copy(
            w_hbm.at[pl.ds(pl.multiple_of(peer * width + h * HD, HD), HD), :],
            w_ref.at[h, pl.ds(peer * HD, HD), :],
            tx.at[8],
        )

    def load_head(h):
        for peer in range(peers):
            load_w(h, peer).start()

    for place in circle:
        @pl.when(seq == place)
        def _():
            count = sum(place in friends for friends in circle.values())
            pl.semaphore_wait(barrier, count + len(near[place]))
    for load in loads:
        load.wait()

    def cols(h):
        return lanes(h, HD)

    def remote(source, target, sent, landed, device):
        return pltpu.make_async_remote_copy(
            src_ref=source, dst_ref=target, send_sem=tx.at[sent], recv_sem=landed,
            device_id=device, device_id_type=MESH,
        )

    def settle(ref, semaphore):
        pltpu.make_async_copy(ref, ref, semaphore).wait()

    def kv_copies(h, first=0, target=1):
        return [
            remote(
                source.at[:, cols(h)], buffer.at[:, cols(h)], first + i, kv_rx.at[i, h],
                {"seq": target},
            )
            for i, (source, buffer) in enumerate(((k_ref, kbuf), (v_ref, vbuf)))
        ]

    def near_copies():
        return [
            remote(
                source.at[:, cols(0)], buffer.at[:, cols(1)], i, kv_rx.at[i, 1], {"seq": 2}
            )
            for i, (source, buffer) in enumerate(((k_ref, kbuf), (v_ref, vbuf)))
        ]

    def far_copies():
        return [
            remote(
                buffer.at[:, cols(0)], buffer.at[:, cols(0)], 2 + i, kv_rx.at[i, 0], {"seq": 2}
            )
            for i, buffer in enumerate((kbuf, vbuf))
        ]

    def query_copy(h, slot, target, sent):
        return remote(
            q_ref.at[:, cols(h)], qbuf.at[slot, :, cols(h)], sent, q_rx.at[slot, h], {"seq": target}
        )

    def row(h, slot):
        return slot * (heads - 1) + h - 1

    def level_copy(h, slot):
        return remote(
            l_send.at[slot, h], l_recv.at[slot, h], 5, l_rx.at[row(h, slot)], {"seq": 2}
        )

    def chunk_copy(h, slot, index):
        place = lanes(peer_of(index), share)
        return remote(
            o_send.at[slot, h, :, place], o_recv.at[slot, h, :, place], 6,
            o_rx.at[row(h, slot), index], {"seq": 2},
        )

    def level_onward(h):
        return remote(l_send.at[1, h], l_recv.at[1, h], 5, l_rx.at[h], {"seq": 3})

    def chunk_onward(h, index):
        place = lanes(peer_of(index), share)
        return remote(
            o_send.at[1, h, :, place], o_recv.at[1, h, :, place], 6, o_rx.at[h, index], {"seq": 3}
        )

    def state_copy(h, target):
        return remote(s_send.at[h], s_recv.at[h], 4, s_rx.at[h], {"seq": target})

    def mixed_copy(h, index):
        target = peer_of(index)
        return remote(
            mixed.at[cols(h), lanes(target, share)], gathered.at[h, lanes(here, HD), :],
            8, m_rx.at[h], {"head": target},
        )

    def loop(body, first=0, last=heads):
        lax.fori_loop(first, last, lambda h, c: (body(h), c)[1], 0)

    causal = lax.broadcasted_iota(jnp.int32, (length, length), 0) <= lax.broadcasted_iota(
        jnp.int32, (length, length), 1
    )

    def level(top, total):
        return top * RATE + jnp.log2(total)

    def own(h):
        query, key, value = q_ref[:, cols(h)], k_ref[:, cols(h)], v_ref[:, cols(h)]
        scores = dot_nt(key, query)
        kept = jnp.where(causal, scores, 0.0)
        coarse = kept.astype(BF16)
        fine = (kept - coarse.astype(F32)).astype(BF16)
        lin[h] = dot_tn(value, coarse) + dot_tn(value, fine)
        scores = jnp.where(causal, scores, FLOOR)
        top = jnp.max(scores, axis=0, keepdims=True)
        expo = jnp.exp2((scores - top) * RATE)
        total = jnp.sum(expo, axis=0, keepdims=True)
        stat[h, 0:1, :] = level(top, total)
        acc[h] = dot_tn(value, expo.astype(BF16)) * recip(total)

    def part(query, pairs):
        scores = [dot_nt(key, query) for key, _ in pairs]
        top = functools.reduce(jnp.maximum, [jnp.max(s, axis=0, keepdims=True) for s in scores])
        expo = [jnp.exp2((s - top) * RATE) for s in scores]
        total = sum(jnp.sum(e, axis=0, keepdims=True) for e in expo)
        output = sum(dot_tn(value, e.astype(BF16)) for e, (_, value) in zip(expo, pairs))
        return level(top, total), output * recip(total)

    def blend(a, b):
        top = jnp.maximum(a[0], b[0])
        left, right = jnp.exp2(a[0] - top), jnp.exp2(b[0] - top)
        total = left + right
        scale = recip(total)
        return top + jnp.log2(total), (left * scale) * a[1] + (right * scale) * b[1]

    def current(h):
        return stat[h, 0:1, :], acc[h]

    def norm(linear):
        square = jnp.mean(linear * linear, axis=0, keepdims=True)
        return linear * recip(jnp.sqrt(square + 1e-06))

    def finish(h, windowed, linear):
        mixed[cols(h), :] = (norm(linear) + windowed).astype(BF16)
        for index in order[:-1]:
            mixed_copy(h, index).start()
        gathered[h, lanes(here, HD), :] = mixed[cols(h), lanes(here, share)]

    def take(h, slot, indices, chunk_of):
        for index in indices:
            chunk_of(h, index).wait_recv()
            place = lanes(peer_of(index), share)
            mine = stat[h, 0:1, place], acc[h, :, place]
            theirs = l_recv[slot, h, 0:1, place], o_recv[slot, h, :, place].astype(F32)
            piece = (lin[h, :, place] + blend(mine, theirs)[1]).astype(BF16)
            if index:
                mixed[cols(h), place] = piece
                mixed_copy(h, index).start()
            else:
                gathered[h, lanes(here, HD), :] = piece

    tile = math.gcd(w_ref.shape[2], 512)

    def project(h, target=None):
        settle(gathered.at[h, pl.ds(0, (peers - 1) * HD)], m_rx.at[h])
        rows = pl.ds(0, peers * HD)
        left = gathered[h, rows, :].T
        target = summed if target is None else target
        for begin in range(0, w_ref.shape[2], tile):
            piece = slice(begin, begin + tile)
            product = jnp.dot(left, w_ref[h, rows, piece], preferred_element_type=F32)
            target[:, piece] = (summed[:, piece] + product).astype(target.dtype)

    def wind_up(slot, level_of, chunk_of):
        level_of(inner).wait_recv()
        take(inner, slot, order[:-2], chunk_of)
        project(inner - 1)
        level_of(last).wait_recv()
        take(last, slot, order[:-1], chunk_of)
        take(inner, slot, order[-2:], chunk_of)
        project(inner)
        take(last, slot, order[-1:], chunk_of)

    def project_before(h):
        pl.when(h > 0)(lambda: project(h - 1))

    def weights():
        lax.fori_loop(0, heads, lambda h, c: (load_head(h), c)[1], 0)
        summed[...] = jnp.zeros_like(summed)

    def tell(slot, device):
        pl.semaphore_signal(gate.at[slot], inc=1, device_id=device, device_id_type=MESH)

    def own_state(h):
        return dot_tn(v_ref[:, cols(h)], k_ref[:, cols(h)])

    later = pl.ds(1, last)

    @pl.when(seq == 0)
    def _():
        def send(h):
            for copy in kv_copies(h):
                copy.start()

        def work(h):
            finish(h, acc[h], lin[h])
            project_before(h)

        @pl.when(core == 1)
        def _():
            loop(send, 0, 2)
            tell(1, {"head": peer_of(1)})

        @pl.when(core == 0)
        def _():
            pl.semaphore_wait(gate.at[1], 1)

        own(0)

        @pl.when(core == 0)
        def _():
            loop(send, 0, 2)

        s_send[last] = own_state(last).astype(BF16)
        state_copy(last, 1).start()
        loop(send, 2)
        weights()
        loop(own, 1)
        pl.semaphore_wait(gate.at[0], 1)
        settle(w_ref, tx.at[8])
        loop(work)
        settle(k_ref, tx.at[0])
        settle(v_ref, tx.at[1])
        state_copy(last, 1).wait_send()

    @pl.when(seq == 1)
    def _():
        for copy in near_copies():
            copy.start()
        tell(0, {"seq": 2})
        weights()

        def first(h):
            own(h)
            s_own[h] = own_state(h)

        loop(first)

        def pre(h):
            for slot in range(2):
                query_copy(h, slot, 1, 0).wait_recv()
                bottom, output = part(
                    qbuf[slot, :, cols(h)], ((k_ref[:, cols(h)], v_ref[:, cols(h)]),)
                )
                pstat[slot, 0:1, :] = bottom
                pacc[slot] = output

        def rest(h, early):
            query = q_ref[:, cols(h)]
            windowed = blend(current(h), part(query, ((kbuf[:, cols(h)], vbuf[:, cols(h)]),)))[1]
            finish(h, windowed, lin[h] + dot_nt(early, query))

        def early_state(h):
            return dot_tn(vbuf[:, cols(h)], kbuf[:, cols(h)])

        for arrived, onward in zip(kv_copies(0), far_copies()):
            arrived.wait_recv()
            onward.start()
        pl.semaphore_wait(gate.at[0], 1)
        tell(0, {"seq": 0})
        settle(w_ref, tx.at[8])
        rest(0, early_state(0).astype(BF16))
        pre(1)

        def early_last():
            state_copy(last, 1).wait_recv()
            s_send[last] = (s_recv[last].astype(F32) + s_own[last]).astype(BF16)
            state_copy(last, 2).start()

        def work(h, stage=0):
            arrived = kv_copies(h)
            arrived[0].wait_recv()
            for slot in range(2):
                scores = dot_nt(kbuf[:, cols(h)], qbuf[slot, :, cols(h)])
                top = jnp.max(scores, axis=0, keepdims=True)
                expo = jnp.exp2((scores - top) * RATE)
                total = jnp.sum(expo, axis=0, keepdims=True)
                pstat[slot, 1:2, :] = level(top, total)
                pstat[slot, 2:3, :] = recip(total)
                ebuf[slot] = expo.astype(BF16)
            arrived[1].wait_recv()
            if stage == 2:
                early = s_recv[h]
            else:
                early = early_state(h)
                s_send[h] = (early + s_own[h]).astype(BF16)
                state_copy(h, 2).start()
                early = early.astype(BF16)
            for slot in (1, 0):
                fresh = dot_tn(vbuf[:, cols(h)], ebuf[slot]) * pstat[slot, 2:3, :]
                bottom, output = blend(
                    (pstat[slot, 0:1, :], pacc[slot]), (pstat[slot, 1:2, :], fresh)
                )
                l_send[slot, h] = bottom
                o_send[slot, h] = output.astype(BF16)
                straight = stage and slot
                (level_onward(h) if straight else level_copy(h, slot)).start()
                if stage < 2:
                    for index in order[:-2] if stage else order:
                        (chunk_onward(h, index) if straight else chunk_copy(h, slot, index)).start()
            if stage == 1:
                @pl.when(core == 1)
                def _():
                    both(h, order[-2:])
            if stage == 2:
                both(h, order[:-1])

                @pl.when(core == 0)
                def _():
                    both(inner, order[-2:])

                both(h, order[-1:])
            elif not stage:
                pl.when(h == 1)(early_last)
            rest(h, early)
            project(h - 1)
            if stage < 2:
                pre(h + 1)

        def both(h, indices):
            for index in indices:
                chunk_copy(h, 0, index).start()
                chunk_onward(h, index).start()

        loop(work, 1, inner)
        work(inner, 1)
        work(last, 2)
        for copy in near_copies() + far_copies():
            copy.wait_send()
        settle(s_send.at[later], tx.at[4])
        settle(l_send.at[:, later], tx.at[5])
        settle(o_send.at[:, later], tx.at[6])

    @pl.when(seq == 2)
    def _():
        for h in range(1, heads):
            query_copy(h, 0, 1, 0).start()
        for h in (inner, last):
            for copy in kv_copies(h, 2, 3):
                copy.start()
        weights()

        def first(h):
            own(h)
            s_own[h] = own_state(h)

        loop(first, 0, 2)
        pl.semaphore_wait(gate.at[0], 1)
        for index in range(1, peers):
            tell(1, {"head": peer_of(index)})
        loop(first, 2)
        pl.semaphore_wait(gate.at[1], peers - 1)
        tell(0, {"seq": 1})

        def pair(h):
            return k_ref[:, cols(h)], v_ref[:, cols(h)]

        def third(h):
            query_copy(h, 1, 2, 0).wait_recv()
            bottom, output = part(qbuf[1, :, cols(h)], (pair(h),))
            pstat[h, 0:1, :] = bottom
            pacc[h] = output

        query_copy(0, 1, 2, 0).wait_recv()
        settle(w_ref, tx.at[8])
        for copy in near_copies() + far_copies():
            copy.wait_recv()
        pairs = [(kbuf[:, cols(i)], vbuf[:, cols(i)]) for i in range(2)]
        early = sum(dot_tn(value, key) for key, value in pairs)
        s_send[0] = (early + s_own[0]).astype(BF16)
        state_copy(0, 3).start()
        bottom, output = part(qbuf[1, :, cols(0)], pairs + [pair(0)])
        l_send[1, 0] = bottom
        o_send[1, 0] = output.astype(BF16)
        level_onward(0).start()
        for index in order:
            chunk_onward(0, index).start()
        query = q_ref[:, cols(0)]
        windowed = blend(current(0), part(query, pairs))[1]
        finish(0, windowed, lin[0] + dot_nt(early.astype(BF16), query))
        loop(third, 1, inner)

        def state(h):
            state_copy(h, 2).wait_recv()
            s_send[h] = (s_recv[h].astype(F32) + s_own[h]).astype(BF16)
            state_copy(h, 3).start()
            lin[h] = norm(lin[h] + dot_nt(s_recv[h], q_ref[:, cols(h)]))

        def level_here(h):
            return level_copy(h, 0)

        def chunk_here(h, index):
            return chunk_copy(h, 0, index)

        def second(h):
            state(h)
            level_copy(h, 1).wait_recv()
            mine, theirs = pstat[h, 0:1, :], l_recv[1, h]
            top = jnp.maximum(mine, theirs)
            left, right = jnp.exp2(mine - top), jnp.exp2(theirs - top)
            total = left + right
            l_send[1, h] = top + jnp.log2(total)
            pstat[h, 1:2, :] = left * recip(total)
            pstat[h, 2:3, :] = right * recip(total)
            level_onward(h).start()
            for index in order:
                chunk_copy(h, 1, index).wait_recv()
                place = lanes(peer_of(index), share)
                output = pstat[h, 1:2, place] * pacc[h, :, place]
                output += pstat[h, 2:3, place] * o_recv[1, h, :, place].astype(F32)
                o_send[1, h, :, place] = output.astype(BF16)
                chunk_onward(h, index).start()

            pl.when(h == 1)(lambda: state(last))
            level_here(h).wait_recv()
            take(h, 0, order, chunk_here)
            project(h - 1)

        loop(second, 1, inner)
        state(inner)
        wind_up(0, level_here, chunk_here)
        settle(q_ref.at[:, pl.ds(HD, width - HD)], tx.at[0])
        settle(k_ref.at[:, pl.ds(inner * HD, 2 * HD)], tx.at[2])
        settle(v_ref.at[:, pl.ds(inner * HD, 2 * HD)], tx.at[3])
        settle(s_send, tx.at[4])
        settle(l_send.at[1, pl.ds(0, inner)], tx.at[5])
        settle(o_send.at[1, pl.ds(0, inner)], tx.at[6])

    @pl.when(seq == 3)
    def _():
        query_copy(1, 1, 1, 0).start()
        query_copy(0, 1, 2, 1).start()
        for h in range(2, heads):
            query_copy(h, 1, 1, 0).start()
            if h <= inner:
                query_copy(h - 1, 1, 2, 1).start()
        weights()
        loop(own)
        for h in (inner, last):
            for copy in kv_copies(h, 2, 3):
                copy.wait_recv()
            bottom, output = blend(
                current(h), part(q_ref[:, cols(h)], ((kbuf[:, cols(h)], vbuf[:, cols(h)]),))
            )
            stat[h, 0:1, :] = bottom
            acc[h] = output

        def state(h):
            state_copy(h, 3).wait_recv()
            lin[h] = norm(lin[h] + dot_nt(s_recv[h], q_ref[:, cols(h)]))

        def work(h):
            state(h)
            level_onward(h).wait_recv()
            take(h, 1, order, chunk_onward)
            project_before(h)

        settle(w_ref, tx.at[8])
        loop(work, 0, inner)
        state(last)
        state(inner)
        wind_up(1, level_onward, chunk_onward)
        settle(q_ref.at[:, pl.ds(HD, width - HD)], tx.at[0])
        settle(q_ref.at[:, pl.ds(0, inner * HD)], tx.at[1])

    project(last, out_ref)
    settle(mixed.at[:, pl.ds(0, length - share)], tx.at[8])


def fused(queries, keys, values, w_out):
    peers = lax.axis_size("head")
    length, width = queries.shape
    heads = width // HD
    share = length // peers
    dma = pltpu.SemaphoreType.DMA
    vmem = pl.BlockSpec(memory_space=pltpu.VMEM)
    return pl.pallas_call(
        functools.partial(kernel, peers),
        out_shape=pltpu.VMEM((share, w_out.shape[1]), BF16),
        in_specs=[pl.BlockSpec(memory_space=pltpu.HBM)] * 4,
        out_specs=vmem,
        scratch_shapes=[
            pltpu.VMEM((length, width), BF16),
            pltpu.VMEM((length, width), BF16),
            pltpu.VMEM((length, width), BF16),
            pltpu.VMEM((heads, peers * HD, w_out.shape[1]), BF16),
            pltpu.VMEM((share, w_out.shape[1]), F32),
            pltpu.VMEM((length, width), BF16),
            pltpu.VMEM((length, width), BF16),
            pltpu.VMEM((2, length, width), BF16),
            pltpu.VMEM((2, length, length), BF16),
            pltpu.VMEM((heads, HD, length), F32),
            pltpu.VMEM((heads, 8, length), F32),
            pltpu.VMEM((2, heads, HD, length), BF16),
            pltpu.VMEM((2, heads, HD, length), BF16),
            pltpu.VMEM((2, heads, 1, length), F32),
            pltpu.VMEM((2, heads, 1, length), F32),
            pltpu.VMEM((heads, HD, HD), F32),
            pltpu.VMEM((heads, HD, HD), BF16),
            pltpu.VMEM((heads, HD, HD), BF16),
            pltpu.VMEM((heads, HD, length), F32),
            pltpu.VMEM((heads, HD, length), F32),
            pltpu.VMEM((heads, 8, length), F32),
            pltpu.VMEM((width, length), BF16),
            pltpu.VMEM((heads, peers * HD, share), BF16),
            dma((9,)), dma((2, heads)), dma((2, heads)),
            dma((2 * heads - 4, peers)), dma((2 * heads - 4,)), dma((heads,)), dma((heads,)),
            pltpu.SemaphoreType.REGULAR((2,)),
        ],
        compiler_params=pltpu.CompilerParams(
            collective_id=0, has_side_effects=True, vmem_limit_bytes=56 * 1024 * 1024
        ),
    )(queries, keys, values, w_out)


def shifted(value, axis, steps):
    count = lax.axis_size(axis)
    first, last = (max(0, -steps), min(count, count - steps))
    return lax.ppermute(value, axis, [(source, source + steps) for source in range(first, last)])


def fits(queries):
    length, width = queries.shape
    blocks = lax.axis_size("seq")
    share = length // lax.axis_size("head")
    whole = share % HD == 0 and width % HD == 0 and width >= 4 * HD and lax.axis_size("head") % 2 == 0
    return blocks == 4 and blocks * length <= WINDOW and whole


def per_device(queries, keys, values, w_out):
    if fits(queries):
        return fused(queries, keys, values, w_out)
    length_dev, width = queries.shape
    heads_dev = width // HD
    block_rows = min(512, length_dev)
    block_count = length_dev // block_rows
    highest = lax.Precision.HIGHEST
    seq_index = lax.axis_index("seq")
    q_blocks = queries.reshape(block_count, block_rows, heads_dev, HD)
    k_blocks = keys.reshape(block_count, block_rows, heads_dev, HD)
    v_blocks = values.reshape(block_count, block_rows, heads_dev, HD)
    block_states = jnp.einsum(
        "bkhd,bkhe->bhde", k_blocks, v_blocks, preferred_element_type=jnp.float32
    )
    own_state = jnp.sum(block_states, axis=0)
    earlier = jnp.cumsum(block_states, axis=0) - block_states
    piece = lax.all_gather(own_state[None], "seq", axis=0, tiled=True)
    order = jnp.arange(piece.shape[0], dtype=jnp.int32)
    keep = order < seq_index
    prefix = jnp.sum(jnp.where(keep[:, None, None, None], piece, 0.0), axis=0)
    causal = jnp.arange(block_rows)[:, None] >= jnp.arange(block_rows)[None, :]
    local_scores = jnp.einsum(
        "bqhd,bkhd->bhqk", q_blocks, k_blocks, preferred_element_type=jnp.float32
    )
    local_scores = jnp.where(causal, local_scores, 0.0)
    intra = jnp.einsum(
        "bhqk,bkhe->bqhe", local_scores, v_blocks.astype(jnp.float32), precision=highest
    )
    state_before = prefix[None] + earlier
    inter = jnp.einsum(
        "bqhd,bhde->bqhe", q_blocks.astype(jnp.float32), state_before, precision=highest
    )
    linear = (intra + inter).reshape(length_dev, heads_dev, HD)
    normed = linear / jnp.sqrt(jnp.mean(linear * linear, axis=-1, keepdims=True) + 1e-06)
    reach = min(WINDOW // length_dev, lax.axis_size("seq") - 1)
    received = [shifted((keys, values), "seq", distance) for distance in range(1, reach + 1)]
    pad_rows = WINDOW - reach * length_dev
    filler = jnp.zeros((pad_rows, width), keys.dtype)
    wide_keys = jnp.concatenate([filler] + [pair[0] for pair in reversed(received)] + [keys], 0)
    wide_values = jnp.concatenate([filler] + [pair[1] for pair in reversed(received)] + [values], 0)
    wide_keys = wide_keys.reshape(-1, heads_dev, HD)
    wide_values = wide_values.reshape(-1, heads_dev, HD)
    scale = 1.0 / math.sqrt(HD)
    span = WINDOW + block_rows
    query_pos = jnp.arange(block_rows, dtype=jnp.int32)[:, None]
    key_pos = jnp.arange(span, dtype=jnp.int32)[None, :]
    band = (key_pos > query_pos) & (key_pos <= query_pos + WINDOW)
    rows_q = queries.reshape(block_rows, heads_dev, HD)
    anchor = seq_index * length_dev + 0 - WINDOW
    valid = band & (anchor + key_pos >= 0)
    scores = (
        jnp.einsum("qhd,khd->hqk", rows_q, wide_keys, preferred_element_type=jnp.float32) * scale
    )
    scores = jnp.where(valid[None], scores, -1e30)
    top = jnp.max(scores, axis=-1, keepdims=True)
    expo = jnp.where(valid[None], jnp.exp(scores - top), 0.0)
    total = jnp.sum(expo, axis=-1)
    weights = expo.astype(jnp.bfloat16)
    summed = jnp.einsum("hqk,khe->qhe", weights, wide_values, preferred_element_type=jnp.float32)
    pieces = summed / jnp.transpose(total)[:, :, None]
    mixed = (normed + pieces).astype(jnp.bfloat16).reshape(length_dev, width)
    head_count = lax.axis_size("head")
    share = length_dev // head_count
    grouped = mixed.reshape(head_count, share, width)
    return jnp.dot(
        lax.all_to_all(grouped, "head", split_axis=0, concat_axis=2, tiled=True)[0],
        w_out,
        preferred_element_type=jnp.float32,
    ).astype(jnp.bfloat16)


def solution(mesh):
    return jax.shard_map(
        per_device,
        mesh=mesh,
        in_specs=(
            P(("groups", "seq"), "head"),
            P(("groups", "seq"), "head"),
            P(("groups", "seq"), "head"),
            P(),
        ),
        out_specs=P(("groups", "seq", "head"), None),
        check_vma=False,
    )
```
